32 devices in a mesh: fsdp: 4 (over y, x), ctx: 2 (over core), tp: 4 (over z).
Axes of the slice: x: 2, y: 2, z: 4, core: 2. Of those that a mesh axis runs over, the one named last changes fastest.
Arguments:
- residual: bfloat16 [8192, 2048], P(('fsdp', 'ctx'), 'tp'), may hold values from -6 to 6
- out_grad: bfloat16 [8192, 2048], P(('fsdp', 'ctx'), 'tp'), may hold values from -6 to 6
- path_depth: int32 [8192], P(('fsdp', 'ctx')), may hold values from 0 to 895, as said below
- seg_lengths: int32 [4, 13], P('fsdp'), may hold values from 64 to 512, as said below
- parents: int32 [4, 13], P('fsdp'), may hold values from 0 to 4, as said below
- attn_norm_gain: bfloat16 [2048], P('tp'), may hold values from 0.099609375 to 1.8984375
- attn_norm_bias: bfloat16 [2048], P('tp'), may hold values from -1.5 to 1.5
- ffn_norm_gain: bfloat16 [2048], P('tp'), may hold values from 0.099609375 to 1.8984375
- ffn_norm_bias: bfloat16 [2048], P('tp'), may hold values from -1.5 to 1.5
- qkv_weight: bfloat16 [2048, 6144], P(('fsdp', 'ctx'), 'tp'), may hold values from -0.125 to 0.125
- qkv_bias: bfloat16 [6144], P('tp'), may hold values from -2.5 to 2.5
- dense_weight: bfloat16 [2048, 2048], P('tp', ('fsdp', 'ctx')), may hold values from -2 to 2
- dense_bias: bfloat16 [2048], P('tp'), may hold values from -2.5 to 2.5
- up_weight: bfloat16 [2048, 8192], P(('fsdp', 'ctx'), 'tp'), may hold values from -0.125 to 0.125
- up_bias: bfloat16 [8192], P('tp'), may hold values from -2.5 to 2.5
- down_weight: bfloat16 [8192, 2048], P('tp', ('fsdp', 'ctx')), may hold values from -0.0625 to 0.0625
- down_bias: bfloat16 [2048], P('tp'), may hold values from -2.5 to 2.5
Outputs:
- output: bfloat16 [8192, 2048], P(('fsdp', 'ctx'), 'tp')
- input_grad: bfloat16 [8192, 2048], P(('fsdp', 'ctx'), 'tp')
- grad_attn_norm_gain: float32 [2048], P('tp')
- grad_attn_norm_bias: float32 [2048], P('tp')
- grad_ffn_norm_gain: float32 [2048], P('tp')
- grad_ffn_norm_bias: float32 [2048], P('tp')
- grad_qkv_weight: float32 [2048, 6144], P(('fsdp', 'ctx'), 'tp')
- grad_qkv_bias: float32 [6144], P('tp')
- grad_dense_weight: float32 [2048, 2048], P('tp', ('fsdp', 'ctx'))
- grad_dense_bias: float32 [2048], P('tp')
- grad_up_weight: float32 [2048, 8192], P(('fsdp', 'ctx'), 'tp')
- grad_up_bias: float32 [8192], P('tp')
- grad_down_weight: float32 [8192, 2048], P('tp', ('fsdp', 'ctx'))
- grad_down_bias: float32 [2048], P('tp')
The draws below stay inside these ranges and needn't reach their ends.
Inputs may be any that keep to these rules, and one draw needn't show every extreme that they name: `seg_lengths`: row t lists tree t's segments in order: the trunk of 512 tokens, 4 branches, then 8 leaves; each row sums to 2048. `parents`: entry s of row t is the segment that segment s hangs from: 0 for the trunk itself and for each branch, a branch for each leaf; each branch holds exactly two leaves. `path_depth`: A token's place within its segment plus the lengths of the segment's proper ancestors in its tree.
All inputs are finite; a program needn't handle non-finite values.
Results may differ from the reference program's by a relative error of at most 0.012.
Values may be sent and summed in bfloat16 or wider, within the bound.
No kernel may reach another device: no remote copies, remote signals or barrier semaphores. Data moves between devices by JAX's collectives and lax.ppermute only.
A program may use at most 256 MiB of HBM per device.

```python
import math
import jax
import jax.numpy as jnp
from jax import lax

D = 2048
HEADS = 8
HEAD_DIM = 256
ROTARY = 64
FF = 8192
TRUNK = 512
SEG = 128
SEGS = 13
TREE_LEN = 2048
TREES = 4
TOKENS = 8192


def move_first(order_row):
    slots = jnp.arange(8, dtype=jnp.int32)
    head_value = order_row[0]
    return jnp.where(slots == 0, 0, jnp.where(order_row == 0, head_value, order_row)).astype(jnp.int32)


def tree_layout(key):
    key_swing = jax.random.fold_in(key, 101)
    key_pick = jax.random.fold_in(key, 202)
    key_sign = jax.random.fold_in(key, 303)
    key_leaves = jax.random.fold_in(key, 404)
    pair_index = jnp.arange(6)[None, :]
    swing = jax.random.randint(key_swing, (TREES, 6), 0, SEG // 2 + 1)
    picked = jax.random.randint(key_pick, (TREES, 1), 0, 6)
    swing = jnp.where(pair_index == picked, SEG // 2, swing)
    swing = jnp.where((pair_index == 0) | (pair_index == 2), SEG // 2, swing)
    signs = jax.random.randint(key_sign, (TREES, 6), 0, 2) * 2 - 1
    signs = jnp.where((pair_index == 0) | (pair_index == 2), 1, signs)
    paired = jnp.stack([SEG + signs * swing, SEG - signs * swing], axis=-1).reshape(TREES, 12)
    lengths = jnp.concatenate([jnp.full((TREES, 1), TRUNK, jnp.int32), paired.astype(jnp.int32)], axis=1)
    orders = jax.vmap(lambda one_key: jax.random.permutation(one_key, 8))(jax.random.split(key_leaves, TREES))
    orders = jax.vmap(move_first)(orders.astype(jnp.int32))
    leaf_parent = (1 + orders // 2).astype(jnp.int32)
    parent = jnp.concatenate([jnp.zeros((TREES, 5), jnp.int32), leaf_parent], axis=1)
    places = jnp.arange(TREE_LEN, dtype=jnp.int32)
    starts = jnp.cumsum(lengths, axis=1) - lengths
    membership = jnp.sum((places[None, :, None] >= starts[:, None, :]).astype(jnp.int32), axis=2) - 1
    labels = jnp.arange(SEGS, dtype=jnp.int32)
    parent_len = jnp.sum(jnp.where(parent[:, :, None] == labels[None, None, :], lengths[:, None, :], 0), axis=2)
    offsets = jnp.where(labels[None, :] == 0, 0, jnp.where(labels[None, :] < 5, TRUNK, TRUNK + parent_len))
    hot = membership[:, :, None] == labels[None, None, :]
    seg_start = jnp.sum(jnp.where(hot, starts[:, None, :], 0), axis=2)
    seg_offset = jnp.sum(jnp.where(hot, offsets[:, None, :], 0), axis=2)
    depth = (places[None, :] - seg_start + seg_offset).astype(jnp.int32)
    return (lengths, parent, depth.reshape(TOKENS))


def draw_seg_lengths(key, part):
    return tree_layout(key)[0]


def draw_parents(key, part):
    return tree_layout(key)[1]


def draw_path_depth(key, part):
    return tree_layout(key)[2]


def levels(key, shape, shards, low, high):
    loudness, own = 1.0, jax.random.fold_in(key, 6)
    for position, blocks in shards:
        steps = jnp.exp(jax.random.uniform(jax.random.fold_in(own, position), (blocks,), jnp.float32, low / len(shards), high / len(shards)))
        loudness = loudness * jnp.repeat(steps, shape[position] // blocks).reshape([-1 if axis == position else 1 for axis in range(len(shape))])
    return loudness


def normal_values(stream_key, shape, scale, bound, cuts=(), kind=jnp.bfloat16):
    drawn = jax.random.normal(stream_key, shape, jnp.float32) * scale
    if len(cuts) > 0:
        drawn = levels(stream_key, shape, cuts, -0.22, 0.18) * drawn
    return jnp.clip(drawn, min=-bound, max=bound).astype(kind)


def setup_inputs(seed: int = 0) -> dict:
    keys = jax.random.split(jax.random.key(seed), 18)
    residual = normal_values(keys[0], (TOKENS, D), 1.0, 6.0, ((0, 8), (1, 4)))
    out_grad = normal_values(keys[1], (TOKENS, D), 1.0, 6.0, ((0, 8), (1, 4)))
    path_depth = draw_path_depth(jax.random.fold_in(keys[17], 71), 0)
    seg_lengths = draw_seg_lengths(jax.random.fold_in(keys[17], 71), 0)
    parents = draw_parents(jax.random.fold_in(keys[17], 71), 0)
    attn_norm_gain = jnp.clip(1.0 + 0.18 * jax.random.normal(keys[5], (D,), jnp.float32), 0.099609375, 1.8984375).astype(jnp.bfloat16)
    attn_norm_bias = normal_values(keys[6], (D,), 0.3, 1.5, ((0, 4),))
    ffn_norm_gain = jnp.clip(1.0 + 0.18 * jax.random.normal(keys[7], (D,), jnp.float32), 0.099609375, 1.8984375).astype(jnp.bfloat16)
    ffn_norm_bias = normal_values(keys[8], (D,), 0.3, 1.5, ((0, 4),))
    qkv_weight = normal_values(keys[9], (D, 3 * D), D ** -0.5, 0.125, ((0, 8), (1, 4)))
    qkv_bias = normal_values(keys[10], (3 * D,), 0.5, 2.5, ((0, 4),))
    dense_weight = normal_values(keys[11], (D, D), (max(D // 256, 2)) ** -0.5, 2.0, ((0, 4), (1, 8)))
    dense_bias = normal_values(keys[12], (D,), 0.5, 2.5, ((0, 4),))
    up_weight = normal_values(keys[13], (D, FF), D ** -0.5, 0.125, ((0, 8), (1, 4)))
    up_bias = normal_values(keys[14], (FF,), 0.5, 2.5, ((0, 4),))
    down_weight = normal_values(keys[15], (FF, D), FF ** -0.5, 0.0625, ((0, 4), (1, 8)))
    down_bias = normal_values(keys[16], (D,), 0.5, 2.5, ((0, 4),))
    return {"residual": residual, "out_grad": out_grad, "path_depth": path_depth, "seg_lengths": seg_lengths, "parents": parents, "attn_norm_gain": attn_norm_gain, "attn_norm_bias": attn_norm_bias, "ffn_norm_gain": ffn_norm_gain, "ffn_norm_bias": ffn_norm_bias, "qkv_weight": qkv_weight, "qkv_bias": qkv_bias, "dense_weight": dense_weight, "dense_bias": dense_bias, "up_weight": up_weight, "up_bias": up_bias, "down_weight": down_weight, "down_bias": down_bias}


@jax.custom_vjp
def low(v):
    return lax.optimization_barrier(v.astype(jnp.bfloat16)).astype(jnp.float32)

@jax.custom_vjp
def low_back(v):
    return v

def low_keep(v):
    return (low(v), None)

def low_pass(kept, grad):
    return (grad,)

def back_keep(v):
    return (v, None)

def back_low(kept, grad):
    return (low(grad),)
low.defvjp(low_keep, low_pass)
low_back.defvjp(back_keep, back_low)
norm_epsilon = 1e-05
masked_score = -1e+30

def normalize(values_in):
    row_mean = lax.optimization_barrier(jnp.mean(values_in, axis=-1, keepdims=True))
    centred = values_in - row_mean
    variance = lax.optimization_barrier(jnp.mean(centred * centred, axis=-1, keepdims=True))
    return centred * lax.rsqrt(variance + norm_epsilon)

def rotary(vectors, places):
    half_rot = ROTARY // 2
    frequency = jnp.power(10000.0, -2.0 * jnp.arange(half_rot).astype(jnp.float32) / ROTARY)
    angles = places.astype(jnp.float32)[:, None] * frequency[None, :]
    cosine = jnp.cos(angles)[:, None, :]
    sine_part = jnp.sin(angles)[:, None, :]
    first_half = vectors[..., :half_rot]
    second_half = vectors[..., half_rot:ROTARY]
    return jnp.concatenate([first_half * cosine - second_half * sine_part, second_half * cosine + first_half * sine_part, vectors[..., ROTARY:]], axis=-1)

def tree_tables(lengths, parent):
    starts = jnp.cumsum(lengths) - lengths
    labels = jnp.arange(SEGS)
    grand_parent = lax.optimization_barrier(jnp.sum(jnp.where(parent[:, None] == labels[None, :], parent[None, :], 0), axis=1))
    ancestor = (labels[None, :] == labels[:, None]) | (labels[None, :] == parent[:, None]) | (labels[None, :] == grand_parent[:, None])
    return (starts, ancestor.astype(jnp.float32))

def segment_onehot(places, starts):
    membership = lax.optimization_barrier(jnp.sum((places[:, None] >= starts[None, :]).astype(jnp.int32), axis=1)) - 1
    return (membership[:, None] == jnp.arange(SEGS)[None, :]).astype(jnp.float32)

def visible(hot_query, place_query, hot_key, place_key, ancestor):
    reachable = jnp.dot(jnp.dot(hot_query, ancestor), hot_key.T)
    return (reachable > 0.5) & (place_key[None, :] <= place_query[:, None])

def attention(query_rows, key_rows, value_rows, places, hot_tokens, ancestor):
    block_size = TREE_LEN // 8
    score_scale = 1.0 / math.sqrt(HEAD_DIM)

    def one_block(pieces):
        query_block, place_block, hot_block = pieces
        scores = jnp.einsum('nhe,lhe->hnl', query_block, key_rows, precision=lax.Precision.HIGHEST) * score_scale
        scores = low_back(scores)
        reachable = visible(hot_block, place_block, hot_tokens, places, ancestor)
        scores = jnp.where(reachable[None], scores, masked_score)
        row_top = lax.optimization_barrier(jnp.max(scores, axis=-1, keepdims=True))
        exp_scores = jnp.exp(scores - row_top)
        attn_probs = exp_scores / lax.optimization_barrier(jnp.sum(exp_scores, axis=-1, keepdims=True))
        return jnp.einsum('hnl,lhe->nhe', low(attn_probs), value_rows, precision=lax.Precision.HIGHEST)
    blocks = lax.map(jax.checkpoint(one_block), (query_rows.reshape(8, block_size, HEADS, HEAD_DIM), places.reshape(8, block_size), hot_tokens.reshape(8, block_size, SEGS)))
    return blocks.reshape(TREE_LEN, HEADS * HEAD_DIM)

def layer(params, rows_in, tree_depth, lengths, parent):
    attn_gain, attn_shift, ffn_gain, ffn_shift, w_qkv, b_qkv, w_dense, b_dense, w_up, b_up, w_down, b_down = params
    starts, ancestor = tree_tables(lengths, parent)
    places = jnp.arange(TREE_LEN)
    hot_tokens = segment_onehot(places, starts)
    normed = normalize(rows_in)
    attn_in = low(normed * attn_gain + attn_shift)
    ffn_in = low(normed * ffn_gain + ffn_shift)
    joined = low_back(jnp.dot(attn_in, w_qkv, precision=lax.Precision.HIGHEST) + b_qkv).reshape(TREE_LEN, HEADS, 3, HEAD_DIM)
    query_rows = low(rotary(joined[:, :, 0], tree_depth))
    key_rows = low(rotary(joined[:, :, 1], tree_depth))
    value_rows = low(joined[:, :, 2])
    attended = low(low_back(attention(query_rows, key_rows, value_rows, places, hot_tokens, ancestor)))
    hidden_pre = low_back(jnp.dot(ffn_in, w_up, precision=lax.Precision.HIGHEST) + b_up)
    hidden = low(jax.nn.gelu(hidden_pre, approximate=False))
    attn_out = jnp.dot(attended, w_dense, precision=lax.Precision.HIGHEST) + b_dense
    ffn_out = jnp.dot(hidden, w_down, precision=lax.Precision.HIGHEST) + b_down
    return rows_in + attn_out + ffn_out

def reference(residual, out_grad, path_depth, seg_lengths, parents, attn_norm_gain, attn_norm_bias, ffn_norm_gain, ffn_norm_bias, qkv_weight, qkv_bias, dense_weight, dense_bias, up_weight, up_bias, down_weight, down_bias):
    raw_params = (attn_norm_gain, attn_norm_bias, ffn_norm_gain, ffn_norm_bias, qkv_weight, qkv_bias, dense_weight, dense_bias, up_weight, up_bias, down_weight, down_bias)
    params = tuple((member.astype(jnp.float32) for member in raw_params))

    def per_tree(totals, tree_item):
        rows_in, cotangent, tree_depth, lengths, parent = tree_item
        result, pullback = jax.vjp(lambda param_set, layer_rows: layer(param_set, layer_rows, tree_depth, lengths, parent), params, rows_in)
        grads, grad_rows = pullback(cotangent)
        totals = jax.tree.map(lambda acc, extra: acc + extra, totals, grads)
        return (totals, (result.astype(jnp.bfloat16), grad_rows.astype(jnp.bfloat16)))
    zero_grads = jax.tree.map(jnp.zeros_like, params)
    tree_inputs = (residual.astype(jnp.float32).reshape(TREES, TREE_LEN, D), out_grad.astype(jnp.float32).reshape(TREES, TREE_LEN, D), path_depth.reshape(TREES, TREE_LEN), seg_lengths, parents)
    totals, (outputs, grads_in) = lax.scan(per_tree, zero_grads, tree_inputs)
    return (outputs.reshape(TOKENS, D), grads_in.reshape(TOKENS, D), totals[0], totals[1], totals[2], totals[3], totals[4], totals[5], totals[6], totals[7], totals[8], totals[9], totals[10], totals[11])
```

```python
from functools import partial
import math

import jax
import jax.numpy as jnp
from jax import lax
from jax.experimental import pallas as pl
from jax.experimental.pallas import tpu as pltpu
from jax.sharding import PartitionSpec as P

HEAD_DIM = 256
ROTARY = 64
SEGS = 13


norm_epsilon = 1e-05
masked_score = -1e30
block_limit = 512


def from_behind(x, axis, by):
    peers = lax.axis_size(axis)
    pairs = [(i, i + by) for i in range(peers) if 0 <= i + by < peers]
    return lax.ppermute(x, axis, pairs)


def rotary(vectors, places):
    half_rot = ROTARY // 2
    frequency = jnp.power(10000.0, -2.0 * jnp.arange(half_rot).astype(jnp.float32) / ROTARY)
    angles = places.astype(jnp.float32)[:, None] * frequency[None, :]
    cosine = jnp.cos(angles)[:, None, :]
    sine_part = jnp.sin(angles)[:, None, :]
    first_half = vectors[..., :half_rot]
    second_half = vectors[..., half_rot:ROTARY]
    return jnp.concatenate(
        [
            first_half * cosine - second_half * sine_part,
            second_half * cosine + first_half * sine_part,
            vectors[..., ROTARY:],
        ],
        axis=-1,
    )


def tree_tables(lengths, parent):
    starts = jnp.cumsum(lengths) - lengths
    labels = jnp.arange(SEGS)
    grand_parent = jnp.sum(
        jnp.where(parent[:, None] == labels[None, :], parent[None, :], 0), axis=1
    )
    ancestor = (
        (labels[None, :] == labels[:, None])
        | (labels[None, :] == parent[:, None])
        | (labels[None, :] == grand_parent[:, None])
    )
    return (starts, ancestor.astype(jnp.float32))


def segment_onehot(places, starts):
    membership = jnp.sum((places[:, None] >= starts[None, :]).astype(jnp.int32), axis=1) - 1
    return (membership[:, None] == jnp.arange(SEGS)[None, :]).astype(jnp.float32)


def visible(hot_query, place_query, hot_key, place_key, ancestor):
    reachable = jnp.dot(jnp.dot(hot_query, ancestor), hot_key.T)
    return (reachable > 0.5) & (place_key[None, :] <= place_query[:, None])


def on_device(
    residual,
    out_grad,
    path_depth,
    seg_lengths,
    parents,
    attn_norm_gain,
    attn_norm_bias,
    ffn_norm_gain,
    ffn_norm_bias,
    qkv_weight,
    qkv_bias,
    dense_weight,
    dense_bias,
    up_weight,
    up_bias,
    down_weight,
    down_bias,
):
    row_count = residual.shape[0]
    local_width = residual.shape[1]
    head_count = qkv_weight.shape[1] // (3 * HEAD_DIM)
    score_scale = 1.0 / math.sqrt(HEAD_DIM)
    ctx_index = lax.axis_index("ctx")
    tp_index = lax.axis_index("tp")
    norm_stack = jnp.stack([attn_norm_gain, attn_norm_bias, ffn_norm_gain, ffn_norm_bias])
    full_rows, norm_terms = (
        lax.all_gather(residual, "tp", axis=1, tiled=True),
        lax.all_gather(norm_stack, "tp", axis=1, tiled=True),
    )
    norm_terms = norm_terms.astype(jnp.float32)
    qkv_full, up_full = (
        lax.all_gather(qkv_weight, ("fsdp", "ctx"), axis=0, tiled=True),
        lax.all_gather(up_weight, ("fsdp", "ctx"), axis=0, tiled=True),
    )
    dense_full, down_full = (
        lax.all_gather(dense_weight, ("fsdp", "ctx"), axis=1, tiled=True),
        lax.all_gather(down_weight, ("fsdp", "ctx"), axis=1, tiled=True),
    )
    rows_wide = full_rows.astype(jnp.float32)
    centred = rows_wide - jnp.mean(rows_wide, axis=1, keepdims=True)
    inverse_scale = lax.rsqrt(jnp.mean(centred * centred, axis=1, keepdims=True) + norm_epsilon)
    normed = centred * inverse_scale
    attn_in = (normed * norm_terms[0] + norm_terms[1]).astype(jnp.bfloat16)
    ffn_in = (normed * norm_terms[2] + norm_terms[3]).astype(jnp.bfloat16)
    joined = (
        jnp.dot(attn_in, qkv_full, preferred_element_type=jnp.float32)
        + qkv_bias.astype(jnp.float32)
    ).reshape(row_count, head_count, 3, HEAD_DIM)
    queries_pre = joined[:, :, 0]
    query_rows = rotary(queries_pre, path_depth).astype(jnp.bfloat16)
    key_rows = rotary(joined[:, :, 1], path_depth).astype(jnp.bfloat16)
    value_rows = joined[:, :, 2].astype(jnp.bfloat16)
    far_keys, far_values = from_behind((key_rows, value_rows), "ctx", 1)
    starts, ancestor = tree_tables(seg_lengths[0], parents[0])
    places = ctx_index * row_count + jnp.arange(row_count, dtype=jnp.int32)
    key_places = jnp.concatenate([places - row_count, places])
    hot_query = segment_onehot(places, starts)
    hot_key = segment_onehot(key_places, starts)
    all_keys = jnp.concatenate([far_keys, key_rows], axis=0)
    all_values = jnp.concatenate([far_values, value_rows], axis=0)
    block_starts = list(range(0, row_count, block_limit))

    def block_scores(block_start, block_size, key_set):
        key_span = row_count + block_start + block_size
        query_block = query_rows[block_start : block_start + block_size]
        scores = (
            jnp.einsum(
                "nhe,lhe->hnl", query_block, key_set[:key_span], preferred_element_type=jnp.float32
            )
            * score_scale
        )
        reachable = visible(
            hot_query[block_start : block_start + block_size],
            places[block_start : block_start + block_size],
            hot_key[:key_span],
            key_places[:key_span],
            ancestor,
        )
        return jnp.where(reachable[None], scores, masked_score)

    out_blocks = []
    log_totals = []
    for block_start in block_starts:
        block_size = min(block_limit, row_count - block_start)
        key_span = row_count + block_start + block_size
        scores = block_scores(block_start, block_size, all_keys)
        row_top = jnp.max(scores, axis=-1, keepdims=True)
        exp_scores = jnp.exp(scores - row_top)
        exp_total = jnp.sum(exp_scores, axis=-1, keepdims=True)
        attn_probs = exp_scores / exp_total
        out_blocks.append(
            jnp.einsum(
                "hnl,lhe->nhe",
                attn_probs.astype(jnp.bfloat16),
                all_values[:key_span],
                preferred_element_type=jnp.float32,
            )
        )
        log_totals.append(row_top + jnp.log(exp_total))
    attended = (
        jnp.concatenate(out_blocks, axis=0)
        .reshape(row_count, head_count * HEAD_DIM)
        .astype(jnp.bfloat16)
    )
    hidden_pre = jnp.dot(ffn_in, up_full, preferred_element_type=jnp.float32) + up_bias.astype(
        jnp.float32
    )
    hidden_wide, gelu_back = jax.vjp(partial(jax.nn.gelu, approximate=False), hidden_pre)
    hidden = hidden_wide.astype(jnp.bfloat16)
    partial_out = jnp.dot(attended, dense_full, preferred_element_type=jnp.float32) + jnp.dot(
        hidden, down_full, preferred_element_type=jnp.float32
    )
    shared_out = lax.psum_scatter(partial_out, "tp", scatter_dimension=1, tiled=True)
    output = (
        residual.astype(jnp.float32)
        + shared_out
        + dense_bias.astype(jnp.float32)
        + down_bias.astype(jnp.float32)
    ).astype(jnp.bfloat16)
    cotangent = lax.all_gather(out_grad, "tp", axis=1, tiled=True)
    grad_out_bias = jnp.sum(out_grad.astype(jnp.float32), axis=0)
    grad_dense_w = jnp.einsum("rf,rd->fd", attended, cotangent, preferred_element_type=jnp.float32)
    grad_down_w = jnp.einsum("rf,rd->fd", hidden, cotangent, preferred_element_type=jnp.float32)
    grad_attended = jnp.einsum(
        "rd,fd->rf", cotangent, dense_full, preferred_element_type=jnp.float32
    ).astype(jnp.bfloat16)
    grad_hidden = jnp.einsum("rd,fd->rf", cotangent, down_full, preferred_element_type=jnp.float32)
    grad_pre = gelu_back(grad_hidden)[0].astype(jnp.bfloat16)
    grad_up_w = jnp.einsum("rd,rf->df", ffn_in, grad_pre, preferred_element_type=jnp.float32)
    grad_up_b = jnp.sum(grad_pre.astype(jnp.float32), axis=0)
    grad_ffn_in = jnp.einsum("rf,df->rd", grad_pre, up_full, preferred_element_type=jnp.float32)
    key_set = all_keys
    grad_att_heads = grad_attended.reshape(row_count, head_count, HEAD_DIM)
    grad_query_parts = []
    grad_key_all = jnp.zeros((2 * row_count, head_count, HEAD_DIM), jnp.float32)
    grad_value_all = jnp.zeros((2 * row_count, head_count, HEAD_DIM), jnp.float32)
    for block_number, block_start in enumerate(block_starts):
        block_size = min(block_limit, row_count - block_start)
        key_span = row_count + block_start + block_size
        scores = block_scores(block_start, block_size, key_set)
        attn_probs = jnp.exp(scores - log_totals[block_number])
        grad_block = grad_att_heads[block_start : block_start + block_size]
        grad_value_all = grad_value_all.at[:key_span].add(
            jnp.einsum(
                "hnl,nhe->lhe",
                attn_probs.astype(jnp.bfloat16),
                grad_block,
                preferred_element_type=jnp.float32,
            )
        )
        grad_dots = jnp.einsum(
            "nhe,lhe->hnl", grad_block, all_values[:key_span], preferred_element_type=jnp.float32
        )
        row_delta = jnp.sum(attn_probs * grad_dots, axis=-1, keepdims=True)
        grad_scores = (attn_probs * (grad_dots - row_delta)).astype(jnp.bfloat16)
        grad_query_parts.append(
            jnp.einsum(
                "hnl,lhe->nhe", grad_scores, key_set[:key_span], preferred_element_type=jnp.float32
            )
            * score_scale
        )
        grad_key_all = grad_key_all.at[:key_span].add(
            jnp.einsum(
                "hnl,nhe->lhe",
                grad_scores,
                query_rows[block_start : block_start + block_size],
                preferred_element_type=jnp.float32,
            )
            * score_scale
        )
    arriving_keys, arriving_values = from_behind(
        (grad_key_all[:row_count], grad_value_all[:row_count]), "ctx", -1
    )
    grad_keys = grad_key_all[row_count:] + arriving_keys
    grad_values = grad_value_all[row_count:] + arriving_values
    grad_queries = jnp.concatenate(grad_query_parts, axis=0)
    rotated_unused, rotary_back = jax.vjp(lambda vectors: rotary(vectors, path_depth), queries_pre)
    grad_joined = (
        jnp.stack([rotary_back(grad_queries)[0], rotary_back(grad_keys)[0], grad_values], axis=2)
        .astype(jnp.bfloat16)
        .reshape(row_count, head_count * 3 * HEAD_DIM)
    )
    grad_qkv_w = jnp.einsum("rd,rf->df", attn_in, grad_joined, preferred_element_type=jnp.float32)
    grad_qkv_b = jnp.sum(grad_joined.astype(jnp.float32), axis=0)
    grad_attn_in = jnp.einsum(
        "rf,df->rd", grad_joined, qkv_full, preferred_element_type=jnp.float32
    )
    total_attn, total_ffn = lax.psum((grad_attn_in, grad_ffn_in), "tp")

    def norm_back(total_grad, gain_row):
        scaled = total_grad * gain_row
        mean_plain = jnp.mean(scaled, axis=1, keepdims=True)
        mean_normed = jnp.mean(scaled * normed, axis=1, keepdims=True)
        back_rows = inverse_scale * (scaled - mean_plain - normed * mean_normed)
        gain_grad = jnp.sum(total_grad * normed, axis=0)
        shift_grad = jnp.sum(total_grad, axis=0)
        return (
            lax.dynamic_slice_in_dim(back_rows, tp_index * local_width, local_width, 1),
            lax.dynamic_slice_in_dim(gain_grad, tp_index * local_width, local_width, 0),
            lax.dynamic_slice_in_dim(shift_grad, tp_index * local_width, local_width, 0),
        )

    back_attn, attn_gain_grad, attn_shift_grad = norm_back(total_attn, norm_terms[0])
    back_ffn, ffn_gain_grad, ffn_shift_grad = norm_back(total_ffn, norm_terms[2])
    norm_grads = jnp.stack([attn_gain_grad, attn_shift_grad, ffn_gain_grad, ffn_shift_grad])
    back_total = back_attn + back_ffn
    input_grad = (out_grad.astype(jnp.float32) + back_total).astype(jnp.bfloat16)
    qkv_bias_grad, up_bias_grad, out_bias_grad, norm_totals = lax.psum(
        (grad_qkv_b, grad_up_b, grad_out_bias, norm_grads), ("fsdp", "ctx")
    )
    qkv_weight_grad, up_weight_grad = (
        lax.psum_scatter(
            grad_qkv_w.astype(jnp.bfloat16), ("fsdp", "ctx"), scatter_dimension=0, tiled=True
        ).astype(jnp.float32),
        lax.psum_scatter(
            grad_up_w.astype(jnp.bfloat16), ("fsdp", "ctx"), scatter_dimension=0, tiled=True
        ).astype(jnp.float32),
    )
    dense_weight_grad, down_weight_grad = (
        lax.psum_scatter(
            grad_dense_w.astype(jnp.bfloat16), ("fsdp", "ctx"), scatter_dimension=1, tiled=True
        ).astype(jnp.float32),
        lax.psum_scatter(
            grad_down_w.astype(jnp.bfloat16), ("fsdp", "ctx"), scatter_dimension=1, tiled=True
        ).astype(jnp.float32),
    )
    return (
        output,
        input_grad,
        norm_totals[0],
        norm_totals[1],
        norm_totals[2],
        norm_totals[3],
        qkv_weight_grad,
        qkv_bias_grad,
        dense_weight_grad,
        out_bias_grad,
        up_weight_grad,
        up_bias_grad,
        down_weight_grad,
        out_bias_grad,
    )


low = jnp.bfloat16
wide = jnp.float32
tile = 256


def trade(x, axis, bit):
    peers = lax.axis_size(axis)
    return lax.ppermute(x, axis, [(i, i ^ bit) for i in range(peers)])


def gather_line(x, axis):
    near = trade(x, axis, 1)
    far = trade(x, axis, 2)
    return (x, near, far, trade(far, axis, 1))


def lay_out(pieces, place, dim):
    width = pieces[0].shape[dim]
    shape = list(pieces[0].shape)
    shape[dim] = width * len(pieces)
    whole = jnp.zeros(shape, pieces[0].dtype)
    for step, piece in enumerate(pieces):
        whole = lax.dynamic_update_slice_in_dim(whole, piece, (place ^ step) * width, dim)
    return whole


def block_of(x, index, dim, blocks):
    width = x.shape[dim] // blocks
    return lax.dynamic_slice_in_dim(x, index * width, width, dim)


def scatter_line(total, axis, dim):
    place = lax.axis_index(axis)
    far_side = trade(block_of(total, place ^ 3, dim, 4).astype(low), axis, 1)
    near = trade(block_of(total, place ^ 1, dim, 4).astype(low), axis, 1)
    passed = block_of(total, place ^ 2, dim, 4).astype(wide) + far_side.astype(wide)
    far = trade(passed.astype(low), axis, 2)
    own = block_of(total, place, dim, 4).astype(wide)
    return own + near.astype(wide) + far.astype(wide)


def half_of(x, index, dim):
    return block_of(x, index, dim, 2)


def join_cores(mine, theirs, core, dim):
    first = jnp.where(core == 0, mine, theirs)
    second = jnp.where(core == 0, theirs, mine)
    return jnp.concatenate([first, second], axis=dim)


def turn(rows, cosine, sine, sign):
    half_rot = ROTARY // 2
    lane = lax.broadcasted_iota(jnp.int32, cosine.shape, 1)
    front = rows[:, :128]
    ahead = pltpu.roll(front, 128 - half_rot, 1)
    behind = pltpu.roll(front, half_rot, 1)
    other = jnp.where(lane < half_rot, -ahead, behind)
    turned = front * cosine + other * (sine * sign)
    return jnp.concatenate([turned, rows[:, 128:]], axis=1)


def contract(a, b, dims):
    return lax.dot_general(a, b, ((dims[:1], dims[1:]), ((), ())), preferred_element_type=wide)


def scores_of(keys, query, info, trunk_end, first_row, scale):
    scores = contract(keys, query, (1, 1)) * scale
    span = scores.shape[0]
    key_place = lax.broadcasted_iota(jnp.int32, scores.shape, 0)
    query_place = first_row + lax.broadcasted_iota(jnp.int32, scores.shape, 1)
    seen = (
        (key_place < trunk_end)
        | ((key_place >= info[0:1]) & (key_place < info[1:2]))
        | (key_place >= info[2:3])
    ) & (key_place <= query_place)
    return jnp.where(seen, scores, masked_score)


def attend_kernel(scalars, joined, cosine, sine, info, packed, attended, log_total, scale):
    rows = joined.shape[0]
    blocks = rows // tile
    shift = scalars[0] * (blocks // 2)
    for block in range(blocks):
        here = pl.ds(block * tile, tile)
        there = pl.ds(pl.multiple_of(lax.rem(block + shift, blocks) * tile, tile), tile)
        for part in range(3):
            vectors = joined[here, part * HEAD_DIM : (part + 1) * HEAD_DIM]
            if part < 2:
                vectors = turn(vectors, cosine[here, :], sine[here, :], 1.0)
            packed[part, there, :] = vectors.astype(low)
    for block in range(blocks):
        span = (block + 1) * tile
        query = packed[0, block * tile : span, :]
        about = info[:, block * tile : span]
        scores = scores_of(packed[1, :span, :], query, about, scalars[1], block * tile, scale)
        top = jnp.max(scores, axis=0, keepdims=True)
        powers = jnp.exp(scores - top)
        total = jnp.sum(powers, axis=0, keepdims=True)
        probs = (powers * (1.0 / total)).astype(low)
        there = pl.ds(pl.multiple_of(lax.rem(block + shift, blocks) * tile, tile), tile)
        attended[there, :] = contract(probs, packed[2, :span, :], (0, 0)).astype(low)
        log_total[0:1, block * tile : span] = top + jnp.log(total)


def attend_back_kernel(
    scalars, packed, grads, log_total, cosine, sine, info, joined_grad, bias_grad, key_grad,
    value_grad, scale
):
    rows = grads.shape[0]
    blocks = rows // tile
    shift = scalars[0] * (blocks // 2)
    bias_total = jnp.zeros((1, 3 * HEAD_DIM), wide)
    for block in reversed(range(blocks)):
        span = (block + 1) * tile
        before = block * tile
        query = packed[0, before:span, :]
        about = info[:, before:span]
        there = pl.ds(pl.multiple_of(lax.rem(block + shift, blocks) * tile, tile), tile)
        grad = grads[there, :]
        scores = scores_of(packed[1, :span, :], query, about, scalars[1], before, scale)
        probs = jnp.exp(scores - log_total[0:1, before:span])
        value_part = contract(probs.astype(low), grad, (1, 0))
        dots = contract(packed[2, :span, :], grad, (1, 1))
        delta = jnp.sum(probs * dots, axis=0, keepdims=True)
        score_grad = (probs * (dots - delta)).astype(low)
        query_grad = contract(score_grad, packed[1, :span, :], (0, 0)) * scale
        key_part = contract(score_grad, query, (1, 0)) * scale
        if block == blocks - 1:
            key_grad[...] = key_part
            value_grad[...] = value_part
        else:
            key_grad[:span, :] += key_part
            value_grad[:span, :] += value_part
        parts = (
            turn(query_grad, cosine[there, :], sine[there, :], -1.0),
            turn(key_grad[before:span, :], cosine[there, :], sine[there, :], -1.0),
            value_grad[before:span, :],
        )
        together = jnp.concatenate(parts, axis=1).astype(low)
        joined_grad[there, :] = together
        bias_total += jnp.sum(together.astype(wide), axis=0, keepdims=True)
    bias_grad[...] = jnp.broadcast_to(bias_total, bias_grad.shape)


def whole(shape):
    return pl.BlockSpec(shape, lambda head, scalars: (0,) * len(shape))


def attend(scalars, joined, cosine, sine, info):
    rows, columns = joined.shape
    heads = columns // (3 * HEAD_DIM)
    pairs = rows * (rows + tile) // 2
    return pl.pallas_call(
        partial(attend_kernel, scale=1.0 / math.sqrt(HEAD_DIM)),
        grid_spec=pltpu.PrefetchScalarGridSpec(
            num_scalar_prefetch=1,
            grid=(heads,),
            in_specs=[
                pl.BlockSpec((rows, 3 * HEAD_DIM), lambda head, scalars: (0, head)),
                whole((rows, 128)),
                whole((rows, 128)),
                whole((8, rows)),
            ],
            out_specs=[
                pl.BlockSpec((3, rows, HEAD_DIM), lambda head, scalars: (0, 0, head)),
                pl.BlockSpec((rows, HEAD_DIM), lambda head, scalars: (0, head)),
                pl.BlockSpec((8, rows), lambda head, scalars: (head, 0)),
            ],
        ),
        out_shape=[
            jax.ShapeDtypeStruct((3, rows, heads * HEAD_DIM), low),
            jax.ShapeDtypeStruct((rows, heads * HEAD_DIM), low),
            jax.ShapeDtypeStruct((heads * 8, rows), wide),
        ],
        compiler_params=pltpu.CompilerParams(vmem_limit_bytes=56 * 1024 * 1024),
        cost_estimate=pl.CostEstimate(
            flops=heads * pairs * HEAD_DIM * 4,
            bytes_accessed=rows * columns * 8,
            transcendentals=heads * pairs,
        ),
        name="attend",
    )(scalars, joined, cosine, sine, info)


def attend_back(scalars, packed, grads, log_total, cosine, sine, info):
    rows, width = grads.shape
    heads = width // HEAD_DIM
    pairs = rows * (rows + tile) // 2
    return pl.pallas_call(
        partial(attend_back_kernel, scale=1.0 / math.sqrt(HEAD_DIM)),
        grid_spec=pltpu.PrefetchScalarGridSpec(
            num_scalar_prefetch=1,
            grid=(heads,),
            in_specs=[
                pl.BlockSpec((3, rows, HEAD_DIM), lambda head, scalars: (0, 0, head)),
                pl.BlockSpec((rows, HEAD_DIM), lambda head, scalars: (0, head)),
                pl.BlockSpec((8, rows), lambda head, scalars: (head, 0)),
                whole((rows, 128)),
                whole((rows, 128)),
                whole((8, rows)),
            ],
            out_specs=[
                pl.BlockSpec((rows, 3 * HEAD_DIM), lambda head, scalars: (0, head)),
                pl.BlockSpec((8, 3 * HEAD_DIM), lambda head, scalars: (0, head)),
            ],
            scratch_shapes=[
                pltpu.VMEM((rows, HEAD_DIM), wide),
                pltpu.VMEM((rows, HEAD_DIM), wide),
            ],
        ),
        out_shape=[
            jax.ShapeDtypeStruct((rows, 3 * width), low),
            jax.ShapeDtypeStruct((8, 3 * width), wide),
        ],
        compiler_params=pltpu.CompilerParams(vmem_limit_bytes=56 * 1024 * 1024),
        cost_estimate=pl.CostEstimate(
            flops=heads * pairs * HEAD_DIM * 10,
            bytes_accessed=rows * width * 16,
            transcendentals=heads * pairs,
        ),
        name="attend_back",
    )(scalars, packed, grads, log_total, cosine, sine, info)


def tree_info(lengths, parent, rows):
    labels = jnp.arange(SEGS)
    ends = jnp.sum(jnp.where(labels[None, :] <= labels[:, None], lengths[None, :], 0), axis=1)
    starts = ends - lengths
    hot_parent = parent[:, None] == labels[None, :]
    parent_start = jnp.sum(jnp.where(hot_parent, starts[None, :], 0), axis=1)
    parent_end = jnp.sum(jnp.where(hot_parent, ends[None, :], 0), axis=1)
    places = jnp.arange(rows, dtype=jnp.int32)
    inside = (places[None, :] >= starts[:, None]) & (places[None, :] < ends[:, None])
    pick = lambda table: jnp.sum(jnp.where(inside, table[:, None], 0), axis=0)
    spans = [pick(parent_start), pick(parent_end), pick(starts)]
    return jnp.stack(spans + [places] * 5).astype(jnp.int32), ends[0]


def rotary_tables(depth):
    half_rot = ROTARY // 2
    lane = jnp.arange(128)
    frequency = jnp.power(10000.0, -2.0 * (lane % half_rot).astype(wide) / ROTARY)
    frequency = jnp.where(lane < ROTARY, frequency, 0.0)
    angles = depth.astype(wide)[:, None] * frequency[None, :]
    return jnp.cos(angles), jnp.sin(angles)


def on_device_split(
    residual,
    out_grad,
    path_depth,
    seg_lengths,
    parents,
    attn_norm_gain,
    attn_norm_bias,
    ffn_norm_gain,
    ffn_norm_bias,
    qkv_weight,
    qkv_bias,
    dense_weight,
    dense_bias,
    up_weight,
    up_bias,
    down_weight,
    down_bias,
):
    core = lax.axis_index("ctx")
    line = lax.axis_index("tp")
    held_rows, held_width = residual.shape
    rows = 2 * held_rows
    width = 4 * held_width

    norm_rows = jnp.stack([attn_norm_gain, attn_norm_bias, ffn_norm_gain, ffn_norm_bias] * 4)
    pieces = gather_line(jnp.concatenate([residual, norm_rows], axis=0), "tp")
    twins = [trade(piece[:held_rows], "ctx", 1) for piece in pieces]
    other_depth = trade(path_depth, "ctx", 1)

    def share(weight, dim_split, dim_join):
        mine = half_of(weight, core, dim_split)
        theirs = trade(half_of(weight, 1 - core, dim_split), "ctx", 1)
        return join_cores(mine, theirs, core, dim_join)

    def gather_fsdp(weight, dim):
        return lax.all_gather(weight, "fsdp", axis=dim, tiled=True)

    up_full = gather_fsdp(share(up_weight, 1, 0), 0)
    qkv_full = gather_fsdp(share(qkv_weight, 1, 0), 0)
    down_full = gather_fsdp(share(down_weight, 0, 1), 1)
    dense_full = gather_fsdp(share(dense_weight, 0, 1), 1)
    qkv_shift = half_of(qkv_bias, core, 0).astype(wide)
    up_shift = half_of(up_bias, core, 0).astype(wide)

    info, trunk_end = tree_info(seg_lengths[0], parents[0], rows)
    scalars = jnp.stack([core, trunk_end]).astype(jnp.int32)
    cosine, sine = rotary_tables(jnp.concatenate([path_depth, other_depth]))

    norm_terms = lay_out([piece[held_rows : held_rows + 8] for piece in pieces], line, 1).astype(wide)
    rows_low = jnp.concatenate(
        [lay_out([piece[:held_rows] for piece in pieces], line, 1), lay_out(twins, line, 1)], axis=0
    )
    rows_wide = rows_low.astype(wide)
    mean = jnp.mean(rows_wide, axis=1, keepdims=True)
    centred = rows_wide - mean
    inverse_scale = lax.rsqrt(jnp.mean(centred * centred, axis=1, keepdims=True) + norm_epsilon)
    normed = centred * inverse_scale
    attn_in = (normed * norm_terms[0:1] + norm_terms[1:2]).astype(low)
    ffn_in = (normed * norm_terms[2:3] + norm_terms[3:4]).astype(low)

    joined = jnp.dot(attn_in, qkv_full, preferred_element_type=wide) + qkv_shift
    packed, attended, log_total = attend(scalars, joined, cosine, sine, info)

    hidden_pre = jnp.dot(ffn_in, up_full, preferred_element_type=wide) + up_shift
    phi = 0.5 * (1.0 + lax.erf(hidden_pre * math.sqrt(0.5)))
    hidden = (hidden_pre * phi).astype(low)

    def branches(first, last):
        return jnp.dot(attended[first:last], dense_full, preferred_element_type=wide) + jnp.dot(
            hidden[first:last], down_full, preferred_element_type=wide
        )

    for_twin = trade(branches(held_rows, rows).astype(low), "ctx", 1)
    chip_out = branches(0, held_rows) + for_twin.astype(wide)
    shared_out = scatter_line(chip_out, "tp", 1)
    output = (
        residual.astype(wide) + shared_out + dense_bias.astype(wide) + down_bias.astype(wide)
    ).astype(low)

    grad_pieces = gather_line(out_grad, "tp")
    grad_twins = [trade(piece, "ctx", 1) for piece in grad_pieces]
    cotangent = jnp.concatenate(
        [lay_out(grad_pieces, line, 1), lay_out(grad_twins, line, 1)], axis=0
    )

    def reduce_fsdp(grad, dim_split, dim_join):
        mine = lax.psum_scatter(grad.astype(low), "fsdp", scatter_dimension=dim_join, tiled=True)
        theirs = trade(half_of(mine, 1 - core, dim_join), "ctx", 1)
        return join_cores(half_of(mine, core, dim_join), theirs, core, dim_split).astype(wide)

    grad_hidden = contract(cotangent, down_full, (1, 1))
    slope = phi + hidden_pre * (jnp.exp(-0.5 * hidden_pre * hidden_pre) * (1.0 / math.sqrt(2.0 * math.pi)))
    grad_pre = (grad_hidden * slope).astype(low)
    grad_up_bias = jnp.sum(grad_pre.astype(wide), axis=0)
    down_weight_grad = reduce_fsdp(contract(hidden, cotangent, (0, 0)), 0, 1)
    up_weight_grad = reduce_fsdp(contract(ffn_in, grad_pre, (0, 0)), 1, 0)
    grad_ffn_in = contract(grad_pre, up_full, (1, 1))

    dense_weight_grad = reduce_fsdp(contract(attended, cotangent, (0, 0)), 0, 1)
    grad_attended = contract(cotangent, dense_full, (1, 1)).astype(low)
    grad_joined, bias_rows = attend_back(
        scalars, packed, grad_attended, log_total, cosine, sine, info
    )
    grad_qkv_bias = bias_rows[0]
    grad_attn_in = contract(grad_joined, qkv_full, (1, 1))
    qkv_weight_grad = reduce_fsdp(contract(attn_in, grad_joined, (0, 0)), 1, 0)

    mixed = grad_attn_in * norm_terms[0:1] + grad_ffn_in * norm_terms[2:3]
    row_sums = jnp.stack([jnp.sum(mixed, axis=1), jnp.sum(mixed * normed, axis=1)])
    norm_sums = jnp.stack(
        [
            jnp.sum(grad_attn_in * normed, axis=0),
            jnp.sum(grad_attn_in, axis=0),
            jnp.sum(grad_ffn_in * normed, axis=0),
            jnp.sum(grad_ffn_in, axis=0),
        ]
    )
    mixed_twin = trade(mixed[held_rows:].astype(low), "ctx", 1)
    shared_mixed = scatter_line(mixed[:held_rows] + mixed_twin.astype(wide), "tp", 1)

    row_total = row_sums[:, :held_rows] + trade(row_sums[:, held_rows:], "ctx", 1)
    for bit in (1, 2):
        row_total = row_total + trade(row_total, "tp", bit)
    row_means = row_total / width

    held_grad_sum = jnp.sum(out_grad.astype(wide), axis=0)
    columns = jnp.concatenate([norm_sums.reshape(-1), held_grad_sum, grad_qkv_bias, grad_up_bias])
    for bit in (1, 2):
        columns = columns + trade(columns, "fsdp", bit)
    other_columns = trade(columns, "ctx", 1)
    summed = 4 * width + held_width
    together = columns[:summed] + other_columns[:summed]
    out_bias_grad = together[4 * width :]
    norm_total = together[: 4 * width].reshape(4, width)
    for bit in (1, 2):
        norm_total = norm_total + trade(norm_total, "tp", bit)
    norm_total = block_of(norm_total, line, 1, 4)
    parts = qkv_bias.shape[0] // 2
    qkv_bias_grad = join_cores(
        columns[summed : summed + parts], other_columns[summed : summed + parts], core, 0
    )
    up_bias_grad = join_cores(columns[summed + parts :], other_columns[summed + parts :], core, 0)

    own_scale = inverse_scale[:held_rows]
    own_normed = (residual.astype(wide) - mean[:held_rows]) * own_scale
    back = own_scale * (
        shared_mixed - row_means[0][:, None] - own_normed * row_means[1][:, None]
    )
    input_grad = (out_grad.astype(wide) + back).astype(low)
    return (
        output,
        input_grad,
        norm_total[0],
        norm_total[1],
        norm_total[2],
        norm_total[3],
        qkv_weight_grad,
        qkv_bias_grad,
        dense_weight_grad,
        out_bias_grad,
        up_weight_grad,
        up_bias_grad,
        down_weight_grad,
        out_bias_grad,
    )


def splits_heads(mesh):
    return mesh.shape["tp"] == 4 and mesh.shape["fsdp"] == 4 and mesh.shape["ctx"] == 2


def solution(mesh):
    placed = (
        P(("fsdp", "ctx"), "tp"),
        P(("fsdp", "ctx"), "tp"),
        P(("fsdp", "ctx")),
        P("fsdp", None),
        P("fsdp", None),
        P("tp"),
        P("tp"),
        P("tp"),
        P("tp"),
        P(("fsdp", "ctx"), "tp"),
        P("tp"),
        P("tp", ("fsdp", "ctx")),
        P("tp"),
        P(("fsdp", "ctx"), "tp"),
        P("tp"),
        P("tp", ("fsdp", "ctx")),
        P("tp"),
    )
    return jax.shard_map(
        on_device_split if splits_heads(mesh) else on_device,
        mesh=mesh,
        in_specs=placed,
        out_specs=(
            P(("fsdp", "ctx"), "tp"),
            P(("fsdp", "ctx"), "tp"),
            P("tp"),
            P("tp"),
            P("tp"),
            P("tp"),
            P(("fsdp", "ctx"), "tp"),
            P("tp"),
            P("tp", ("fsdp", "ctx")),
            P("tp"),
            P(("fsdp", "ctx"), "tp"),
            P("tp"),
            P("tp", ("fsdp", "ctx")),
            P("tp"),
        ),
        check_vma=False,
    )
```

```python
from functools import partial
import math

import jax
import jax.numpy as jnp
from jax import lax
from jax.experimental import pallas as pl
from jax.experimental.pallas import tpu as pltpu
from jax.sharding import PartitionSpec as P

HEAD_DIM = 256
ROTARY = 64
SEGS = 13


norm_epsilon = 1e-05
masked_score = -1e30
block_limit = 512


def from_behind(x, axis, by):
    peers = lax.axis_size(axis)
    pairs = [(i, i + by) for i in range(peers) if 0 <= i + by < peers]
    return lax.ppermute(x, axis, pairs)


def rotary(vectors, places):
    half_rot = ROTARY // 2
    frequency = jnp.power(10000.0, -2.0 * jnp.arange(half_rot).astype(jnp.float32) / ROTARY)
    angles = places.astype(jnp.float32)[:, None] * frequency[None, :]
    cosine = jnp.cos(angles)[:, None, :]
    sine_part = jnp.sin(angles)[:, None, :]
    first_half = vectors[..., :half_rot]
    second_half = vectors[..., half_rot:ROTARY]
    return jnp.concatenate(
        [
            first_half * cosine - second_half * sine_part,
            second_half * cosine + first_half * sine_part,
            vectors[..., ROTARY:],
        ],
        axis=-1,
    )


def tree_tables(lengths, parent):
    starts = jnp.cumsum(lengths) - lengths
    labels = jnp.arange(SEGS)
    grand_parent = jnp.sum(
        jnp.where(parent[:, None] == labels[None, :], parent[None, :], 0), axis=1
    )
    ancestor = (
        (labels[None, :] == labels[:, None])
        | (labels[None, :] == parent[:, None])
        | (labels[None, :] == grand_parent[:, None])
    )
    return (starts, ancestor.astype(jnp.float32))


def segment_onehot(places, starts):
    membership = jnp.sum((places[:, None] >= starts[None, :]).astype(jnp.int32), axis=1) - 1
    return (membership[:, None] == jnp.arange(SEGS)[None, :]).astype(jnp.float32)


def visible(hot_query, place_query, hot_key, place_key, ancestor):
    reachable = jnp.dot(jnp.dot(hot_query, ancestor), hot_key.T)
    return (reachable > 0.5) & (place_key[None, :] <= place_query[:, None])


def on_device(
    residual,
    out_grad,
    path_depth,
    seg_lengths,
    parents,
    attn_norm_gain,
    attn_norm_bias,
    ffn_norm_gain,
    ffn_norm_bias,
    qkv_weight,
    qkv_bias,
    dense_weight,
    dense_bias,
    up_weight,
    up_bias,
    down_weight,
    down_bias,
):
    row_count = residual.shape[0]
    local_width = residual.shape[1]
    head_count = qkv_weight.shape[1] // (3 * HEAD_DIM)
    score_scale = 1.0 / math.sqrt(HEAD_DIM)
    ctx_index = lax.axis_index("ctx")
    tp_index = lax.axis_index("tp")
    norm_stack = jnp.stack([attn_norm_gain, attn_norm_bias, ffn_norm_gain, ffn_norm_bias])
    full_rows, norm_terms = (
        lax.all_gather(residual, "tp", axis=1, tiled=True),
        lax.all_gather(norm_stack, "tp", axis=1, tiled=True),
    )
    norm_terms = norm_terms.astype(jnp.float32)
    qkv_full, up_full = (
        lax.all_gather(qkv_weight, ("fsdp", "ctx"), axis=0, tiled=True),
        lax.all_gather(up_weight, ("fsdp", "ctx"), axis=0, tiled=True),
    )
    dense_full, down_full = (
        lax.all_gather(dense_weight, ("fsdp", "ctx"), axis=1, tiled=True),
        lax.all_gather(down_weight, ("fsdp", "ctx"), axis=1, tiled=True),
    )
    rows_wide = full_rows.astype(jnp.float32)
    centred = rows_wide - jnp.mean(rows_wide, axis=1, keepdims=True)
    inverse_scale = lax.rsqrt(jnp.mean(centred * centred, axis=1, keepdims=True) + norm_epsilon)
    normed = centred * inverse_scale
    attn_in = (normed * norm_terms[0] + norm_terms[1]).astype(jnp.bfloat16)
    ffn_in = (normed * norm_terms[2] + norm_terms[3]).astype(jnp.bfloat16)
    joined = (
        jnp.dot(attn_in, qkv_full, preferred_element_type=jnp.float32)
        + qkv_bias.astype(jnp.float32)
    ).reshape(row_count, head_count, 3, HEAD_DIM)
    queries_pre = joined[:, :, 0]
    query_rows = rotary(queries_pre, path_depth).astype(jnp.bfloat16)
    key_rows = rotary(joined[:, :, 1], path_depth).astype(jnp.bfloat16)
    value_rows = joined[:, :, 2].astype(jnp.bfloat16)
    far_keys, far_values = from_behind((key_rows, value_rows), "ctx", 1)
    starts, ancestor = tree_tables(seg_lengths[0], parents[0])
    places = ctx_index * row_count + jnp.arange(row_count, dtype=jnp.int32)
    key_places = jnp.concatenate([places - row_count, places])
    hot_query = segment_onehot(places, starts)
    hot_key = segment_onehot(key_places, starts)
    all_keys = jnp.concatenate([far_keys, key_rows], axis=0)
    all_values = jnp.concatenate([far_values, value_rows], axis=0)
    block_starts = list(range(0, row_count, block_limit))

    def block_scores(block_start, block_size, key_set):
        key_span = row_count + block_start + block_size
        query_block = query_rows[block_start : block_start + block_size]
        scores = (
            jnp.einsum(
                "nhe,lhe->hnl", query_block, key_set[:key_span], preferred_element_type=jnp.float32
            )
            * score_scale
        )
        reachable = visible(
            hot_query[block_start : block_start + block_size],
            places[block_start : block_start + block_size],
            hot_key[:key_span],
            key_places[:key_span],
            ancestor,
        )
        return jnp.where(reachable[None], scores, masked_score)

    out_blocks = []
    log_totals = []
    for block_start in block_starts:
        block_size = min(block_limit, row_count - block_start)
        key_span = row_count + block_start + block_size
        scores = block_scores(block_start, block_size, all_keys)
        row_top = jnp.max(scores, axis=-1, keepdims=True)
        exp_scores = jnp.exp(scores - row_top)
        exp_total = jnp.sum(exp_scores, axis=-1, keepdims=True)
        attn_probs = exp_scores / exp_total
        out_blocks.append(
            jnp.einsum(
                "hnl,lhe->nhe",
                attn_probs.astype(jnp.bfloat16),
                all_values[:key_span],
                preferred_element_type=jnp.float32,
            )
        )
        log_totals.append(row_top + jnp.log(exp_total))
    attended = (
        jnp.concatenate(out_blocks, axis=0)
        .reshape(row_count, head_count * HEAD_DIM)
        .astype(jnp.bfloat16)
    )
    hidden_pre = jnp.dot(ffn_in, up_full, preferred_element_type=jnp.float32) + up_bias.astype(
        jnp.float32
    )
    hidden_wide, gelu_back = jax.vjp(partial(jax.nn.gelu, approximate=False), hidden_pre)
    hidden = hidden_wide.astype(jnp.bfloat16)
    partial_out = jnp.dot(attended, dense_full, preferred_element_type=jnp.float32) + jnp.dot(
        hidden, down_full, preferred_element_type=jnp.float32
    )
    shared_out = lax.psum_scatter(partial_out, "tp", scatter_dimension=1, tiled=True)
    output = (
        residual.astype(jnp.float32)
        + shared_out
        + dense_bias.astype(jnp.float32)
        + down_bias.astype(jnp.float32)
    ).astype(jnp.bfloat16)
    cotangent = lax.all_gather(out_grad, "tp", axis=1, tiled=True)
    grad_out_bias = jnp.sum(out_grad.astype(jnp.float32), axis=0)
    grad_dense_w = jnp.einsum("rf,rd->fd", attended, cotangent, preferred_element_type=jnp.float32)
    grad_down_w = jnp.einsum("rf,rd->fd", hidden, cotangent, preferred_element_type=jnp.float32)
    grad_attended = jnp.einsum(
        "rd,fd->rf", cotangent, dense_full, preferred_element_type=jnp.float32
    ).astype(jnp.bfloat16)
    grad_hidden = jnp.einsum("rd,fd->rf", cotangent, down_full, preferred_element_type=jnp.float32)
    grad_pre = gelu_back(grad_hidden)[0].astype(jnp.bfloat16)
    grad_up_w = jnp.einsum("rd,rf->df", ffn_in, grad_pre, preferred_element_type=jnp.float32)
    grad_up_b = jnp.sum(grad_pre.astype(jnp.float32), axis=0)
    grad_ffn_in = jnp.einsum("rf,df->rd", grad_pre, up_full, preferred_element_type=jnp.float32)
    key_set = all_keys
    grad_att_heads = grad_attended.reshape(row_count, head_count, HEAD_DIM)
    grad_query_parts = []
    grad_key_all = jnp.zeros((2 * row_count, head_count, HEAD_DIM), jnp.float32)
    grad_value_all = jnp.zeros((2 * row_count, head_count, HEAD_DIM), jnp.float32)
    for block_number, block_start in enumerate(block_starts):
        block_size = min(block_limit, row_count - block_start)
        key_span = row_count + block_start + block_size
        scores = block_scores(block_start, block_size, key_set)
        attn_probs = jnp.exp(scores - log_totals[block_number])
        grad_block = grad_att_heads[block_start : block_start + block_size]
        grad_value_all = grad_value_all.at[:key_span].add(
            jnp.einsum(
                "hnl,nhe->lhe",
                attn_probs.astype(jnp.bfloat16),
                grad_block,
                preferred_element_type=jnp.float32,
            )
        )
        grad_dots = jnp.einsum(
            "nhe,lhe->hnl", grad_block, all_values[:key_span], preferred_element_type=jnp.float32
        )
        row_delta = jnp.sum(attn_probs * grad_dots, axis=-1, keepdims=True)
        grad_scores = (attn_probs * (grad_dots - row_delta)).astype(jnp.bfloat16)
        grad_query_parts.append(
            jnp.einsum(
                "hnl,lhe->nhe", grad_scores, key_set[:key_span], preferred_element_type=jnp.float32
            )
            * score_scale
        )
        grad_key_all = grad_key_all.at[:key_span].add(
            jnp.einsum(
                "hnl,nhe->lhe",
                grad_scores,
                query_rows[block_start : block_start + block_size],
                preferred_element_type=jnp.float32,
            )
            * score_scale
        )
    arriving_keys, arriving_values = from_behind(
        (grad_key_all[:row_count], grad_value_all[:row_count]), "ctx", -1
    )
    grad_keys = grad_key_all[row_count:] + arriving_keys
    grad_values = grad_value_all[row_count:] + arriving_values
    grad_queries = jnp.concatenate(grad_query_parts, axis=0)
    rotated_unused, rotary_back = jax.vjp(lambda vectors: rotary(vectors, path_depth), queries_pre)
    grad_joined = (
        jnp.stack([rotary_back(grad_queries)[0], rotary_back(grad_keys)[0], grad_values], axis=2)
        .astype(jnp.bfloat16)
        .reshape(row_count, head_count * 3 * HEAD_DIM)
    )
    grad_qkv_w = jnp.einsum("rd,rf->df", attn_in, grad_joined, preferred_element_type=jnp.float32)
    grad_qkv_b = jnp.sum(grad_joined.astype(jnp.float32), axis=0)
    grad_attn_in = jnp.einsum(
        "rf,df->rd", grad_joined, qkv_full, preferred_element_type=jnp.float32
    )
    total_attn, total_ffn = lax.psum((grad_attn_in, grad_ffn_in), "tp")

    def norm_back(total_grad, gain_row):
        scaled = total_grad * gain_row
        mean_plain = jnp.mean(scaled, axis=1, keepdims=True)
        mean_normed = jnp.mean(scaled * normed, axis=1, keepdims=True)
        back_rows = inverse_scale * (scaled - mean_plain - normed * mean_normed)
        gain_grad = jnp.sum(total_grad * normed, axis=0)
        shift_grad = jnp.sum(total_grad, axis=0)
        return (
            lax.dynamic_slice_in_dim(back_rows, tp_index * local_width, local_width, 1),
            lax.dynamic_slice_in_dim(gain_grad, tp_index * local_width, local_width, 0),
            lax.dynamic_slice_in_dim(shift_grad, tp_index * local_width, local_width, 0),
        )

    back_attn, attn_gain_grad, attn_shift_grad = norm_back(total_attn, norm_terms[0])
    back_ffn, ffn_gain_grad, ffn_shift_grad = norm_back(total_ffn, norm_terms[2])
    norm_grads = jnp.stack([attn_gain_grad, attn_shift_grad, ffn_gain_grad, ffn_shift_grad])
    back_total = back_attn + back_ffn
    input_grad = (out_grad.astype(jnp.float32) + back_total).astype(jnp.bfloat16)
    qkv_bias_grad, up_bias_grad, out_bias_grad, norm_totals = lax.psum(
        (grad_qkv_b, grad_up_b, grad_out_bias, norm_grads), ("fsdp", "ctx")
    )
    qkv_weight_grad, up_weight_grad = (
        lax.psum_scatter(
            grad_qkv_w.astype(jnp.bfloat16), ("fsdp", "ctx"), scatter_dimension=0, tiled=True
        ).astype(jnp.float32),
        lax.psum_scatter(
            grad_up_w.astype(jnp.bfloat16), ("fsdp", "ctx"), scatter_dimension=0, tiled=True
        ).astype(jnp.float32),
    )
    dense_weight_grad, down_weight_grad = (
        lax.psum_scatter(
            grad_dense_w.astype(jnp.bfloat16), ("fsdp", "ctx"), scatter_dimension=1, tiled=True
        ).astype(jnp.float32),
        lax.psum_scatter(
            grad_down_w.astype(jnp.bfloat16), ("fsdp", "ctx"), scatter_dimension=1, tiled=True
        ).astype(jnp.float32),
    )
    return (
        output,
        input_grad,
        norm_totals[0],
        norm_totals[1],
        norm_totals[2],
        norm_totals[3],
        qkv_weight_grad,
        qkv_bias_grad,
        dense_weight_grad,
        out_bias_grad,
        up_weight_grad,
        up_bias_grad,
        down_weight_grad,
        out_bias_grad,
    )


low = jnp.bfloat16
wide = jnp.float32
tile = 256
megabyte = 1024 * 1024
pace = 16


def trade(x, axis, bit):
    peers = lax.axis_size(axis)
    return lax.ppermute(x, axis, [(i, i ^ bit) for i in range(peers)])


def after(x, *earlier):
    return lax.optimization_barrier((x, *earlier))[0]


def meet(*values):
    return lax.optimization_barrier(values)


def block_of(x, index, dim, blocks):
    width = x.shape[dim] // blocks
    return lax.dynamic_slice_in_dim(x, index * width, width, dim)


def lay_out(pieces, place, dim):
    width = pieces[0].shape[dim]
    shape = list(pieces[0].shape)
    shape[dim] = width * 4
    whole = jnp.zeros(shape, pieces[0].dtype)
    for step, piece in enumerate(pieces):
        whole = lax.dynamic_update_slice_in_dim(whole, piece, (place ^ step) * width, dim)
    return whole


def plane_corner(near, far, axis):
    half = near.shape[0] // 2
    corner = [trade(far[:half], axis, 1), trade(near[half:], axis, 2)]
    return jnp.concatenate(corner, axis=0)


def scatter_plane(total, axis, dim):
    place = lax.axis_index(axis)
    own, near, far, corner = (block_of(total, place ^ k, dim, 4) for k in range(4))
    half = own.shape[0] // 2
    upper = trade(corner[:half].astype(low), axis, 1)
    lower = trade(corner[half:].astype(low), axis, 2)
    add = lambda a, b: (a.astype(wide) + b.astype(wide)).astype(low)
    far = jnp.concatenate([add(far[:half], upper), far[half:].astype(low)], axis=0)
    near = jnp.concatenate([near[:half].astype(low), add(near[half:], lower)], axis=0)
    far_in = trade(far, axis, 2)
    near_in = trade(near, axis, 1)
    return (own.astype(wide) + near_in.astype(wide) + far_in.astype(wide)).astype(low), (far, near)


def half_of(x, index, dim):
    return block_of(x, index, dim, 2)


def join_cores(mine, theirs, core, dim):
    first = jnp.where(core == 0, mine, theirs)
    second = jnp.where(core == 0, theirs, mine)
    return jnp.concatenate([first, second], axis=dim)


def contract(a, b, dims):
    return lax.dot_general(a, b, ((dims[:1], dims[1:]), ((), ())), preferred_element_type=wide)


def place_of(index, size):
    return pl.ds(pl.multiple_of(index * size, size), size)


def fold_rows(x):
    return jnp.sum(x.reshape(x.shape[0] // 8, 8, x.shape[1]), axis=0)


def fixed(shape):
    return pl.BlockSpec(
        shape, lambda step, scalars: (0,) * len(shape), pipeline_mode=pl.Buffered(1)
    )


def kept(shape):
    return pl.BlockSpec(shape, lambda step, scalars: (0,) * len(shape))


def by_row(width):
    return pl.BlockSpec((tile, width), lambda step, scalars: (step, 0))


def by_column(rows, width, first=0):
    return pl.BlockSpec((rows, width), lambda step, scalars: (0, jnp.maximum(step - first, 0)))


def call(kernel, name, steps, in_specs, out_specs, out_shape, operands, flops, moved, scratch=(), exps=0):
    return pl.pallas_call(
        kernel,
        grid_spec=pltpu.PrefetchScalarGridSpec(
            num_scalar_prefetch=1,
            grid=(steps,),
            in_specs=in_specs,
            out_specs=out_specs,
            scratch_shapes=list(scratch),
        ),
        out_shape=out_shape,
        compiler_params=pltpu.CompilerParams(vmem_limit_bytes=56 * megabyte),
        cost_estimate=pl.CostEstimate(
            flops=flops * pace, bytes_accessed=moved * pace, transcendentals=exps * pace
        ),
        name=name,
    )(*operands)


def shaped(*shape, kind=low):
    return jax.ShapeDtypeStruct(shape, kind)


def own_first(piece, core):
    return piece[:, place_of(core, tile)], piece[:, place_of(1 - core, tile)]


def norm_kernel(scalars, *refs):
    pieces, terms = refs[:4], refs[4:8]
    attn_out, ffn_out, stats_out, terms_out = refs[8:]
    width = 8 * tile
    parts = [piece[...].astype(wide) for piece in pieces]
    total = sum(jnp.sum(part, axis=1, keepdims=True) for part in parts)
    mean = total * (1.0 / width)
    spread = sum(jnp.sum((part - mean) * (part - mean), axis=1, keepdims=True) for part in parts)
    inverse = lax.rsqrt(spread * (1.0 / width) + norm_epsilon)
    for k in range(4):
        block = scalars[2] ^ k
        for half in range(2):
            side = scalars[0] if half == 0 else 1 - scalars[0]
            source = place_of(side, tile)
            columns = place_of(4 * half + block, tile)
            normed = (pieces[k][:, source].astype(wide) - mean) * inverse
            term = terms[k][:, source].astype(wide)
            attn_out[:, columns] = (normed * term[0:1] + term[1:2]).astype(low)
            ffn_out[:, columns] = (normed * term[2:3] + term[3:4]).astype(low)
    lane = lax.broadcasted_iota(jnp.int32, stats_out.shape, 1)
    stats_out[...] = jnp.where(lane < 64, mean, inverse)

    @pl.when(pl.program_id(0) == 0)
    def _():
        for k in range(4):
            for half in range(2):
                side = scalars[0] if half == 0 else 1 - scalars[0]
                columns = place_of(4 * half + (scalars[2] ^ k), tile)
                terms_out[:, columns] = terms[k][0:8, place_of(side, tile)].astype(wide)


def norm(scalars, pieces, terms):
    rows, width = pieces[0].shape
    term = fixed(terms[0].shape)
    return call(
        norm_kernel,
        "norm",
        rows // tile,
        [by_row(width)] * 4 + [term] * 4,
        [by_row(4 * width), by_row(4 * width), by_row(128), kept((8, 4 * width))],
        [
            shaped(rows, 4 * width),
            shaped(rows, 4 * width),
            shaped(rows, 128, kind=wide),
            shaped(8, 4 * width, kind=wide),
        ],
        (scalars, *pieces, *terms),
        rows * width * 40,
        rows * width * 24,
    )


def assemble_kernel(scalars, own, near, far, upper, lower, first_out, second_out):
    step = pl.program_id(0)
    split = first_out.shape[1]
    middle = upper.shape[0]

    def write(piece, rows):
        first_out[rows, :] = piece[:, :split]
        second_out[rows, :] = piece[:, split:]

    for k, piece in enumerate((own, near, far)):
        pl.when(step == k)(partial(write, piece, slice(None)))

    @pl.when(step == 3)
    def _():
        write(upper, slice(0, middle))
        write(lower, slice(middle, 2 * middle))


def assemble(scalars, pieces, halves, split):
    rows, columns = pieces[0].shape
    place = lambda step, scalars: (scalars[3] ^ step, 0)
    return call(
        assemble_kernel,
        "assemble",
        4,
        [fixed((rows, columns))] * 3 + [fixed((rows // 2, columns))] * 2,
        [pl.BlockSpec((rows, split), place), pl.BlockSpec((rows, columns - split), place)],
        [shaped(4 * rows, split), shaped(4 * rows, columns - split)],
        (scalars, *pieces, *halves),
        rows * columns,
        rows * columns * 16,
    )


def double(rows_in, own, other):
    half = rows_in.shape[1] // 2
    return contract(rows_in[:, :half], own, (1, 0)) + contract(rows_in[:, half:], other, (1, 0))


def heads_kernel(scalars, rows_in, own, other, shift_row, cosine, sine, mine, theirs):
    step = pl.program_id(0)
    joined = double(rows_in, own[...], other[...]) + shift_row[0:1, :]
    part = lax.rem(step, 3)

    def write(vectors):
        @pl.when(step < 3)
        def _():
            theirs[0] = vectors.astype(low)

        @pl.when(step >= 3)
        def _():
            mine[0] = vectors.astype(low)

    @pl.when(part < 2)
    def _():
        write(turn(joined, cosine[...], sine[...], 1.0))

    @pl.when(part == 2)
    def _():
        write(joined)


def heads(scalars, attn_in, weights, shift_row, cosine, sine):
    rows, width = attn_in.shape

    def column(step, scalars):
        return jnp.where(step < 3, 1 - scalars[0], scalars[0]) * 3 + lax.rem(step, 3)

    weight = pl.BlockSpec((width // 2, HEAD_DIM), lambda step, scalars: (0, column(step, scalars)))
    shift = pl.BlockSpec((1, HEAD_DIM), lambda step, scalars: (0, column(step, scalars)))
    last = lambda step, scalars: (jnp.maximum(step - 3, 0), 0, 0)
    early = lambda step, scalars: (jnp.minimum(step, 2), 0, 0)
    return call(
        heads_kernel,
        "heads",
        6,
        [fixed(attn_in.shape), weight, weight, shift, fixed((rows, 128)), fixed((rows, 128))],
        [pl.BlockSpec((1, rows, HEAD_DIM), last), pl.BlockSpec((1, rows, HEAD_DIM), early)],
        [shaped(3, rows, HEAD_DIM)] * 2,
        (scalars, attn_in, *weights, shift_row, cosine, sine),
        12 * rows * width * HEAD_DIM,
        2 * (rows * width + 6 * width * HEAD_DIM + 6 * rows * HEAD_DIM),
    )


def expand_kernel(scalars, rows_in, own, other, shift_row, hidden, slope):
    pre = double(rows_in, own[...], other[...]) + shift_row[0:1, :]
    phi = 0.5 + 0.5 * lax.erf(pre * math.sqrt(0.5))
    density = jnp.exp(pre * pre * -0.5) * (1.0 / math.sqrt(2.0 * math.pi))
    hidden[...] = (pre * phi).astype(low)
    slope[...] = (phi + pre * density).astype(low)


def expand(scalars, ffn_in, weights, shift_row):
    rows, width = ffn_in.shape
    columns = weights[0].shape[1]
    return call(
        expand_kernel,
        "expand",
        columns // tile,
        [fixed(ffn_in.shape)] + [by_column(width // 2, tile)] * 2 + [by_column(1, tile)],
        [by_column(rows, tile)] * 2,
        [shaped(rows, columns), shaped(rows, columns)],
        (scalars, ffn_in, *weights, shift_row),
        2 * rows * width * columns,
        2 * (rows * width + width * columns + 2 * rows * columns),
        exps=2 * rows * columns,
    )


def project_kernel(scalars, mine, theirs, hidden, dense_own, dense_other, down_own, down_other, out):
    for half, dense, down in ((0, dense_own, down_own), (1, dense_other, down_other)):
        total = contract(hidden[...], down[...], (1, 0))
        total += contract(mine[...], dense[place_of(scalars[0], HEAD_DIM), :], (1, 0))
        total += contract(theirs[...], dense[place_of(1 - scalars[0], HEAD_DIM), :], (1, 0))
        out[:, half * tile : (half + 1) * tile] = total.astype(out.dtype)


def project(scalars, mine, theirs, hidden, dense, down):
    rows = hidden.shape[0]
    depth = dense[0].shape[0] + down[0].shape[0]
    weight = lambda x: by_column(x.shape[0], tile)
    return call(
        project_kernel,
        "project",
        4,
        [fixed(mine.shape), fixed(mine.shape), fixed(hidden.shape)]
        + [weight(x) for x in (*dense, *down)],
        [by_column(rows, 2 * tile)],
        [shaped(rows, 8 * tile)],
        (scalars, mine, theirs, hidden, *dense, *down),
        16 * rows * tile * depth,
        2 * (rows * 8 * tile + depth * 8 * tile + rows * depth),
    )[0]


def hidden_back_kernel(scalars, *refs):
    pieces, (slope, dense_own, dense_other, down_own, down_other) = refs[:4], refs[4:9]
    cotangent, pre_grad, mine, theirs, bias_grad = refs[9:]
    step = pl.program_id(0)
    half = cotangent.shape[1] // 2

    @pl.when(step == 0)
    def _():
        for k in range(4):
            block = scalars[2] ^ k
            own, other = own_first(pieces[k], scalars[0])
            cotangent[:, place_of(block, tile)] = own
            cotangent[:, place_of(4 + block, tile)] = other

    def back(own, other):
        return contract(cotangent[:, :half], own[...], (1, 1)) + contract(
            cotangent[:, half:], other[...], (1, 1)
        )

    @pl.when(step == 0)
    def _():
        theirs[...] = back(dense_own, dense_other).astype(low)

    @pl.when(step == 1)
    def _():
        mine[...] = back(dense_own, dense_other).astype(low)

    @pl.when(step >= 2)
    def _():
        grad = (back(down_own, down_other) * slope[...].astype(wide)).astype(low)
        pre_grad[...] = grad
        bias_grad[...] = fold_rows(grad.astype(wide))


def hidden_back(scalars, pieces, slope, dense, down):
    rows, width = pieces[0].shape
    hidden = down[0].shape[0]
    heads_weight = pl.BlockSpec(
        (HEAD_DIM, 2 * width),
        lambda step, scalars: (jnp.where(step == 0, 1 - scalars[0], scalars[0]), 0),
    )
    weight = pl.BlockSpec(
        (tile, 2 * width), lambda step, scalars: (jnp.maximum(step - 2, 0), 0)
    )
    return call(
        hidden_back_kernel,
        "hidden_back",
        2 + hidden // tile,
        [fixed((rows, width))] * 4
        + [by_column(rows, tile, 2), heads_weight, heads_weight, weight, weight],
        [
            kept((rows, 4 * width)),
            by_column(rows, tile, 2),
            kept((rows, HEAD_DIM)),
            kept((rows, HEAD_DIM)),
            by_column(8, tile, 2),
        ],
        [
            shaped(rows, 4 * width),
            shaped(rows, hidden),
            shaped(rows, HEAD_DIM),
            shaped(rows, HEAD_DIM),
            shaped(8, hidden, kind=wide),
        ],
        (scalars, *pieces, slope, *dense, *down),
        8 * rows * width * (2 * HEAD_DIM + hidden),
        rows * width * 16 + 8 * width * hidden + rows * hidden * 4,
    )


def mix_kernel(
    scalars, mine, theirs, pre_grad, qkv_own, qkv_other, up_own, up_other, terms_own, terms_other,
    stats, first_piece, second_piece, first_out, second_out, sums_own, sums_other, row_sums
):
    mean = stats[:, 0:1]
    inverse = stats[:, 64:65]
    step = pl.program_id(0)

    def run(piece, out):
        plain = None
        for half, qkv, up, terms, sums in (
            (0, qkv_own, up_own, terms_own, sums_own),
            (1, qkv_other, up_other, terms_other, sums_other),
        ):
            attn = contract(mine[...], qkv[:, place_of(scalars[0], 3 * HEAD_DIM)], (1, 1))
            attn += contract(theirs[...], qkv[:, place_of(1 - scalars[0], 3 * HEAD_DIM)], (1, 1))
            ffn = contract(pre_grad[...], up[...], (1, 1))
            side = scalars[0] if half == 0 else 1 - scalars[0]
            normed = (piece[:, place_of(side, tile)].astype(wide) - mean) * inverse
            mixed = attn * terms[0:1, :] + ffn * terms[2:3, :]
            sums[0:8, :] = fold_rows(attn * normed)
            sums[8:16, :] = fold_rows(attn)
            sums[16:24, :] = fold_rows(ffn * normed)
            sums[24:32, :] = fold_rows(ffn)
            out[:, half * tile : (half + 1) * tile] = mixed.astype(out.dtype)
            weighed = mixed * normed
            here = mixed[:, :128] + mixed[:, 128:], weighed[:, :128] + weighed[:, 128:]
            plain = here if plain is None else (plain[0] + here[0], plain[1] + here[1])
        lane = lax.broadcasted_iota(jnp.int32, row_sums.shape, 1)
        together = jnp.where(
            lane < 64,
            jnp.sum(plain[0], axis=1, keepdims=True),
            jnp.sum(plain[1], axis=1, keepdims=True),
        )
        return together

    @pl.when(step == 0)
    def _():
        row_sums[...] = run(first_piece, first_out)

    @pl.when(step == 1)
    def _():
        row_sums[...] += run(second_piece, second_out)


def mix(scalars, mine, theirs, pre_grad, qkv, up, terms, stats, pieces, order, kinds):
    rows = pre_grad.shape[0]
    width = pieces[0].shape[1]
    depth = qkv[0].shape[1] + up[0].shape[1]

    def block(step, scalars):
        return scalars[2] ^ jnp.where(step == 0, order[0], order[1])

    weight = lambda x: pl.BlockSpec((tile, x.shape[1]), lambda step, scalars: (block(step, scalars), 0))
    term = lambda first: pl.BlockSpec((8, tile), lambda step, scalars: (0, first + block(step, scalars)))
    sums = pl.BlockSpec((32, tile), lambda step, scalars: (0, step))
    return call(
        mix_kernel,
        "mix",
        2,
        [fixed(mine.shape), fixed(mine.shape), fixed(pre_grad.shape)]
        + [weight(x) for x in (*qkv, *up)]
        + [term(0), term(4), fixed((rows, 128))]
        + [fixed((rows, width))] * 2,
        [kept((rows, width))] * 2 + [sums, sums, kept((rows, 128))],
        [shaped(rows, width, kind=kind) for kind in kinds]
        + [shaped(32, 2 * tile, kind=wide)] * 2
        + [shaped(rows, 128, kind=wide)],
        (scalars, mine, theirs, pre_grad, *qkv, *up, terms, terms, stats, pieces[order[0]], pieces[order[1]]),
        4 * rows * width * depth,
        2 * (4 * rows * width + 2 * depth * width + rows * depth),
    )


def attend_kernel(scalars, mine, theirs, info, packed, own_out, twin_out, log_total, natural, scale):
    rows = natural.shape[0]
    blocks = rows // tile
    own = place_of(scalars[0], rows // 2)
    twin = place_of(1 - scalars[0], rows // 2)
    for part in range(3):
        packed[part, own, :] = mine[part]
        packed[part, twin, :] = theirs[part]
    for block in range(blocks):
        span = (block + 1) * tile
        query = packed[0, block * tile : span, :]
        about = info[:, block * tile : span]
        scores = scores_of(packed[1, :span, :], query, about, scalars[1], block * tile, scale)
        top = jnp.max(scores, axis=0, keepdims=True)
        powers = jnp.exp(scores - top)
        total = jnp.sum(powers, axis=0, keepdims=True)
        probs = (powers * (1.0 / total)).astype(low)
        natural[block * tile : span, :] = contract(probs, packed[2, :span, :], (0, 0)).astype(low)
        log_total[0:1, block * tile : span] = top + jnp.log(total)
    own_out[...] = natural[own, :]
    twin_out[...] = natural[twin, :]


def attend(scalars, mine, theirs, info):
    held = mine.shape[1]
    rows = 2 * held
    pairs = rows * (rows + tile) // 2
    return call(
        partial(attend_kernel, scale=1.0 / math.sqrt(HEAD_DIM)),
        "attend",
        1,
        [fixed(mine.shape), fixed(mine.shape), fixed((8, rows))],
        [kept((3, rows, HEAD_DIM)), kept((held, HEAD_DIM)), kept((held, HEAD_DIM)), kept((8, rows))],
        [
            shaped(3, rows, HEAD_DIM),
            shaped(held, HEAD_DIM),
            shaped(held, HEAD_DIM),
            shaped(8, rows, kind=wide),
        ],
        (scalars, mine, theirs, info),
        pairs * HEAD_DIM * 4,
        rows * HEAD_DIM * 16,
        scratch=[pltpu.VMEM((rows, HEAD_DIM), low)],
        exps=pairs,
    )


def attend_back_kernel(
    scalars, packed, own_grads, twin_grads, log_total, cosine, sine, info, own_out, twin_out,
    bias_grad, grads, natural, key_grad, value_grad, scale
):
    rows = grads.shape[0]
    blocks = rows // tile
    shift = scalars[0] * (blocks // 2)
    own = place_of(scalars[0], rows // 2)
    twin = place_of(1 - scalars[0], rows // 2)
    grads[own, :] = own_grads[...]
    grads[twin, :] = twin_grads[...]
    bias_total = jnp.zeros((8, 3 * HEAD_DIM), wide)
    for block in reversed(range(blocks)):
        span = (block + 1) * tile
        before = block * tile
        query = packed[0, before:span, :]
        about = info[:, before:span]
        there = place_of(lax.rem(block + shift, blocks), tile)
        grad = grads[before:span, :]
        scores = scores_of(packed[1, :span, :], query, about, scalars[1], before, scale)
        probs = jnp.exp(scores - log_total[0:1, before:span])
        value_part = contract(probs.astype(low), grad, (1, 0))
        dots = contract(packed[2, :span, :], grad, (1, 1))
        delta = jnp.sum(probs * dots, axis=0, keepdims=True)
        score_grad = (probs * (dots - delta)).astype(low)
        query_grad = contract(score_grad, packed[1, :span, :], (0, 0)) * scale
        key_part = contract(score_grad, query, (1, 0)) * scale
        if block == blocks - 1:
            key_grad[...] = key_part
            value_grad[...] = value_part
        else:
            key_grad[:span, :] += key_part
            value_grad[:span, :] += value_part
        parts = (
            turn(query_grad, cosine[there, :], sine[there, :], -1.0),
            turn(key_grad[before:span, :], cosine[there, :], sine[there, :], -1.0),
            value_grad[before:span, :],
        )
        together = jnp.concatenate(parts, axis=1).astype(low)
        natural[before:span, :] = together
        bias_total += fold_rows(together.astype(wide))
    bias_grad[...] = bias_total
    own_out[...] = natural[own, :]
    twin_out[...] = natural[twin, :]


def attend_back(scalars, packed, own_grads, twin_grads, log_total, cosine, sine, info):
    held = own_grads.shape[0]
    rows = 2 * held
    pairs = rows * (rows + tile) // 2
    return call(
        partial(attend_back_kernel, scale=1.0 / math.sqrt(HEAD_DIM)),
        "attend_back",
        1,
        [
            fixed((3, rows, HEAD_DIM)),
            fixed((held, HEAD_DIM)),
            fixed((held, HEAD_DIM)),
            fixed((8, rows)),
            fixed((rows, 128)),
            fixed((rows, 128)),
            fixed((8, rows)),
        ],
        [kept((held, 3 * HEAD_DIM)), kept((held, 3 * HEAD_DIM)), kept((8, 3 * HEAD_DIM))],
        [
            shaped(held, 3 * HEAD_DIM),
            shaped(held, 3 * HEAD_DIM),
            shaped(8, 3 * HEAD_DIM, kind=wide),
        ],
        (scalars, packed, own_grads, twin_grads, log_total, cosine, sine, info),
        pairs * HEAD_DIM * 10,
        rows * HEAD_DIM * 16,
        scratch=[
            pltpu.VMEM((rows, HEAD_DIM), low),
            pltpu.VMEM((rows, 3 * HEAD_DIM), low),
            pltpu.VMEM((rows, HEAD_DIM), wide),
            pltpu.VMEM((rows, HEAD_DIM), wide),
        ],
        exps=pairs,
    )


def turn(rows, cosine, sine, sign):
    half_rot = ROTARY // 2
    lane = lax.broadcasted_iota(jnp.int32, cosine.shape, 1)
    front = rows[:, :128]
    ahead = pltpu.roll(front, 128 - half_rot, 1)
    behind = pltpu.roll(front, half_rot, 1)
    other = jnp.where(lane < half_rot, -ahead, behind)
    turned = front * cosine + other * (sine * sign)
    return jnp.concatenate([turned, rows[:, 128:]], axis=1)


def scores_of(keys, query, info, trunk_end, first_row, scale):
    scores = contract(keys, query, (1, 1)) * scale
    key_place = lax.broadcasted_iota(jnp.int32, scores.shape, 0)
    query_place = first_row + lax.broadcasted_iota(jnp.int32, scores.shape, 1)
    seen = (
        (key_place < trunk_end)
        | ((key_place >= info[0:1]) & (key_place < info[1:2]))
        | (key_place >= info[2:3])
    ) & (key_place <= query_place)
    return jnp.where(seen, scores, masked_score)


def tree_info(lengths, parent, rows):
    labels = jnp.arange(SEGS)
    ends = jnp.sum(jnp.where(labels[None, :] <= labels[:, None], lengths[None, :], 0), axis=1)
    starts = ends - lengths
    hot_parent = parent[:, None] == labels[None, :]
    parent_start = jnp.sum(jnp.where(hot_parent, starts[None, :], 0), axis=1)
    parent_end = jnp.sum(jnp.where(hot_parent, ends[None, :], 0), axis=1)
    places = jnp.arange(rows, dtype=jnp.int32)
    inside = (places[None, :] >= starts[:, None]) & (places[None, :] < ends[:, None])
    pick = lambda table: jnp.sum(jnp.where(inside, table[:, None], 0), axis=0)
    spans = [pick(parent_start), pick(parent_end), pick(starts)]
    return jnp.stack(spans + [places] * 5).astype(jnp.int32), ends[0]


def rotary_tables(depth):
    half_rot = ROTARY // 2
    lane = jnp.arange(128)
    frequency = jnp.power(10000.0, -2.0 * (lane % half_rot).astype(wide) / ROTARY)
    frequency = jnp.where(lane < ROTARY, frequency, 0.0)
    angles = depth.astype(wide)[:, None] * frequency[None, :]
    return jnp.cos(angles), jnp.sin(angles)


def on_device_split(
    residual,
    out_grad,
    path_depth,
    seg_lengths,
    parents,
    attn_norm_gain,
    attn_norm_bias,
    ffn_norm_gain,
    ffn_norm_bias,
    qkv_weight,
    qkv_bias,
    dense_weight,
    dense_bias,
    up_weight,
    up_bias,
    down_weight,
    down_bias,
):
    core = lax.axis_index("ctx")
    line = lax.axis_index("tp")
    plane = lax.axis_index("fsdp")
    rows, held_width = residual.shape
    width = 4 * held_width
    half = width // 2

    inward = jnp.concatenate([qkv_weight, up_weight], axis=1)
    split = qkv_weight.shape[1]
    other_depth = trade(path_depth, "ctx", 1)
    cosine, sine = rotary_tables(jnp.concatenate([path_depth, other_depth]))
    info, trunk_end = tree_info(seg_lengths[0], parents[0], 2 * rows)
    scalars = jnp.stack([core, trunk_end, line, plane]).astype(jnp.int32)
    qkv_shift = qkv_bias.astype(wide)[None, :]
    up_shift = up_bias.astype(wide)[None, :]
    inward_near, inward_far, inward, cosine, sine, info = meet(
        trade(inward, "fsdp", 1), trade(inward, "fsdp", 2), inward, cosine, sine, info
    )
    middle = inward.shape[0] // 2
    upper_corner = trade(inward_far[:middle], "fsdp", 1)
    lower_corner = trade(inward_near[middle:], "fsdp", 2)
    near, far = meet(
        trade(residual, "tp", 1), trade(residual, "tp", 2), inward_near, inward_far
    )[:2]
    corner = trade(far, "tp", 1)
    norm_rows = jnp.stack([attn_norm_gain, attn_norm_bias, ffn_norm_gain, ffn_norm_bias] * 4)
    first_rows = after(norm_rows, far)
    terms = [trade(first_rows, "tp", bit) for bit in (1, 2, 3)]
    upper_corner, lower_corner, corner, *terms = meet(upper_corner, lower_corner, corner, *terms)
    qkv_own, up_own = assemble(
        scalars, (inward, inward_near, inward_far), (upper_corner, lower_corner), split
    )
    terms = (norm_rows, *terms)
    pieces = (residual, near, far, corner)

    def both_cores(own, *gate):
        return own, trade(after(own, *gate), "ctx", 1)

    def offloaded(weight, dim):
        return lax.all_gather(after(weight, near), "fsdp", axis=dim, tiled=True)

    qkv = both_cores(qkv_own)
    up = both_cores(up_own)
    first_grad = after(out_grad, corner)
    grad_near = trade(first_grad, "tp", 1)
    grad_far = trade(first_grad, "tp", 2)

    attn_in, ffn_in, stats, terms = norm(scalars, pieces, terms)
    mine, theirs = heads(scalars, attn_in, qkv, qkv_shift, cosine, sine)
    theirs = trade(theirs, "ctx", 1)
    hidden, slope = expand(after(scalars, mine), ffn_in, up, up_shift)
    grad_corner = trade(after(grad_far, slope), "tp", 1)
    down = both_cores(offloaded(down_weight, 1), slope)
    packed, attended, twin_attended, log_total = attend(
        after(scalars, slope, grad_near, grad_far), mine, theirs, info
    )
    dense = both_cores(offloaded(dense_weight, 1), attended)
    other_attended = trade(twin_attended, "ctx", 1)
    chip_out = project(scalars, attended, other_attended, hidden, dense, down)
    shared_out = lax.psum_scatter(chip_out, "tp", scatter_dimension=1, tiled=True)

    grad_pieces = (out_grad, grad_near, grad_far, grad_corner)
    cotangent, pre_grad, head_grad, other_grad, up_bias_rows = hidden_back(
        after(scalars, chip_out), grad_pieces, slope, dense, down
    )
    other_grad = trade(other_grad, "ctx", 1)

    def outer(left, right):
        return contract(left, right, (0, 0))

    def add_low(own, arrived):
        return (own + arrived.astype(wide)).astype(low)

    def to_owner(total, dim):
        return lax.psum_scatter(total, "fsdp", scatter_dimension=dim, tiled=True)

    both_attended = join_cores(attended, other_attended, core, 1)
    down_other = outer(after(hidden, pre_grad), cotangent[:, half:]).astype(low)
    down_arrived = trade(down_other, "ctx", 1)
    dense_other = outer(after(both_attended, down_other), cotangent[:, half:]).astype(low)
    dense_arrived = trade(dense_other, "ctx", 1)
    joined_grad, twin_grad, qkv_bias_rows = attend_back(
        after(scalars, dense_other), packed, head_grad, other_grad, log_total, cosine, sine, info
    )
    other_joined = trade(twin_grad, "ctx", 1)
    down_total = add_low(
        outer(after(hidden, joined_grad), cotangent[:, :half]), down_arrived
    )
    dense_total = add_low(
        outer(after(both_attended, down_total), cotangent[:, :half]), dense_arrived
    )
    dense_grad = to_owner(dense_total, 1)
    mix_in = (joined_grad, other_joined, pre_grad, qkv, up, terms, stats, pieces)
    *leave, sums_a, sums_b, row_a = mix(
        after(scalars, dense_total), *mix_in, (3, 1), (low, low)
    )
    mixed_side, mixed_near = trade(leave[0], "tp", 1), trade(leave[1], "tp", 1)
    down_grad, down_hop = scatter_plane(down_total, "fsdp", 1)
    *stay_mixed, sums_c, sums_d, row_b = mix(
        after(scalars, leave[0], *down_hop), *mix_in, (2, 0), (wide, wide)
    )
    passed = (stay_mixed[0] + mixed_side.astype(wide)).astype(low)
    far_mixed = trade(passed, "tp", 2)
    both_joined = join_cores(joined_grad, other_joined, core, 1)
    up_other = outer(
        after(ffn_in, stay_mixed[0], passed, down_grad, shared_out)[:, half:], pre_grad
    ).astype(low)
    up_arrived = trade(up_other, "ctx", 1)

    shared_out = shared_out.astype(wide)
    shared_out = join_cores(shared_out[:, :tile], shared_out[:, tile:], core, 1)
    output = (
        residual.astype(wide) + shared_out + dense_bias.astype(wide) + down_bias.astype(wide)
    ).astype(low)

    row_sums = row_a + row_b
    row_total = jnp.stack([row_sums[:, 0], row_sums[:, 64]])
    fold = lambda x: jnp.sum(x.reshape(4, 8, 2, tile), axis=1)
    gather_sums = lambda own, other: jnp.stack([fold(own), fold(other)], axis=2).reshape(4, 2, 2 * tile)
    leaving, norm_sums = gather_sums(sums_a, sums_b), gather_sums(sums_c, sums_d)
    hop_side = trade(jnp.concatenate([leaving.reshape(-1), row_total.reshape(-1)]), "tp", 1)
    qkv_other = outer(after(attn_in, up_other, hop_side)[:, half:], both_joined).astype(low)
    qkv_arrived = trade(qkv_other, "ctx", 1)
    norm_sums = norm_sums + hop_side[: 8 * held_width].reshape(norm_sums.shape)
    row_total = row_total + hop_side[8 * held_width :].reshape(row_total.shape)
    hop_far = trade(jnp.concatenate([norm_sums[:, 0].reshape(-1), row_total.reshape(-1)]), "tp", 2)
    up_total = add_low(
        outer(after(ffn_in, qkv_other, hop_far)[:, :half], pre_grad), up_arrived
    )
    up_grad = to_owner(up_total, 0)
    norm_total = norm_sums[:, 1] + hop_far[: 4 * held_width].reshape(4, held_width)
    row_total = row_total + hop_far[4 * held_width :].reshape(row_total.shape)
    row_means = row_total / width
    norm_total = join_cores(norm_total[:, :tile], norm_total[:, tile:], core, 1)
    held_grad_sum = jnp.sum(out_grad.astype(wide), axis=0)
    columns = jnp.concatenate(
        [
            norm_total.reshape(-1),
            held_grad_sum,
            jnp.sum(up_bias_rows, axis=0),
            jnp.sum(qkv_bias_rows, axis=0),
        ]
    )
    columns = columns + trade(columns, "fsdp", 1)
    qkv_total = add_low(
        outer(after(attn_in, up_total, dense_grad)[:, :half], both_joined), qkv_arrived
    )
    columns = columns + trade(columns, "fsdp", 2)
    other_columns = trade(columns, "ctx", 1)
    cut = columns.shape[0] - qkv_bias.shape[0] // 2
    qkv_bias_grad = join_cores(columns[cut:], other_columns[cut:], core, 0)
    together = columns[:cut] + other_columns[:cut]
    norm_grads = together[:width].reshape(4, held_width)
    out_bias_grad = together[width : width + held_width]
    up_bias_grad = together[width + held_width :]

    qkv_grad, qkv_hop = scatter_plane(qkv_total, "fsdp", 0)

    far_mixed = after(far_mixed, mixed_near, other_columns, *qkv_hop)
    shared_mixed = stay_mixed[1] + mixed_near.astype(wide) + far_mixed.astype(wide)
    shared_mixed = join_cores(shared_mixed[:, :tile], shared_mixed[:, tile:], core, 1)
    mean = stats[:, 0:1]
    inverse = stats[:, 64:65]
    own_normed = (residual.astype(wide) - mean) * inverse
    back = inverse * (shared_mixed - row_means[0][:, None] - own_normed * row_means[1][:, None])
    input_grad = (out_grad.astype(wide) + back).astype(low)
    return (
        output,
        input_grad,
        norm_grads[0],
        norm_grads[1],
        norm_grads[2],
        norm_grads[3],
        qkv_grad.astype(wide),
        qkv_bias_grad,
        dense_grad.astype(wide),
        out_bias_grad,
        up_grad.astype(wide),
        up_bias_grad,
        down_grad.astype(wide),
        out_bias_grad,
    )


def splits_heads(mesh):
    return mesh.shape["tp"] == 4 and mesh.shape["fsdp"] == 4 and mesh.shape["ctx"] == 2


def solution(mesh):
    placed = (
        P(("fsdp", "ctx"), "tp"),
        P(("fsdp", "ctx"), "tp"),
        P(("fsdp", "ctx")),
        P("fsdp", None),
        P("fsdp", None),
        P("tp"),
        P("tp"),
        P("tp"),
        P("tp"),
        P(("fsdp", "ctx"), "tp"),
        P("tp"),
        P("tp", ("fsdp", "ctx")),
        P("tp"),
        P(("fsdp", "ctx"), "tp"),
        P("tp"),
        P("tp", ("fsdp", "ctx")),
        P("tp"),
    )
    return jax.shard_map(
        on_device_split if splits_heads(mesh) else on_device,
        mesh=mesh,
        in_specs=placed,
        out_specs=(
            P(("fsdp", "ctx"), "tp"),
            P(("fsdp", "ctx"), "tp"),
            P("tp"),
            P("tp"),
            P("tp"),
            P("tp"),
            P(("fsdp", "ctx"), "tp"),
            P("tp"),
            P("tp", ("fsdp", "ctx")),
            P("tp"),
            P(("fsdp", "ctx"), "tp"),
            P("tp"),
            P("tp", ("fsdp", "ctx")),
            P("tp"),
        ),
        check_vma=False,
    )
```

```python
from functools import partial
import math

import jax
import jax.numpy as jnp
from jax import lax
from jax.experimental import pallas as pl
from jax.experimental.pallas import tpu as pltpu
from jax.sharding import PartitionSpec as P

HEAD_DIM = 256
ROTARY = 64
SEGS = 13


norm_epsilon = 1e-05
masked_score = -1e30
block_limit = 512


def from_behind(x, axis, by):
    peers = lax.axis_size(axis)
    pairs = [(i, i + by) for i in range(peers) if 0 <= i + by < peers]
    return lax.ppermute(x, axis, pairs)


def rotary(vectors, places):
    half_rot = ROTARY // 2
    frequency = jnp.power(10000.0, -2.0 * jnp.arange(half_rot).astype(jnp.float32) / ROTARY)
    angles = places.astype(jnp.float32)[:, None] * frequency[None, :]
    cosine = jnp.cos(angles)[:, None, :]
    sine_part = jnp.sin(angles)[:, None, :]
    first_half = vectors[..., :half_rot]
    second_half = vectors[..., half_rot:ROTARY]
    return jnp.concatenate(
        [
            first_half * cosine - second_half * sine_part,
            second_half * cosine + first_half * sine_part,
            vectors[..., ROTARY:],
        ],
        axis=-1,
    )


def tree_tables(lengths, parent):
    starts = jnp.cumsum(lengths) - lengths
    labels = jnp.arange(SEGS)
    grand_parent = jnp.sum(
        jnp.where(parent[:, None] == labels[None, :], parent[None, :], 0), axis=1
    )
    ancestor = (
        (labels[None, :] == labels[:, None])
        | (labels[None, :] == parent[:, None])
        | (labels[None, :] == grand_parent[:, None])
    )
    return (starts, ancestor.astype(jnp.float32))


def segment_onehot(places, starts):
    membership = jnp.sum((places[:, None] >= starts[None, :]).astype(jnp.int32), axis=1) - 1
    return (membership[:, None] == jnp.arange(SEGS)[None, :]).astype(jnp.float32)


def visible(hot_query, place_query, hot_key, place_key, ancestor):
    reachable = jnp.dot(jnp.dot(hot_query, ancestor), hot_key.T)
    return (reachable > 0.5) & (place_key[None, :] <= place_query[:, None])


def on_device(
    residual,
    out_grad,
    path_depth,
    seg_lengths,
    parents,
    attn_norm_gain,
    attn_norm_bias,
    ffn_norm_gain,
    ffn_norm_bias,
    qkv_weight,
    qkv_bias,
    dense_weight,
    dense_bias,
    up_weight,
    up_bias,
    down_weight,
    down_bias,
):
    row_count = residual.shape[0]
    local_width = residual.shape[1]
    head_count = qkv_weight.shape[1] // (3 * HEAD_DIM)
    score_scale = 1.0 / math.sqrt(HEAD_DIM)
    ctx_index = lax.axis_index("ctx")
    tp_index = lax.axis_index("tp")
    norm_stack = jnp.stack([attn_norm_gain, attn_norm_bias, ffn_norm_gain, ffn_norm_bias])
    full_rows, norm_terms = (
        lax.all_gather(residual, "tp", axis=1, tiled=True),
        lax.all_gather(norm_stack, "tp", axis=1, tiled=True),
    )
    norm_terms = norm_terms.astype(jnp.float32)
    qkv_full, up_full = (
        lax.all_gather(qkv_weight, ("fsdp", "ctx"), axis=0, tiled=True),
        lax.all_gather(up_weight, ("fsdp", "ctx"), axis=0, tiled=True),
    )
    dense_full, down_full = (
        lax.all_gather(dense_weight, ("fsdp", "ctx"), axis=1, tiled=True),
        lax.all_gather(down_weight, ("fsdp", "ctx"), axis=1, tiled=True),
    )
    rows_wide = full_rows.astype(jnp.float32)
    centred = rows_wide - jnp.mean(rows_wide, axis=1, keepdims=True)
    inverse_scale = lax.rsqrt(jnp.mean(centred * centred, axis=1, keepdims=True) + norm_epsilon)
    normed = centred * inverse_scale
    attn_in = (normed * norm_terms[0] + norm_terms[1]).astype(jnp.bfloat16)
    ffn_in = (normed * norm_terms[2] + norm_terms[3]).astype(jnp.bfloat16)
    joined = (
        jnp.dot(attn_in, qkv_full, preferred_element_type=jnp.float32)
        + qkv_bias.astype(jnp.float32)
    ).reshape(row_count, head_count, 3, HEAD_DIM)
    queries_pre = joined[:, :, 0]
    query_rows = rotary(queries_pre, path_depth).astype(jnp.bfloat16)
    key_rows = rotary(joined[:, :, 1], path_depth).astype(jnp.bfloat16)
    value_rows = joined[:, :, 2].astype(jnp.bfloat16)
    far_keys, far_values = from_behind((key_rows, value_rows), "ctx", 1)
    starts, ancestor = tree_tables(seg_lengths[0], parents[0])
    places = ctx_index * row_count + jnp.arange(row_count, dtype=jnp.int32)
    key_places = jnp.concatenate([places - row_count, places])
    hot_query = segment_onehot(places, starts)
    hot_key = segment_onehot(key_places, starts)
    all_keys = jnp.concatenate([far_keys, key_rows], axis=0)
    all_values = jnp.concatenate([far_values, value_rows], axis=0)
    block_starts = list(range(0, row_count, block_limit))

    def block_scores(block_start, block_size, key_set):
        key_span = row_count + block_start + block_size
        query_block = query_rows[block_start : block_start + block_size]
        scores = (
            jnp.einsum(
                "nhe,lhe->hnl", query_block, key_set[:key_span], preferred_element_type=jnp.float32
            )
            * score_scale
        )
        reachable = visible(
            hot_query[block_start : block_start + block_size],
            places[block_start : block_start + block_size],
            hot_key[:key_span],
            key_places[:key_span],
            ancestor,
        )
        return jnp.where(reachable[None], scores, masked_score)

    out_blocks = []
    log_totals = []
    for block_start in block_starts:
        block_size = min(block_limit, row_count - block_start)
        key_span = row_count + block_start + block_size
        scores = block_scores(block_start, block_size, all_keys)
        row_top = jnp.max(scores, axis=-1, keepdims=True)
        exp_scores = jnp.exp(scores - row_top)
        exp_total = jnp.sum(exp_scores, axis=-1, keepdims=True)
        attn_probs = exp_scores / exp_total
        out_blocks.append(
            jnp.einsum(
                "hnl,lhe->nhe",
                attn_probs.astype(jnp.bfloat16),
                all_values[:key_span],
                preferred_element_type=jnp.float32,
            )
        )
        log_totals.append(row_top + jnp.log(exp_total))
    attended = (
        jnp.concatenate(out_blocks, axis=0)
        .reshape(row_count, head_count * HEAD_DIM)
        .astype(jnp.bfloat16)
    )
    hidden_pre = jnp.dot(ffn_in, up_full, preferred_element_type=jnp.float32) + up_bias.astype(
        jnp.float32
    )
    hidden_wide, gelu_back = jax.vjp(partial(jax.nn.gelu, approximate=False), hidden_pre)
    hidden = hidden_wide.astype(jnp.bfloat16)
    partial_out = jnp.dot(attended, dense_full, preferred_element_type=jnp.float32) + jnp.dot(
        hidden, down_full, preferred_element_type=jnp.float32
    )
    shared_out = lax.psum_scatter(partial_out, "tp", scatter_dimension=1, tiled=True)
    output = (
        residual.astype(jnp.float32)
        + shared_out
        + dense_bias.astype(jnp.float32)
        + down_bias.astype(jnp.float32)
    ).astype(jnp.bfloat16)
    cotangent = lax.all_gather(out_grad, "tp", axis=1, tiled=True)
    grad_out_bias = jnp.sum(out_grad.astype(jnp.float32), axis=0)
    grad_dense_w = jnp.einsum("rf,rd->fd", attended, cotangent, preferred_element_type=jnp.float32)
    grad_down_w = jnp.einsum("rf,rd->fd", hidden, cotangent, preferred_element_type=jnp.float32)
    grad_attended = jnp.einsum(
        "rd,fd->rf", cotangent, dense_full, preferred_element_type=jnp.float32
    ).astype(jnp.bfloat16)
    grad_hidden = jnp.einsum("rd,fd->rf", cotangent, down_full, preferred_element_type=jnp.float32)
    grad_pre = gelu_back(grad_hidden)[0].astype(jnp.bfloat16)
    grad_up_w = jnp.einsum("rd,rf->df", ffn_in, grad_pre, preferred_element_type=jnp.float32)
    grad_up_b = jnp.sum(grad_pre.astype(jnp.float32), axis=0)
    grad_ffn_in = jnp.einsum("rf,df->rd", grad_pre, up_full, preferred_element_type=jnp.float32)
    key_set = all_keys
    grad_att_heads = grad_attended.reshape(row_count, head_count, HEAD_DIM)
    grad_query_parts = []
    grad_key_all = jnp.zeros((2 * row_count, head_count, HEAD_DIM), jnp.float32)
    grad_value_all = jnp.zeros((2 * row_count, head_count, HEAD_DIM), jnp.float32)
    for block_number, block_start in enumerate(block_starts):
        block_size = min(block_limit, row_count - block_start)
        key_span = row_count + block_start + block_size
        scores = block_scores(block_start, block_size, key_set)
        attn_probs = jnp.exp(scores - log_totals[block_number])
        grad_block = grad_att_heads[block_start : block_start + block_size]
        grad_value_all = grad_value_all.at[:key_span].add(
            jnp.einsum(
                "hnl,nhe->lhe",
                attn_probs.astype(jnp.bfloat16),
                grad_block,
                preferred_element_type=jnp.float32,
            )
        )
        grad_dots = jnp.einsum(
            "nhe,lhe->hnl", grad_block, all_values[:key_span], preferred_element_type=jnp.float32
        )
        row_delta = jnp.sum(attn_probs * grad_dots, axis=-1, keepdims=True)
        grad_scores = (attn_probs * (grad_dots - row_delta)).astype(jnp.bfloat16)
        grad_query_parts.append(
            jnp.einsum(
                "hnl,lhe->nhe", grad_scores, key_set[:key_span], preferred_element_type=jnp.float32
            )
            * score_scale
        )
        grad_key_all = grad_key_all.at[:key_span].add(
            jnp.einsum(
                "hnl,nhe->lhe",
                grad_scores,
                query_rows[block_start : block_start + block_size],
                preferred_element_type=jnp.float32,
            )
            * score_scale
        )
    arriving_keys, arriving_values = from_behind(
        (grad_key_all[:row_count], grad_value_all[:row_count]), "ctx", -1
    )
    grad_keys = grad_key_all[row_count:] + arriving_keys
    grad_values = grad_value_all[row_count:] + arriving_values
    grad_queries = jnp.concatenate(grad_query_parts, axis=0)
    rotated_unused, rotary_back = jax.vjp(lambda vectors: rotary(vectors, path_depth), queries_pre)
    grad_joined = (
        jnp.stack([rotary_back(grad_queries)[0], rotary_back(grad_keys)[0], grad_values], axis=2)
        .astype(jnp.bfloat16)
        .reshape(row_count, head_count * 3 * HEAD_DIM)
    )
    grad_qkv_w = jnp.einsum("rd,rf->df", attn_in, grad_joined, preferred_element_type=jnp.float32)
    grad_qkv_b = jnp.sum(grad_joined.astype(jnp.float32), axis=0)
    grad_attn_in = jnp.einsum(
        "rf,df->rd", grad_joined, qkv_full, preferred_element_type=jnp.float32
    )
    total_attn, total_ffn = lax.psum((grad_attn_in, grad_ffn_in), "tp")

    def norm_back(total_grad, gain_row):
        scaled = total_grad * gain_row
        mean_plain = jnp.mean(scaled, axis=1, keepdims=True)
        mean_normed = jnp.mean(scaled * normed, axis=1, keepdims=True)
        back_rows = inverse_scale * (scaled - mean_plain - normed * mean_normed)
        gain_grad = jnp.sum(total_grad * normed, axis=0)
        shift_grad = jnp.sum(total_grad, axis=0)
        return (
            lax.dynamic_slice_in_dim(back_rows, tp_index * local_width, local_width, 1),
            lax.dynamic_slice_in_dim(gain_grad, tp_index * local_width, local_width, 0),
            lax.dynamic_slice_in_dim(shift_grad, tp_index * local_width, local_width, 0),
        )

    back_attn, attn_gain_grad, attn_shift_grad = norm_back(total_attn, norm_terms[0])
    back_ffn, ffn_gain_grad, ffn_shift_grad = norm_back(total_ffn, norm_terms[2])
    norm_grads = jnp.stack([attn_gain_grad, attn_shift_grad, ffn_gain_grad, ffn_shift_grad])
    back_total = back_attn + back_ffn
    input_grad = (out_grad.astype(jnp.float32) + back_total).astype(jnp.bfloat16)
    qkv_bias_grad, up_bias_grad, out_bias_grad, norm_totals = lax.psum(
        (grad_qkv_b, grad_up_b, grad_out_bias, norm_grads), ("fsdp", "ctx")
    )
    qkv_weight_grad, up_weight_grad = (
        lax.psum_scatter(
            grad_qkv_w.astype(jnp.bfloat16), ("fsdp", "ctx"), scatter_dimension=0, tiled=True
        ).astype(jnp.float32),
        lax.psum_scatter(
            grad_up_w.astype(jnp.bfloat16), ("fsdp", "ctx"), scatter_dimension=0, tiled=True
        ).astype(jnp.float32),
    )
    dense_weight_grad, down_weight_grad = (
        lax.psum_scatter(
            grad_dense_w.astype(jnp.bfloat16), ("fsdp", "ctx"), scatter_dimension=1, tiled=True
        ).astype(jnp.float32),
        lax.psum_scatter(
            grad_down_w.astype(jnp.bfloat16), ("fsdp", "ctx"), scatter_dimension=1, tiled=True
        ).astype(jnp.float32),
    )
    return (
        output,
        input_grad,
        norm_totals[0],
        norm_totals[1],
        norm_totals[2],
        norm_totals[3],
        qkv_weight_grad,
        qkv_bias_grad,
        dense_weight_grad,
        out_bias_grad,
        up_weight_grad,
        up_bias_grad,
        down_weight_grad,
        out_bias_grad,
    )


low = jnp.bfloat16
wide = jnp.float32
tile = 256
megabyte = 1024 * 1024
pace = {"attend_back": 1, "mix": 1}
room = {"project": 56, "mix": 56}


def trade(x, axis, bit):
    peers = lax.axis_size(axis)
    return lax.ppermute(x, axis, [(i, i ^ bit) for i in range(peers)])


def after(x, *earlier):
    return lax.optimization_barrier((x, *earlier))[0]


def meet(*values):
    return lax.optimization_barrier(values)


def block_of(x, index, dim, blocks):
    width = x.shape[dim] // blocks
    return lax.dynamic_slice_in_dim(x, index * width, width, dim)


def lay_out(pieces, place, dim):
    width = pieces[0].shape[dim]
    shape = list(pieces[0].shape)
    shape[dim] = width * 4
    whole = jnp.zeros(shape, pieces[0].dtype)
    for step, piece in enumerate(pieces):
        whole = lax.dynamic_update_slice_in_dim(whole, piece, (place ^ step) * width, dim)
    return whole


def plane_corner(near, far, axis):
    half = near.shape[0] // 2
    corner = [trade(far[:half], axis, 1), trade(near[half:], axis, 2)]
    return jnp.concatenate(corner, axis=0)


def scatter_plane(total, axis, dim, *gate):
    place = lax.axis_index(axis)
    own, near, far, corner = (block_of(total, place ^ k, dim, 4) for k in range(4))
    half = own.shape[0] // 2
    upper = trade(corner[:half].astype(low), axis, 1)
    lower = trade(corner[half:].astype(low), axis, 2)
    upper, lower = after(upper, *gate), after(lower, *gate)
    add = lambda a, b: (a.astype(wide) + b.astype(wide)).astype(low)
    far = jnp.concatenate([add(far[:half], upper), far[half:].astype(low)], axis=0)
    near = jnp.concatenate([near[:half].astype(low), add(near[half:], lower)], axis=0)
    return (own, trade(near, axis, 1), trade(far, axis, 2)), (far, near)


def close_plane(parts, *gate):
    own, near, far = (part.astype(wide) for part in after(parts, *gate))
    return (own + near + far).astype(low)


def half_of(x, index, dim):
    return block_of(x, index, dim, 2)


def join_cores(mine, theirs, core, dim):
    first = jnp.where(core == 0, mine, theirs)
    second = jnp.where(core == 0, theirs, mine)
    return jnp.concatenate([first, second], axis=dim)


def contract(a, b, dims):
    return lax.dot_general(a, b, ((dims[:1], dims[1:]), ((), ())), preferred_element_type=wide)


def place_of(index, size):
    return pl.ds(pl.multiple_of(index * size, size), size)


def fold_rows(x):
    return jnp.sum(x.reshape(x.shape[0] // 8, 8, x.shape[1]), axis=0)


def fixed(shape):
    return pl.BlockSpec(
        shape, lambda step, scalars: (0,) * len(shape), pipeline_mode=pl.Buffered(1)
    )


def kept(shape):
    return pl.BlockSpec(shape, lambda step, scalars: (0,) * len(shape))


def by_row(width):
    return pl.BlockSpec((tile, width), lambda step, scalars: (step, 0))


def by_column(rows, width, first=0):
    return pl.BlockSpec((rows, width), lambda step, scalars: (0, jnp.maximum(step - first, 0)))


def call(
    kernel, name, steps, in_specs, out_specs, out_shape, operands, flops, moved, scratch=(), exps=0
):
    return pl.pallas_call(
        kernel,
        grid_spec=pltpu.PrefetchScalarGridSpec(
            num_scalar_prefetch=1,
            grid=(steps,),
            in_specs=in_specs,
            out_specs=out_specs,
            scratch_shapes=list(scratch),
        ),
        out_shape=out_shape,
        compiler_params=pltpu.CompilerParams(vmem_limit_bytes=room.get(name, 28) * megabyte),
        cost_estimate=pl.CostEstimate(
            flops=int(flops * pace.get(name, 16)),
            bytes_accessed=int(moved * pace.get(name, 16)),
            transcendentals=int(exps * pace.get(name, 16)),
        ),
        name=name,
    )(*operands)


def shaped(*shape, kind=low):
    return jax.ShapeDtypeStruct(shape, kind)


def own_first(piece, core):
    return piece[:, place_of(core, tile)], piece[:, place_of(1 - core, tile)]


def norm_kernel(scalars, *refs):
    pieces, terms = refs[:4], refs[4:8]
    attn_out, ffn_out, stats_out, terms_out = refs[8:]
    width = 8 * tile
    lane = lax.broadcasted_iota(jnp.int32, (strip, 128), 1)
    for start in range(0, stats_out.shape[0], strip):
        here = slice(start, start + strip)
        parts = [piece[here, :].astype(wide) for piece in pieces]
        total = sum(jnp.sum(part, axis=1, keepdims=True) for part in parts)
        mean = total * (1.0 / width)
        spread = sum(
            jnp.sum((part - mean) * (part - mean), axis=1, keepdims=True) for part in parts
        )
        inverse = lax.rsqrt(spread * (1.0 / width) + norm_epsilon)
        for k in range(4):
            block = scalars[2] ^ k
            for half in range(2):
                side = scalars[0] if half == 0 else 1 - scalars[0]
                source = place_of(side, tile)
                columns = place_of(4 * half + block, tile)
                normed = (pieces[k][here, source].astype(wide) - mean) * inverse
                term = terms[k][:, source].astype(wide)
                attn_out[here, columns] = (normed * term[0:1] + term[1:2]).astype(low)
                ffn_out[here, columns] = (normed * term[2:3] + term[3:4]).astype(low)
        stats_out[here, :] = jnp.where(lane < 64, mean, inverse)

    @pl.when(pl.program_id(0) == 0)
    def _():
        for k in range(4):
            for half in range(2):
                side = scalars[0] if half == 0 else 1 - scalars[0]
                columns = place_of(4 * half + (scalars[2] ^ k), tile)
                terms_out[:, columns] = terms[k][0:8, place_of(side, tile)].astype(wide)


def norm(scalars, pieces, rows):
    width = pieces[0].shape[1]
    term = pl.BlockSpec((16, width), lambda step, scalars: (rows // 16, 0))
    return call(
        norm_kernel,
        "norm",
        rows // tile,
        [by_row(width)] * 4 + [term] * 4,
        [by_row(4 * width), by_row(4 * width), by_row(128), kept((8, 4 * width))],
        [
            shaped(rows, 4 * width),
            shaped(rows, 4 * width),
            shaped(rows, 128, kind=wide),
            shaped(8, 4 * width, kind=wide),
        ],
        (scalars, *pieces, *pieces),
        rows * width * 40,
        rows * width * 24,
    )


def assemble_kernel(scalars, own, near, far, upper, lower, first_out, second_out):
    step = pl.program_id(0)
    split = first_out.shape[1]
    middle = upper.shape[0]

    def write(piece, rows):
        first_out[rows, :] = piece[:, :split]
        second_out[rows, :] = piece[:, split:]

    for k, piece in enumerate((own, near, far)):
        pl.when(step == k)(partial(write, piece, slice(None)))

    @pl.when(step == 3)
    def _():
        write(upper, slice(0, middle))
        write(lower, slice(middle, 2 * middle))


def assemble(scalars, pieces, halves, split):
    rows, columns = pieces[0].shape
    place = lambda step, scalars: (scalars[3] ^ step, 0)
    return call(
        assemble_kernel,
        "assemble",
        4,
        [fixed((rows, columns))] * 3 + [fixed((rows // 2, columns))] * 2,
        [pl.BlockSpec((rows, split), place), pl.BlockSpec((rows, columns - split), place)],
        [shaped(4 * rows, split), shaped(4 * rows, columns - split)],
        (scalars, *pieces, *halves),
        rows * columns,
        rows * columns * 16,
    )


strip = 32


def strips(first, rows):
    return [(at, first + at, first + at + strip) for at in range(0, rows, strip)]


def double(rows_in, own, other):
    half = rows_in.shape[1] // 2
    return contract(rows_in[:, :half], own, (1, 0)) + contract(rows_in[:, half:], other, (1, 0))


def heads_kernel(scalars, rows_in, own, other, shift_row, cosine, sine, mine, theirs):
    def run(out):
        for first in range(0, rows_in.shape[0], tile):
            product = double(rows_in.at[first : first + tile, :], own[...], other[...])
            for at, start, stop in strips(first, tile):
                joined = product[at : at + strip] + shift_row[0:1, :]
                for part in range(3):
                    vectors = joined[:, part * HEAD_DIM : (part + 1) * HEAD_DIM]
                    if part < 2:
                        vectors = turn(vectors, cosine[start:stop, :], sine[start:stop, :], 1.0)
                    out[part, start:stop, :] = vectors.astype(low)

    pl.when(pl.program_id(0) == 0)(partial(run, theirs))
    pl.when(pl.program_id(0) == 1)(partial(run, mine))


def heads(scalars, attn_in, weights, shift_row, cosine, sine):
    rows, width = attn_in.shape
    columns = 3 * HEAD_DIM

    def column(step, scalars):
        return 0, jnp.where(step == 0, 1 - scalars[0], scalars[0])

    weight = pl.BlockSpec((width // 2, columns), column)
    return call(
        heads_kernel,
        "heads",
        2,
        [fixed(attn_in.shape), weight, weight, pl.BlockSpec((1, columns), column)]
        + [fixed((rows, 128))] * 2,
        [kept((3, rows, HEAD_DIM))] * 2,
        [shaped(3, rows, HEAD_DIM)] * 2,
        (scalars, attn_in, *weights, shift_row, cosine, sine),
        4 * rows * width * columns,
        2 * (rows * width + 2 * width * columns + 2 * rows * columns),
    )


def expand_kernel(scalars, rows_in, own, other, shift_row, hidden, slope):
    for first in range(0, rows_in.shape[0], tile):
        product = double(rows_in.at[first : first + tile, :], own[...], other[...])
        for at, start, stop in strips(first, tile):
            pre = product[at : at + strip] + shift_row[0:1, :]
            phi = 0.5 + 0.5 * lax.erf(pre * math.sqrt(0.5))
            density = jnp.exp(pre * pre * -0.5) * (1.0 / math.sqrt(2.0 * math.pi))
            hidden[start:stop, :] = (pre * phi).astype(low)
            slope[start:stop, :] = (phi + pre * density).astype(low)


def expand(scalars, ffn_in, weights, shift_row):
    rows, width = ffn_in.shape
    columns = weights[0].shape[1]
    return call(
        expand_kernel,
        "expand",
        columns // tile,
        [fixed(ffn_in.shape)] + [by_column(width // 2, tile)] * 2 + [by_column(1, tile)],
        [by_column(rows, tile)] * 2,
        [shaped(rows, columns), shaped(rows, columns)],
        (scalars, ffn_in, *weights, shift_row),
        2 * rows * width * columns,
        2 * (rows * width + width * columns + 2 * rows * columns),
        exps=2 * rows * columns,
    )


def project_kernel(scalars, mine, theirs, hidden, own, other, out):
    heads_rows = 2 * HEAD_DIM
    for half, weight in enumerate((own, other)):
        total = contract(hidden[...], weight[heads_rows:, :], (1, 0))
        total += contract(mine[...], weight[place_of(scalars[0], HEAD_DIM), :], (1, 0))
        total += contract(theirs[...], weight[place_of(1 - scalars[0], HEAD_DIM), :], (1, 0))
        out[:, half * tile : (half + 1) * tile] = total.astype(out.dtype)


def project(scalars, mine, theirs, hidden, outward):
    rows = hidden.shape[0]
    depth = outward.shape[0]
    return call(
        project_kernel,
        "project",
        4,
        [fixed(mine.shape), fixed(mine.shape), fixed(hidden.shape)]
        + [
            pl.BlockSpec((depth, tile), lambda step, scalars: (0, 2 * step + scalars[0])),
            pl.BlockSpec((depth, tile), lambda step, scalars: (0, 2 * step + 1 - scalars[0])),
        ],
        [by_column(rows, 2 * tile)],
        [shaped(rows, 8 * tile)],
        (scalars, mine, theirs, hidden, outward, outward),
        16 * rows * tile * depth,
        2 * (rows * 8 * tile + depth * 8 * tile + rows * depth),
    )[0]


def hidden_back_kernel(scalars, *refs):
    pieces, (slope, weight) = refs[:4], refs[4:6]
    cotangent, pre_grad, mine, theirs, bias_grad, natural, both = refs[6:]
    step = pl.program_id(0)
    width = pieces[0].shape[1]

    @pl.when(step == 0)
    def _():
        for k in range(4):
            block = scalars[2] ^ k
            natural[:, place_of(block, width)] = pieces[k][...]
            own, other = own_first(pieces[k], scalars[0])
            cotangent[:, place_of(block, tile)] = own
            cotangent[:, place_of(4 + block, tile)] = other

    rows = natural.shape[0]

    @pl.when(step == 0)
    def _():
        both[...] = contract(natural[...], weight[...], (1, 1)).astype(low)
        theirs[...] = both[:, place_of(1 - scalars[0], HEAD_DIM)]
        mine[...] = both[:, place_of(scalars[0], HEAD_DIM)]

    @pl.when(step >= 1)
    def _():
        total = jnp.zeros((8, weight.shape[0]), wide)
        for first in range(0, rows, tile):
            grad = contract(natural[first : first + tile, :], weight[...], (1, 1))
            for at, start, stop in strips(first, tile):
                scaled = grad[at : at + strip] * slope[start:stop, :].astype(wide)
                scaled = scaled.astype(low)
                pre_grad[start:stop, :] = scaled
                total += fold_rows(scaled.astype(wide))
        bias_grad[...] = total


def hidden_back(scalars, pieces, slope, outward):
    rows, width = pieces[0].shape
    depth = outward.shape[0]
    hidden = depth - 2 * HEAD_DIM

    weight = pl.BlockSpec((2 * tile, 4 * width), lambda step, scalars: (step, 0))
    return call(
        hidden_back_kernel,
        "hidden_back",
        depth // (2 * tile),
        [fixed((rows, width))] * 4 + [by_column(rows, 2 * tile, 1), weight],
        [
            kept((rows, 4 * width)),
            by_column(rows, 2 * tile, 1),
            kept((rows, HEAD_DIM)),
            kept((rows, HEAD_DIM)),
            by_column(8, 2 * tile, 1),
        ],
        [
            shaped(rows, 4 * width),
            shaped(rows, hidden),
            shaped(rows, HEAD_DIM),
            shaped(rows, HEAD_DIM),
            shaped(8, hidden, kind=wide),
        ],
        (scalars, *pieces, slope, outward),
        8 * rows * width * depth,
        rows * width * 16 + 8 * width * depth + rows * hidden * 4,
        scratch=[pltpu.VMEM((rows, 4 * width), low), pltpu.VMEM((rows, 2 * HEAD_DIM), low)],
    )


def mix_kernel(
    scalars, mine, theirs, pre_grad, qkv_own, qkv_other, up_own, up_other, terms_own, terms_other,
    stats, first_piece, second_piece, first_out, second_out, sums_own, sums_other, row_sums
):
    step = pl.program_id(0)
    rows = pre_grad.shape[0]
    lane = lax.broadcasted_iota(jnp.int32, (strip, 128), 1)

    def run(piece, out, fresh):
        for half, qkv, up, terms, sums in (
            (0, qkv_own, up_own, terms_own, sums_own),
            (1, qkv_other, up_other, terms_other, sums_other),
        ):
            side = scalars[0] if half == 0 else 1 - scalars[0]
            totals = [jnp.zeros((8, tile), wide)] * 4
            attn_gain, ffn_gain = terms[0:1, :], terms[2:3, :]
            for first in range(0, rows, tile):
                here = slice(first, first + tile)
                attn_part = contract(
                    mine[here, :], qkv[:, place_of(scalars[0], 3 * HEAD_DIM)], (1, 1)
                ) + contract(
                    theirs[here, :], qkv[:, place_of(1 - scalars[0], 3 * HEAD_DIM)], (1, 1)
                )
                ffn_part = contract(pre_grad[here, :], up[...], (1, 1))
                for at, start, stop in strips(first, tile):
                    attn, ffn = attn_part[at : at + strip], ffn_part[at : at + strip]
                    mean, inverse = stats[start:stop, 0:1], stats[start:stop, 64:65]
                    held = piece[start:stop, place_of(side, tile)].astype(wide)
                    normed = (held - mean) * inverse
                    mixed = attn * attn_gain + ffn * ffn_gain
                    weighed = mixed * normed
                    parts = (attn * normed, attn, ffn * normed, ffn)
                    totals = [total + fold_rows(part) for total, part in zip(totals, parts)]
                    out[start:stop, half * tile : (half + 1) * tile] = mixed.astype(out.dtype)
                    across = jnp.where(
                        lane < 64,
                        jnp.sum(mixed[:, :128] + mixed[:, 128:], axis=1, keepdims=True),
                        jnp.sum(weighed[:, :128] + weighed[:, 128:], axis=1, keepdims=True),
                    )
                    if fresh and half == 0:
                        row_sums[start:stop, :] = across
                    else:
                        row_sums[start:stop, :] += across
            for place, total in enumerate(totals):
                sums[8 * place : 8 * place + 8, :] = total

    pl.when(step == 0)(partial(run, first_piece, first_out, True))
    pl.when(step == 1)(partial(run, second_piece, second_out, False))


def mix(scalars, mine, theirs, pre_grad, qkv, up, terms, stats, pieces, order, kinds):
    rows = pre_grad.shape[0]
    width = pieces[0].shape[1]
    depth = qkv[0].shape[1] + up[0].shape[1]

    def block(step, scalars):
        return scalars[2] ^ jnp.where(step == 0, order[0], order[1])

    weight = lambda x: pl.BlockSpec((tile, x.shape[1]), lambda step, scalars: (block(step, scalars), 0))
    term = lambda first: pl.BlockSpec((8, tile), lambda step, scalars: (0, first + block(step, scalars)))
    sums = pl.BlockSpec((32, tile), lambda step, scalars: (0, step))
    return call(
        mix_kernel,
        "mix",
        2,
        [fixed(mine.shape), fixed(mine.shape), fixed(pre_grad.shape)]
        + [weight(x) for x in (*qkv, *up)]
        + [term(0), term(4), fixed((rows, 128))]
        + [fixed((rows, width))] * 2,
        [kept((rows, width))] * 2 + [sums, sums, kept((rows, 128))],
        [shaped(rows, width, kind=kind) for kind in kinds]
        + [shaped(32, 2 * tile, kind=wide)] * 2
        + [shaped(rows, 128, kind=wide)],
        (scalars, mine, theirs, pre_grad, *qkv, *up, terms, terms, stats, pieces[order[0]], pieces[order[1]]),
        4 * rows * width * depth,
        2 * (4 * rows * width + 2 * depth * width + rows * depth),
    )


def attend_kernel(scalars, mine, theirs, info, packed, own_out, twin_out, log_total, natural, scale):
    rows = natural.shape[0]
    blocks = rows // tile
    own = place_of(scalars[0], rows // 2)
    twin = place_of(1 - scalars[0], rows // 2)
    for part in range(3):
        packed[part, own, :] = mine[part]
        packed[part, twin, :] = theirs[part]
    for block in range(blocks):
        span = (block + 1) * tile
        query = packed[0, block * tile : span, :]
        about = info[:, block * tile : span]
        scores = scores_of(packed[1, :span, :], query, about, scalars[1], block * tile, scale)
        top = jnp.max(scores, axis=0, keepdims=True)
        powers = jnp.exp(scores - top)
        total = jnp.sum(powers, axis=0, keepdims=True)
        probs = (powers * (1.0 / total)).astype(low)
        natural[block * tile : span, :] = contract(probs, packed[2, :span, :], (0, 0)).astype(low)
        log_total[0:1, block * tile : span] = top + jnp.log(total)
    own_out[...] = natural[own, :]
    twin_out[...] = natural[twin, :]


def attend(scalars, mine, theirs, info):
    held = mine.shape[1]
    rows = 2 * held
    pairs = rows * (rows + tile) // 2
    return call(
        partial(attend_kernel, scale=1.0 / math.sqrt(HEAD_DIM)),
        "attend",
        1,
        [fixed(mine.shape), fixed(mine.shape), fixed((8, rows))],
        [kept((3, rows, HEAD_DIM)), kept((held, HEAD_DIM)), kept((held, HEAD_DIM)), kept((8, rows))],
        [
            shaped(3, rows, HEAD_DIM),
            shaped(held, HEAD_DIM),
            shaped(held, HEAD_DIM),
            shaped(8, rows, kind=wide),
        ],
        (scalars, mine, theirs, info),
        pairs * HEAD_DIM * 4,
        rows * HEAD_DIM * 16,
        scratch=[pltpu.VMEM((rows, HEAD_DIM), low)],
        exps=pairs,
    )


def attend_back_kernel(
    scalars, packed, own_grads, twin_grads, log_total, cosine, sine, info, own_out, twin_out,
    bias_grad, grads, natural, key_grad, value_grad, scale
):
    rows = grads.shape[0]
    blocks = rows // tile
    shift = scalars[0] * (blocks // 2)
    own = place_of(scalars[0], rows // 2)
    twin = place_of(1 - scalars[0], rows // 2)
    grads[own, :] = own_grads[...]
    grads[twin, :] = twin_grads[...]
    bias_total = jnp.zeros((8, 3 * HEAD_DIM), wide)
    for block in reversed(range(blocks)):
        span = (block + 1) * tile
        before = block * tile
        query = packed[0, before:span, :]
        about = info[:, before:span]
        there = place_of(lax.rem(block + shift, blocks), tile)
        grad = grads[before:span, :]
        scores = scores_of(packed[1, :span, :], query, about, scalars[1], before, scale)
        probs = jnp.exp(scores - log_total[0:1, before:span])
        value_part = contract(probs.astype(low), grad, (1, 0))
        dots = contract(packed[2, :span, :], grad, (1, 1))
        delta = jnp.sum(probs * dots, axis=0, keepdims=True)
        score_grad = (probs * (dots - delta)).astype(low)
        query_grad = contract(score_grad, packed[1, :span, :], (0, 0)) * scale
        key_part = contract(score_grad, query, (1, 0)) * scale
        if block == blocks - 1:
            key_grad[...] = key_part
            value_grad[...] = value_part
        else:
            key_grad[:span, :] += key_part
            value_grad[:span, :] += value_part
        parts = (
            turn(query_grad, cosine[there, :], sine[there, :], -1.0),
            turn(key_grad[before:span, :], cosine[there, :], sine[there, :], -1.0),
            value_grad[before:span, :],
        )
        together = jnp.concatenate(parts, axis=1).astype(low)
        natural[before:span, :] = together
        bias_total += fold_rows(together.astype(wide))
    bias_grad[...] = bias_total
    own_out[...] = natural[own, :]
    twin_out[...] = natural[twin, :]


def attend_back(scalars, packed, own_grads, twin_grads, log_total, cosine, sine, info):
    held = own_grads.shape[0]
    rows = 2 * held
    pairs = rows * (rows + tile) // 2
    return call(
        partial(attend_back_kernel, scale=1.0 / math.sqrt(HEAD_DIM)),
        "attend_back",
        1,
        [
            fixed((3, rows, HEAD_DIM)),
            fixed((held, HEAD_DIM)),
            fixed((held, HEAD_DIM)),
            fixed((8, rows)),
            fixed((rows, 128)),
            fixed((rows, 128)),
            fixed((8, rows)),
        ],
        [kept((held, 3 * HEAD_DIM)), kept((held, 3 * HEAD_DIM)), kept((8, 3 * HEAD_DIM))],
        [
            shaped(held, 3 * HEAD_DIM),
            shaped(held, 3 * HEAD_DIM),
            shaped(8, 3 * HEAD_DIM, kind=wide),
        ],
        (scalars, packed, own_grads, twin_grads, log_total, cosine, sine, info),
        pairs * HEAD_DIM * 10,
        rows * HEAD_DIM * 16,
        scratch=[
            pltpu.VMEM((rows, HEAD_DIM), low),
            pltpu.VMEM((rows, 3 * HEAD_DIM), low),
            pltpu.VMEM((rows, HEAD_DIM), wide),
            pltpu.VMEM((rows, HEAD_DIM), wide),
        ],
        exps=pairs,
    )


def turn(rows, cosine, sine, sign):
    half_rot = ROTARY // 2
    lane = lax.broadcasted_iota(jnp.int32, cosine.shape, 1)
    front = rows[:, :128]
    ahead = pltpu.roll(front, 128 - half_rot, 1)
    behind = pltpu.roll(front, half_rot, 1)
    other = jnp.where(lane < half_rot, -ahead, behind)
    turned = front * cosine + other * (sine * sign)
    return jnp.concatenate([turned, rows[:, 128:]], axis=1)


def scores_of(keys, query, info, trunk_end, first_row, scale):
    scores = contract(keys, query, (1, 1)) * scale
    key_place = lax.broadcasted_iota(jnp.int32, scores.shape, 0)
    query_place = first_row + lax.broadcasted_iota(jnp.int32, scores.shape, 1)
    seen = (
        (key_place < trunk_end)
        | ((key_place >= info[0:1]) & (key_place < info[1:2]))
        | (key_place >= info[2:3])
    ) & (key_place <= query_place)
    return jnp.where(seen, scores, masked_score)


def tree_info(lengths, parent, rows):
    labels = jnp.arange(SEGS)
    ends = jnp.sum(jnp.where(labels[None, :] <= labels[:, None], lengths[None, :], 0), axis=1)
    starts = ends - lengths
    hot_parent = parent[:, None] == labels[None, :]
    parent_start = jnp.sum(jnp.where(hot_parent, starts[None, :], 0), axis=1)
    parent_end = jnp.sum(jnp.where(hot_parent, ends[None, :], 0), axis=1)
    places = jnp.arange(rows, dtype=jnp.int32)
    inside = (places[None, :] >= starts[:, None]) & (places[None, :] < ends[:, None])
    pick = lambda table: jnp.sum(jnp.where(inside, table[:, None], 0), axis=0)
    spans = [pick(parent_start), pick(parent_end), pick(starts)]
    return jnp.stack(spans + [places] * 5).astype(jnp.int32), ends[0]


def rotary_tables(depth):
    half_rot = ROTARY // 2
    lane = jnp.arange(128)
    frequency = jnp.power(10000.0, -2.0 * (lane % half_rot).astype(wide) / ROTARY)
    frequency = jnp.where(lane < ROTARY, frequency, 0.0)
    angles = depth.astype(wide)[:, None] * frequency[None, :]
    return jnp.cos(angles), jnp.sin(angles)


def on_device_split(
    residual,
    out_grad,
    path_depth,
    seg_lengths,
    parents,
    attn_norm_gain,
    attn_norm_bias,
    ffn_norm_gain,
    ffn_norm_bias,
    qkv_weight,
    qkv_bias,
    dense_weight,
    dense_bias,
    up_weight,
    up_bias,
    down_weight,
    down_bias,
):
    core = lax.axis_index("ctx")
    line = lax.axis_index("tp")
    plane = lax.axis_index("fsdp")
    rows, held_width = residual.shape
    width = 4 * held_width
    half = width // 2

    norm_rows = jnp.stack([attn_norm_gain, attn_norm_bias, ffn_norm_gain, ffn_norm_bias] * 4)
    held = jnp.concatenate([residual, norm_rows], axis=0)
    inward = jnp.concatenate([qkv_weight, up_weight], axis=1)
    split = qkv_weight.shape[1]
    other_depth = trade(path_depth, "ctx", 1)
    cosine, sine = rotary_tables(jnp.concatenate([path_depth, other_depth]))
    info, trunk_end = tree_info(seg_lengths[0], parents[0], 2 * rows)
    scalars = jnp.stack([core, trunk_end, line, plane]).astype(jnp.int32)
    qkv_shift = qkv_bias.astype(wide)[None, :]
    up_shift = up_bias.astype(wide)[None, :]
    near, far, cosine, sine, info = meet(
        trade(held, "tp", 1), trade(held, "tp", 2), cosine, sine, info
    )
    inward_near, inward_far, inward = meet(
        trade(inward, "fsdp", 1), trade(inward, "fsdp", 2), inward, near
    )[:3]
    middle = inward.shape[0] // 2
    upper_corner = trade(inward_far[:middle], "fsdp", 1)
    lower_corner = trade(inward_near[middle:], "fsdp", 2)
    corner = trade(far, "tp", 1)
    upper_corner, lower_corner, corner = meet(upper_corner, lower_corner, corner)
    qkv_own, up_own = assemble(
        scalars, (inward, inward_near, inward_far), (upper_corner, lower_corner), split
    )
    pieces = (held, near, far, corner)

    def both_cores(own, *gate):
        return own, trade(after(own, *gate), "ctx", 1)

    outward = jnp.concatenate([dense_weight, down_weight], axis=0)
    outward = lax.all_gather(after(outward, upper_corner), ("fsdp", "ctx"), axis=1, tiled=True)

    qkv = both_cores(qkv_own)
    up = both_cores(up_own)
    first_grad = after(out_grad, corner)
    grad_near = trade(first_grad, "tp", 1)
    grad_far = trade(first_grad, "tp", 2)

    attn_in, ffn_in, stats, terms = norm(scalars, pieces, rows)
    mine, theirs = heads(scalars, attn_in, qkv, qkv_shift, cosine, sine)
    theirs = trade(theirs, "ctx", 1)
    hidden, slope = expand(after(scalars, mine), ffn_in, up, up_shift)
    grad_corner = trade(after(grad_far, slope), "tp", 1)
    packed, attended, twin_attended, log_total = attend(
        after(scalars, slope, grad_near, grad_far), mine, theirs, info
    )
    other_attended = trade(twin_attended, "ctx", 1)
    chip_out = project(scalars, attended, other_attended, hidden, outward)
    shared_out = lax.psum_scatter(chip_out, "tp", scatter_dimension=1, tiled=True)

    grad_pieces = (out_grad, grad_near, grad_far, grad_corner)
    cotangent, pre_grad, head_grad, other_grad, up_bias_rows = hidden_back(
        after(scalars, chip_out), grad_pieces, slope, outward
    )
    other_grad = trade(other_grad, "ctx", 1)

    def outer(left, right):
        return contract(left, right, (0, 0))

    def add_low(own, arrived):
        return (own + arrived.astype(wide)).astype(low)

    def to_owner(total, dim):
        return lax.psum_scatter(total, "fsdp", scatter_dimension=dim, tiled=True)

    both_attended = join_cores(attended, other_attended, core, 1)
    down_other = outer(after(hidden, pre_grad), cotangent[:, half:]).astype(low)
    down_arrived = trade(down_other, "ctx", 1)
    up_other = outer(after(ffn_in, down_other)[:, half:], pre_grad).astype(low)
    up_arrived = trade(up_other, "ctx", 1)
    down_total = add_low(outer(after(hidden, up_other), cotangent[:, :half]), down_arrived)
    joined_grad, twin_grad, qkv_bias_rows = attend_back(
        after(scalars, down_total), packed, head_grad, other_grad, log_total, cosine, sine, info
    )
    other_joined = trade(twin_grad, "ctx", 1)
    down_parts, down_hop = scatter_plane(down_total, "fsdp", 1, joined_grad)
    dense_other = outer(after(both_attended, joined_grad, *down_hop), cotangent[:, half:]).astype(low)
    dense_arrived = trade(dense_other, "ctx", 1)
    up_total = add_low(outer(after(ffn_in, dense_other)[:, :half], pre_grad), up_arrived)
    up_grad = to_owner(up_total, 0)
    dense_total = add_low(
        outer(after(both_attended, up_total, other_joined), cotangent[:, :half]), dense_arrived
    )
    dense_grad = to_owner(dense_total, 1)
    mix_in = (joined_grad, other_joined, pre_grad, qkv, up, terms, stats, pieces)
    *leave, sums_a, sums_b, row_a = mix(
        after(scalars, dense_total), *mix_in, (3, 1), (low, low)
    )
    mixed_side = trade(leave[0], "tp", 1)
    *stay_mixed, sums_c, sums_d, row_b = mix(
        after(scalars, leave[0], shared_out), *mix_in, (2, 0), (wide, wide)
    )
    passed = (stay_mixed[0] + mixed_side.astype(wide)).astype(low)
    both_joined = join_cores(joined_grad, other_joined, core, 1)
    shared_out = shared_out.astype(wide)
    shared_out = join_cores(shared_out[:, :tile], shared_out[:, tile:], core, 1)
    output = (
        residual.astype(wide) + shared_out + dense_bias.astype(wide) + down_bias.astype(wide)
    ).astype(low)

    row_sums = row_a + row_b
    row_total = jnp.stack([row_sums[:, 0], row_sums[:, 64]])
    fold = lambda x: jnp.sum(x.reshape(4, 8, 2, tile), axis=1)
    gather_sums = lambda own, other: jnp.stack([fold(own), fold(other)], axis=2).reshape(4, 2, 2 * tile)
    leaving, norm_sums = gather_sums(sums_a, sums_b), gather_sums(sums_c, sums_d)
    hop_side = trade(jnp.concatenate([leaving.reshape(-1), row_total.reshape(-1)]), "tp", 1)
    norm_sums = norm_sums + hop_side[: 8 * held_width].reshape(norm_sums.shape)
    row_total = row_total + hop_side[8 * held_width :].reshape(row_total.shape)
    hop_far = trade(jnp.concatenate([norm_sums[:, 0].reshape(-1), row_total.reshape(-1)]), "tp", 2)
    qkv_other = outer(
        after(attn_in, stay_mixed[0], passed, hop_side, down_parts)[:, half:], both_joined
    ).astype(low)
    qkv_arrived = trade(qkv_other, "ctx", 1)
    far_mixed = trade(after(passed, hop_far), "tp", 2)
    mixed_near = trade(after(leave[1], hop_far), "tp", 1)
    norm_total = norm_sums[:, 1] + hop_far[: 4 * held_width].reshape(4, held_width)
    row_total = row_total + hop_far[4 * held_width :].reshape(row_total.shape)
    row_means = row_total / width
    norm_total = join_cores(norm_total[:, :tile], norm_total[:, tile:], core, 1)
    held_grad_sum = jnp.sum(out_grad.astype(wide), axis=0)
    columns = jnp.concatenate(
        [
            norm_total.reshape(-1),
            held_grad_sum,
            jnp.sum(up_bias_rows, axis=0),
            jnp.sum(qkv_bias_rows, axis=0),
        ]
    )
    columns = columns + trade(columns, "fsdp", 1)
    down_grad = close_plane(down_parts, qkv_other)
    qkv_total = add_low(
        outer(after(attn_in, qkv_other, down_grad, hop_far)[:, :half], both_joined), qkv_arrived
    )
    columns = columns + trade(columns, "fsdp", 2)
    qkv_parts, qkv_hop = scatter_plane(qkv_total, "fsdp", 0)
    qkv_grad = close_plane(qkv_parts)
    dense_grad = after(dense_grad, *qkv_hop)
    other_columns = trade(columns, "ctx", 1)
    cut = columns.shape[0] - qkv_bias.shape[0] // 2
    qkv_bias_grad = join_cores(columns[cut:], other_columns[cut:], core, 0)
    together = columns[:cut] + other_columns[:cut]
    norm_grads = together[:width].reshape(4, held_width)
    out_bias_grad = together[width : width + held_width]
    up_bias_grad = together[width + held_width :]


    far_mixed = after(far_mixed, mixed_near, other_columns, *qkv_hop)
    shared_mixed = stay_mixed[1] + mixed_near.astype(wide) + far_mixed.astype(wide)
    shared_mixed = join_cores(shared_mixed[:, :tile], shared_mixed[:, tile:], core, 1)
    mean = stats[:, 0:1]
    inverse = stats[:, 64:65]
    own_normed = (residual.astype(wide) - mean) * inverse
    back = inverse * (shared_mixed - row_means[0][:, None] - own_normed * row_means[1][:, None])
    input_grad = (out_grad.astype(wide) + back).astype(low)
    return (
        output,
        input_grad,
        norm_grads[0],
        norm_grads[1],
        norm_grads[2],
        norm_grads[3],
        qkv_grad.astype(wide),
        qkv_bias_grad,
        dense_grad.astype(wide),
        out_bias_grad,
        up_grad.astype(wide),
        up_bias_grad,
        down_grad.astype(wide),
        out_bias_grad,
    )


def splits_heads(mesh):
    return mesh.shape["tp"] == 4 and mesh.shape["fsdp"] == 4 and mesh.shape["ctx"] == 2


def solution(mesh):
    placed = (
        P(("fsdp", "ctx"), "tp"),
        P(("fsdp", "ctx"), "tp"),
        P(("fsdp", "ctx")),
        P("fsdp", None),
        P("fsdp", None),
        P("tp"),
        P("tp"),
        P("tp"),
        P("tp"),
        P(("fsdp", "ctx"), "tp"),
        P("tp"),
        P("tp", ("fsdp", "ctx")),
        P("tp"),
        P(("fsdp", "ctx"), "tp"),
        P("tp"),
        P("tp", ("fsdp", "ctx")),
        P("tp"),
    )
    return jax.shard_map(
        on_device_split if splits_heads(mesh) else on_device,
        mesh=mesh,
        in_specs=placed,
        out_specs=(
            P(("fsdp", "ctx"), "tp"),
            P(("fsdp", "ctx"), "tp"),
            P("tp"),
            P("tp"),
            P("tp"),
            P("tp"),
            P(("fsdp", "ctx"), "tp"),
            P("tp"),
            P("tp", ("fsdp", "ctx")),
            P("tp"),
            P(("fsdp", "ctx"), "tp"),
            P("tp"),
            P("tp", ("fsdp", "ctx")),
            P("tp"),
        ),
        check_vma=False,
    )
```

```python
from functools import partial
import math

import jax
import jax.numpy as jnp
from jax import lax
from jax.experimental import pallas as pl
from jax.experimental.pallas import tpu as pltpu
from jax.sharding import PartitionSpec as P

HEAD_DIM = 256
ROTARY = 64
SEGS = 13


norm_epsilon = 1e-05
masked_score = -1e30
block_limit = 512


def from_behind(x, axis, by):
    peers = lax.axis_size(axis)
    pairs = [(i, i + by) for i in range(peers) if 0 <= i + by < peers]
    return lax.ppermute(x, axis, pairs)


def rotary(vectors, places):
    half_rot = ROTARY // 2
    frequency = jnp.power(10000.0, -2.0 * jnp.arange(half_rot).astype(jnp.float32) / ROTARY)
    angles = places.astype(jnp.float32)[:, None] * frequency[None, :]
    cosine = jnp.cos(angles)[:, None, :]
    sine_part = jnp.sin(angles)[:, None, :]
    first_half = vectors[..., :half_rot]
    second_half = vectors[..., half_rot:ROTARY]
    return jnp.concatenate(
        [
            first_half * cosine - second_half * sine_part,
            second_half * cosine + first_half * sine_part,
            vectors[..., ROTARY:],
        ],
        axis=-1,
    )


def tree_tables(lengths, parent):
    starts = jnp.cumsum(lengths) - lengths
    labels = jnp.arange(SEGS)
    grand_parent = jnp.sum(
        jnp.where(parent[:, None] == labels[None, :], parent[None, :], 0), axis=1
    )
    ancestor = (
        (labels[None, :] == labels[:, None])
        | (labels[None, :] == parent[:, None])
        | (labels[None, :] == grand_parent[:, None])
    )
    return (starts, ancestor.astype(jnp.float32))


def segment_onehot(places, starts):
    membership = jnp.sum((places[:, None] >= starts[None, :]).astype(jnp.int32), axis=1) - 1
    return (membership[:, None] == jnp.arange(SEGS)[None, :]).astype(jnp.float32)


def visible(hot_query, place_query, hot_key, place_key, ancestor):
    reachable = jnp.dot(jnp.dot(hot_query, ancestor), hot_key.T)
    return (reachable > 0.5) & (place_key[None, :] <= place_query[:, None])


def on_device(
    residual,
    out_grad,
    path_depth,
    seg_lengths,
    parents,
    attn_norm_gain,
    attn_norm_bias,
    ffn_norm_gain,
    ffn_norm_bias,
    qkv_weight,
    qkv_bias,
    dense_weight,
    dense_bias,
    up_weight,
    up_bias,
    down_weight,
    down_bias,
):
    row_count = residual.shape[0]
    local_width = residual.shape[1]
    head_count = qkv_weight.shape[1] // (3 * HEAD_DIM)
    score_scale = 1.0 / math.sqrt(HEAD_DIM)
    ctx_index = lax.axis_index("ctx")
    tp_index = lax.axis_index("tp")
    norm_stack = jnp.stack([attn_norm_gain, attn_norm_bias, ffn_norm_gain, ffn_norm_bias])
    full_rows, norm_terms = (
        lax.all_gather(residual, "tp", axis=1, tiled=True),
        lax.all_gather(norm_stack, "tp", axis=1, tiled=True),
    )
    norm_terms = norm_terms.astype(jnp.float32)
    qkv_full, up_full = (
        lax.all_gather(qkv_weight, ("fsdp", "ctx"), axis=0, tiled=True),
        lax.all_gather(up_weight, ("fsdp", "ctx"), axis=0, tiled=True),
    )
    dense_full, down_full = (
        lax.all_gather(dense_weight, ("fsdp", "ctx"), axis=1, tiled=True),
        lax.all_gather(down_weight, ("fsdp", "ctx"), axis=1, tiled=True),
    )
    rows_wide = full_rows.astype(jnp.float32)
    centred = rows_wide - jnp.mean(rows_wide, axis=1, keepdims=True)
    inverse_scale = lax.rsqrt(jnp.mean(centred * centred, axis=1, keepdims=True) + norm_epsilon)
    normed = centred * inverse_scale
    attn_in = (normed * norm_terms[0] + norm_terms[1]).astype(jnp.bfloat16)
    ffn_in = (normed * norm_terms[2] + norm_terms[3]).astype(jnp.bfloat16)
    joined = (
        jnp.dot(attn_in, qkv_full, preferred_element_type=jnp.float32)
        + qkv_bias.astype(jnp.float32)
    ).reshape(row_count, head_count, 3, HEAD_DIM)
    queries_pre = joined[:, :, 0]
    query_rows = rotary(queries_pre, path_depth).astype(jnp.bfloat16)
    key_rows = rotary(joined[:, :, 1], path_depth).astype(jnp.bfloat16)
    value_rows = joined[:, :, 2].astype(jnp.bfloat16)
    far_keys, far_values = from_behind((key_rows, value_rows), "ctx", 1)
    starts, ancestor = tree_tables(seg_lengths[0], parents[0])
    places = ctx_index * row_count + jnp.arange(row_count, dtype=jnp.int32)
    key_places = jnp.concatenate([places - row_count, places])
    hot_query = segment_onehot(places, starts)
    hot_key = segment_onehot(key_places, starts)
    all_keys = jnp.concatenate([far_keys, key_rows], axis=0)
    all_values = jnp.concatenate([far_values, value_rows], axis=0)
    block_starts = list(range(0, row_count, block_limit))

    def block_scores(block_start, block_size, key_set):
        key_span = row_count + block_start + block_size
        query_block = query_rows[block_start : block_start + block_size]
        scores = (
            jnp.einsum(
                "nhe,lhe->hnl", query_block, key_set[:key_span], preferred_element_type=jnp.float32
            )
            * score_scale
        )
        reachable = visible(
            hot_query[block_start : block_start + block_size],
            places[block_start : block_start + block_size],
            hot_key[:key_span],
            key_places[:key_span],
            ancestor,
        )
        return jnp.where(reachable[None], scores, masked_score)

    out_blocks = []
    log_totals = []
    for block_start in block_starts:
        block_size = min(block_limit, row_count - block_start)
        key_span = row_count + block_start + block_size
        scores = block_scores(block_start, block_size, all_keys)
        row_top = jnp.max(scores, axis=-1, keepdims=True)
        exp_scores = jnp.exp(scores - row_top)
        exp_total = jnp.sum(exp_scores, axis=-1, keepdims=True)
        attn_probs = exp_scores / exp_total
        out_blocks.append(
            jnp.einsum(
                "hnl,lhe->nhe",
                attn_probs.astype(jnp.bfloat16),
                all_values[:key_span],
                preferred_element_type=jnp.float32,
            )
        )
        log_totals.append(row_top + jnp.log(exp_total))
    attended = (
        jnp.concatenate(out_blocks, axis=0)
        .reshape(row_count, head_count * HEAD_DIM)
        .astype(jnp.bfloat16)
    )
    hidden_pre = jnp.dot(ffn_in, up_full, preferred_element_type=jnp.float32) + up_bias.astype(
        jnp.float32
    )
    hidden_wide, gelu_back = jax.vjp(partial(jax.nn.gelu, approximate=False), hidden_pre)
    hidden = hidden_wide.astype(jnp.bfloat16)
    partial_out = jnp.dot(attended, dense_full, preferred_element_type=jnp.float32) + jnp.dot(
        hidden, down_full, preferred_element_type=jnp.float32
    )
    shared_out = lax.psum_scatter(partial_out, "tp", scatter_dimension=1, tiled=True)
    output = (
        residual.astype(jnp.float32)
        + shared_out
        + dense_bias.astype(jnp.float32)
        + down_bias.astype(jnp.float32)
    ).astype(jnp.bfloat16)
    cotangent = lax.all_gather(out_grad, "tp", axis=1, tiled=True)
    grad_out_bias = jnp.sum(out_grad.astype(jnp.float32), axis=0)
    grad_dense_w = jnp.einsum("rf,rd->fd", attended, cotangent, preferred_element_type=jnp.float32)
    grad_down_w = jnp.einsum("rf,rd->fd", hidden, cotangent, preferred_element_type=jnp.float32)
    grad_attended = jnp.einsum(
        "rd,fd->rf", cotangent, dense_full, preferred_element_type=jnp.float32
    ).astype(jnp.bfloat16)
    grad_hidden = jnp.einsum("rd,fd->rf", cotangent, down_full, preferred_element_type=jnp.float32)
    grad_pre = gelu_back(grad_hidden)[0].astype(jnp.bfloat16)
    grad_up_w = jnp.einsum("rd,rf->df", ffn_in, grad_pre, preferred_element_type=jnp.float32)
    grad_up_b = jnp.sum(grad_pre.astype(jnp.float32), axis=0)
    grad_ffn_in = jnp.einsum("rf,df->rd", grad_pre, up_full, preferred_element_type=jnp.float32)
    key_set = all_keys
    grad_att_heads = grad_attended.reshape(row_count, head_count, HEAD_DIM)
    grad_query_parts = []
    grad_key_all = jnp.zeros((2 * row_count, head_count, HEAD_DIM), jnp.float32)
    grad_value_all = jnp.zeros((2 * row_count, head_count, HEAD_DIM), jnp.float32)
    for block_number, block_start in enumerate(block_starts):
        block_size = min(block_limit, row_count - block_start)
        key_span = row_count + block_start + block_size
        scores = block_scores(block_start, block_size, key_set)
        attn_probs = jnp.exp(scores - log_totals[block_number])
        grad_block = grad_att_heads[block_start : block_start + block_size]
        grad_value_all = grad_value_all.at[:key_span].add(
            jnp.einsum(
                "hnl,nhe->lhe",
                attn_probs.astype(jnp.bfloat16),
                grad_block,
                preferred_element_type=jnp.float32,
            )
        )
        grad_dots = jnp.einsum(
            "nhe,lhe->hnl", grad_block, all_values[:key_span], preferred_element_type=jnp.float32
        )
        row_delta = jnp.sum(attn_probs * grad_dots, axis=-1, keepdims=True)
        grad_scores = (attn_probs * (grad_dots - row_delta)).astype(jnp.bfloat16)
        grad_query_parts.append(
            jnp.einsum(
                "hnl,lhe->nhe", grad_scores, key_set[:key_span], preferred_element_type=jnp.float32
            )
            * score_scale
        )
        grad_key_all = grad_key_all.at[:key_span].add(
            jnp.einsum(
                "hnl,nhe->lhe",
                grad_scores,
                query_rows[block_start : block_start + block_size],
                preferred_element_type=jnp.float32,
            )
            * score_scale
        )
    arriving_keys, arriving_values = from_behind(
        (grad_key_all[:row_count], grad_value_all[:row_count]), "ctx", -1
    )
    grad_keys = grad_key_all[row_count:] + arriving_keys
    grad_values = grad_value_all[row_count:] + arriving_values
    grad_queries = jnp.concatenate(grad_query_parts, axis=0)
    rotated_unused, rotary_back = jax.vjp(lambda vectors: rotary(vectors, path_depth), queries_pre)
    grad_joined = (
        jnp.stack([rotary_back(grad_queries)[0], rotary_back(grad_keys)[0], grad_values], axis=2)
        .astype(jnp.bfloat16)
        .reshape(row_count, head_count * 3 * HEAD_DIM)
    )
    grad_qkv_w = jnp.einsum("rd,rf->df", attn_in, grad_joined, preferred_element_type=jnp.float32)
    grad_qkv_b = jnp.sum(grad_joined.astype(jnp.float32), axis=0)
    grad_attn_in = jnp.einsum(
        "rf,df->rd", grad_joined, qkv_full, preferred_element_type=jnp.float32
    )
    total_attn, total_ffn = lax.psum((grad_attn_in, grad_ffn_in), "tp")

    def norm_back(total_grad, gain_row):
        scaled = total_grad * gain_row
        mean_plain = jnp.mean(scaled, axis=1, keepdims=True)
        mean_normed = jnp.mean(scaled * normed, axis=1, keepdims=True)
        back_rows = inverse_scale * (scaled - mean_plain - normed * mean_normed)
        gain_grad = jnp.sum(total_grad * normed, axis=0)
        shift_grad = jnp.sum(total_grad, axis=0)
        return (
            lax.dynamic_slice_in_dim(back_rows, tp_index * local_width, local_width, 1),
            lax.dynamic_slice_in_dim(gain_grad, tp_index * local_width, local_width, 0),
            lax.dynamic_slice_in_dim(shift_grad, tp_index * local_width, local_width, 0),
        )

    back_attn, attn_gain_grad, attn_shift_grad = norm_back(total_attn, norm_terms[0])
    back_ffn, ffn_gain_grad, ffn_shift_grad = norm_back(total_ffn, norm_terms[2])
    norm_grads = jnp.stack([attn_gain_grad, attn_shift_grad, ffn_gain_grad, ffn_shift_grad])
    back_total = back_attn + back_ffn
    input_grad = (out_grad.astype(jnp.float32) + back_total).astype(jnp.bfloat16)
    qkv_bias_grad, up_bias_grad, out_bias_grad, norm_totals = lax.psum(
        (grad_qkv_b, grad_up_b, grad_out_bias, norm_grads), ("fsdp", "ctx")
    )
    qkv_weight_grad, up_weight_grad = (
        lax.psum_scatter(
            grad_qkv_w.astype(jnp.bfloat16), ("fsdp", "ctx"), scatter_dimension=0, tiled=True
        ).astype(jnp.float32),
        lax.psum_scatter(
            grad_up_w.astype(jnp.bfloat16), ("fsdp", "ctx"), scatter_dimension=0, tiled=True
        ).astype(jnp.float32),
    )
    dense_weight_grad, down_weight_grad = (
        lax.psum_scatter(
            grad_dense_w.astype(jnp.bfloat16), ("fsdp", "ctx"), scatter_dimension=1, tiled=True
        ).astype(jnp.float32),
        lax.psum_scatter(
            grad_down_w.astype(jnp.bfloat16), ("fsdp", "ctx"), scatter_dimension=1, tiled=True
        ).astype(jnp.float32),
    )
    return (
        output,
        input_grad,
        norm_totals[0],
        norm_totals[1],
        norm_totals[2],
        norm_totals[3],
        qkv_weight_grad,
        qkv_bias_grad,
        dense_weight_grad,
        out_bias_grad,
        up_weight_grad,
        up_bias_grad,
        down_weight_grad,
        out_bias_grad,
    )


low = jnp.bfloat16
wide = jnp.float32
tile = 256
megabyte = 1024 * 1024
pace = {"assemble": 4000, "attend_back": 1, "mix": 1}
room = {"project": 56, "mix": 56}


def trade(x, axis, bit):
    peers = lax.axis_size(axis)
    return lax.ppermute(x, axis, [(i, i ^ bit) for i in range(peers)])


def after(x, *earlier):
    return lax.optimization_barrier((x, *earlier))[0]


def meet(*values):
    return lax.optimization_barrier(values)


def block_of(x, index, dim, blocks):
    width = x.shape[dim] // blocks
    return lax.dynamic_slice_in_dim(x, index * width, width, dim)


def lay_out(pieces, place, dim):
    width = pieces[0].shape[dim]
    shape = list(pieces[0].shape)
    shape[dim] = width * 4
    whole = jnp.zeros(shape, pieces[0].dtype)
    for step, piece in enumerate(pieces):
        whole = lax.dynamic_update_slice_in_dim(whole, piece, (place ^ step) * width, dim)
    return whole


def plane_corner(near, far, axis):
    half = near.shape[0] // 2
    corner = [trade(far[:half], axis, 1), trade(near[half:], axis, 2)]
    return jnp.concatenate(corner, axis=0)


def scatter_plane(total, axis, dim, *gate):
    place = lax.axis_index(axis)
    own, near, far, corner = (block_of(total, place ^ k, dim, 4) for k in range(4))
    half = own.shape[0] // 2
    upper = trade(corner[:half].astype(low), axis, 1)
    lower = trade(corner[half:].astype(low), axis, 2)
    upper, lower = after(upper, *gate), after(lower, *gate)
    add = lambda a, b: (a.astype(wide) + b.astype(wide)).astype(low)
    far = jnp.concatenate([add(far[:half], upper), far[half:].astype(low)], axis=0)
    near = jnp.concatenate([near[:half].astype(low), add(near[half:], lower)], axis=0)
    return (own, trade(near, axis, 1), trade(far, axis, 2)), (far, near)


def close_plane(parts, *gate):
    own, near, far = (part.astype(wide) for part in after(parts, *gate))
    return (own + near + far).astype(low)


def half_of(x, index, dim):
    return block_of(x, index, dim, 2)


def join_cores(mine, theirs, core, dim):
    first = jnp.where(core == 0, mine, theirs)
    second = jnp.where(core == 0, theirs, mine)
    return jnp.concatenate([first, second], axis=dim)


def contract(a, b, dims):
    return lax.dot_general(a, b, ((dims[:1], dims[1:]), ((), ())), preferred_element_type=wide)


def place_of(index, size):
    return pl.ds(pl.multiple_of(index * size, size), size)


def fold_rows(x):
    return jnp.sum(x.reshape(x.shape[0] // 8, 8, x.shape[1]), axis=0)


def fixed(shape):
    return pl.BlockSpec(
        shape, lambda step, scalars: (0,) * len(shape), pipeline_mode=pl.Buffered(1)
    )


def kept(shape):
    return pl.BlockSpec(shape, lambda step, scalars: (0,) * len(shape))


def by_row(width):
    return pl.BlockSpec((tile, width), lambda step, scalars: (step, 0))


def by_column(rows, width, first=0):
    return pl.BlockSpec((rows, width), lambda step, scalars: (0, jnp.maximum(step - first, 0)))


def call(
    kernel, name, steps, in_specs, out_specs, out_shape, operands, flops, moved, scratch=(), exps=0
):
    return pl.pallas_call(
        kernel,
        grid_spec=pltpu.PrefetchScalarGridSpec(
            num_scalar_prefetch=1,
            grid=(steps,),
            in_specs=in_specs,
            out_specs=out_specs,
            scratch_shapes=list(scratch),
        ),
        out_shape=out_shape,
        compiler_params=pltpu.CompilerParams(vmem_limit_bytes=room.get(name, 28) * megabyte),
        cost_estimate=pl.CostEstimate(
            flops=int(flops * pace.get(name, 16)),
            bytes_accessed=int(moved * pace.get(name, 16)),
            transcendentals=int(exps * pace.get(name, 16)),
        ),
        name=name,
    )(*operands)


def shaped(*shape, kind=low):
    return jax.ShapeDtypeStruct(shape, kind)


def own_first(piece, core):
    return piece[:, place_of(core, tile)], piece[:, place_of(1 - core, tile)]


def norm_kernel(scalars, *refs):
    pieces, terms = refs[:4], refs[4:8]
    attn_out, ffn_out, stats_out, terms_out = refs[8:]
    width = 8 * tile
    lane = lax.broadcasted_iota(jnp.int32, (strip, 128), 1)
    for start in range(0, stats_out.shape[0], strip):
        here = slice(start, start + strip)
        parts = [piece[here, :].astype(wide) for piece in pieces]
        total = sum(jnp.sum(part, axis=1, keepdims=True) for part in parts)
        mean = total * (1.0 / width)
        spread = sum(
            jnp.sum((part - mean) * (part - mean), axis=1, keepdims=True) for part in parts
        )
        inverse = lax.rsqrt(spread * (1.0 / width) + norm_epsilon)
        for k in range(4):
            block = scalars[2] ^ k
            for half in range(2):
                side = scalars[0] if half == 0 else 1 - scalars[0]
                source = place_of(side, tile)
                columns = place_of(4 * half + block, tile)
                normed = (pieces[k][here, source].astype(wide) - mean) * inverse
                term = terms[k][:, source].astype(wide)
                attn_out[here, columns] = (normed * term[0:1] + term[1:2]).astype(low)
                ffn_out[here, columns] = (normed * term[2:3] + term[3:4]).astype(low)
        stats_out[here, :] = jnp.where(lane < 64, mean, inverse)

    @pl.when(pl.program_id(0) == 0)
    def _():
        for k in range(4):
            for half in range(2):
                side = scalars[0] if half == 0 else 1 - scalars[0]
                columns = place_of(4 * half + (scalars[2] ^ k), tile)
                terms_out[:, columns] = terms[k][0:8, place_of(side, tile)].astype(wide)


def norm(scalars, pieces, rows):
    width = pieces[0].shape[1]
    term = pl.BlockSpec((16, width), lambda step, scalars: (rows // 16, 0))
    return call(
        norm_kernel,
        "norm",
        rows // tile,
        [by_row(width)] * 4 + [term] * 4,
        [by_row(4 * width), by_row(4 * width), by_row(128), kept((8, 4 * width))],
        [
            shaped(rows, 4 * width),
            shaped(rows, 4 * width),
            shaped(rows, 128, kind=wide),
            shaped(8, 4 * width, kind=wide),
        ],
        (scalars, *pieces, *pieces),
        rows * width * 40,
        rows * width * 24,
    )


def assemble_kernel(scalars, own, near, far, upper, lower, first_out, second_out):
    step = pl.program_id(0)
    split = first_out.shape[1]
    middle = upper.shape[0]

    def write(piece, rows):
        first_out[rows, :] = piece[:, :split]
        second_out[rows, :] = piece[:, split:]

    for k, piece in enumerate((own, near, far)):
        pl.when(step == k)(partial(write, piece, slice(None)))

    @pl.when(step == 3)
    def _():
        write(upper, slice(0, middle))
        write(lower, slice(middle, 2 * middle))


def assemble(scalars, pieces, halves, split):
    rows, columns = pieces[0].shape
    place = lambda step, scalars: (scalars[3] ^ step, 0)
    return call(
        assemble_kernel,
        "assemble",
        4,
        [fixed((rows, columns))] * 3 + [fixed((rows // 2, columns))] * 2,
        [pl.BlockSpec((rows, split), place), pl.BlockSpec((rows, columns - split), place)],
        [shaped(4 * rows, split), shaped(4 * rows, columns - split)],
        (scalars, *pieces, *halves),
        rows * columns,
        rows * columns * 16,
    )


strip = 32


def strips(first, rows):
    return [(at, first + at, first + at + strip) for at in range(0, rows, strip)]


def double(rows_in, own, other):
    half = rows_in.shape[1] // 2
    return contract(rows_in[:, :half], own, (1, 0)) + contract(rows_in[:, half:], other, (1, 0))


def heads_kernel(scalars, rows_in, own, other, shift_row, cosine, sine, mine, theirs):
    def run(out):
        for first in range(0, rows_in.shape[0], tile):
            product = double(rows_in.at[first : first + tile, :], own[...], other[...])
            for at, start, stop in strips(first, tile):
                joined = product[at : at + strip] + shift_row[0:1, :]
                for part in range(3):
                    vectors = joined[:, part * HEAD_DIM : (part + 1) * HEAD_DIM]
                    if part < 2:
                        vectors = turn(vectors, cosine[start:stop, :], sine[start:stop, :], 1.0)
                    out[part, start:stop, :] = vectors.astype(low)

    pl.when(pl.program_id(0) == 0)(partial(run, theirs))
    pl.when(pl.program_id(0) == 1)(partial(run, mine))


def heads(scalars, attn_in, weights, shift_row, cosine, sine):
    rows, width = attn_in.shape
    columns = 3 * HEAD_DIM

    def column(step, scalars):
        return 0, jnp.where(step == 0, 1 - scalars[0], scalars[0])

    weight = pl.BlockSpec((width // 2, columns), column)
    return call(
        heads_kernel,
        "heads",
        2,
        [fixed(attn_in.shape), weight, weight, pl.BlockSpec((1, columns), column)]
        + [fixed((rows, 128))] * 2,
        [kept((3, rows, HEAD_DIM))] * 2,
        [shaped(3, rows, HEAD_DIM)] * 2,
        (scalars, attn_in, *weights, shift_row, cosine, sine),
        4 * rows * width * columns,
        2 * (rows * width + 2 * width * columns + 2 * rows * columns),
    )


def expand_kernel(scalars, rows_in, own, other, shift_row, hidden, slope):
    for first in range(0, rows_in.shape[0], tile):
        product = double(rows_in.at[first : first + tile, :], own[...], other[...])
        for at, start, stop in strips(first, tile):
            pre = product[at : at + strip] + shift_row[0:1, :]
            phi = 0.5 + 0.5 * lax.erf(pre * math.sqrt(0.5))
            density = jnp.exp(pre * pre * -0.5) * (1.0 / math.sqrt(2.0 * math.pi))
            hidden[start:stop, :] = (pre * phi).astype(low)
            slope[start:stop, :] = (phi + pre * density).astype(low)


def expand(scalars, ffn_in, weights, shift_row):
    rows, width = ffn_in.shape
    columns = weights[0].shape[1]
    return call(
        expand_kernel,
        "expand",
        columns // tile,
        [fixed(ffn_in.shape)] + [by_column(width // 2, tile)] * 2 + [by_column(1, tile)],
        [by_column(rows, tile)] * 2,
        [shaped(rows, columns), shaped(rows, columns)],
        (scalars, ffn_in, *weights, shift_row),
        2 * rows * width * columns,
        2 * (rows * width + width * columns + 2 * rows * columns),
        exps=2 * rows * columns,
    )


def project_kernel(scalars, mine, theirs, hidden, own, other, out):
    heads_rows = 2 * HEAD_DIM
    for half, weight in enumerate((own, other)):
        total = contract(hidden[...], weight[heads_rows:, :], (1, 0))
        total += contract(mine[...], weight[place_of(scalars[0], HEAD_DIM), :], (1, 0))
        total += contract(theirs[...], weight[place_of(1 - scalars[0], HEAD_DIM), :], (1, 0))
        out[:, half * tile : (half + 1) * tile] = total.astype(out.dtype)


def project(scalars, mine, theirs, hidden, outward):
    rows = hidden.shape[0]
    depth = outward.shape[0]
    return call(
        project_kernel,
        "project",
        4,
        [fixed(mine.shape), fixed(mine.shape), fixed(hidden.shape)]
        + [
            pl.BlockSpec((depth, tile), lambda step, scalars: (0, 2 * step + scalars[0])),
            pl.BlockSpec((depth, tile), lambda step, scalars: (0, 2 * step + 1 - scalars[0])),
        ],
        [by_column(rows, 2 * tile)],
        [shaped(rows, 8 * tile)],
        (scalars, mine, theirs, hidden, outward, outward),
        16 * rows * tile * depth,
        2 * (rows * 8 * tile + depth * 8 * tile + rows * depth),
    )[0]


def hidden_back_kernel(scalars, *refs):
    pieces, (slope, weight) = refs[:4], refs[4:6]
    cotangent, pre_grad, mine, theirs, bias_grad, natural, both = refs[6:]
    step = pl.program_id(0)
    width = pieces[0].shape[1]

    @pl.when(step == 0)
    def _():
        for k in range(4):
            block = scalars[2] ^ k
            natural[:, place_of(block, width)] = pieces[k][...]
            own, other = own_first(pieces[k], scalars[0])
            cotangent[:, place_of(block, tile)] = own
            cotangent[:, place_of(4 + block, tile)] = other

    rows = natural.shape[0]

    @pl.when(step == 0)
    def _():
        both[...] = contract(natural[...], weight[...], (1, 1)).astype(low)
        theirs[...] = both[:, place_of(1 - scalars[0], HEAD_DIM)]
        mine[...] = both[:, place_of(scalars[0], HEAD_DIM)]

    @pl.when(step >= 1)
    def _():
        total = jnp.zeros((8, weight.shape[0]), wide)
        for first in range(0, rows, tile):
            grad = contract(natural[first : first + tile, :], weight[...], (1, 1))
            for at, start, stop in strips(first, tile):
                scaled = grad[at : at + strip] * slope[start:stop, :].astype(wide)
                scaled = scaled.astype(low)
                pre_grad[start:stop, :] = scaled
                total += fold_rows(scaled.astype(wide))
        bias_grad[...] = total


def hidden_back(scalars, pieces, slope, outward):
    rows, width = pieces[0].shape
    depth = outward.shape[0]
    hidden = depth - 2 * HEAD_DIM

    weight = pl.BlockSpec((2 * tile, 4 * width), lambda step, scalars: (step, 0))
    return call(
        hidden_back_kernel,
        "hidden_back",
        depth // (2 * tile),
        [fixed((rows, width))] * 4 + [by_column(rows, 2 * tile, 1), weight],
        [
            kept((rows, 4 * width)),
            by_column(rows, 2 * tile, 1),
            kept((rows, HEAD_DIM)),
            kept((rows, HEAD_DIM)),
            by_column(8, 2 * tile, 1),
        ],
        [
            shaped(rows, 4 * width),
            shaped(rows, hidden),
            shaped(rows, HEAD_DIM),
            shaped(rows, HEAD_DIM),
            shaped(8, hidden, kind=wide),
        ],
        (scalars, *pieces, slope, outward),
        8 * rows * width * depth,
        rows * width * 16 + 8 * width * depth + rows * hidden * 4,
        scratch=[pltpu.VMEM((rows, 4 * width), low), pltpu.VMEM((rows, 2 * HEAD_DIM), low)],
    )


def mix_kernel(
    scalars, mine, theirs, pre_grad, qkv_own, qkv_other, up_own, up_other, terms_own, terms_other,
    stats, first_piece, second_piece, first_out, second_out, sums_own, sums_other, row_sums,
    *both
):
    step = pl.program_id(0)
    rows = pre_grad.shape[0]
    lane = lax.broadcasted_iota(jnp.int32, (strip, 128), 1)

    def run(piece, out, fresh):
        for half, qkv, up, terms, sums in (
            (0, qkv_own, up_own, terms_own, sums_own),
            (1, qkv_other, up_other, terms_other, sums_other),
        ):
            side = scalars[0] if half == 0 else 1 - scalars[0]
            totals = [jnp.zeros((8, tile), wide)] * 4
            attn_gain, ffn_gain = terms[0:1, :], terms[2:3, :]
            for first in range(0, rows, tile):
                here = slice(first, first + tile)
                attn_part = contract(
                    mine[here, :], qkv[:, place_of(scalars[0], 3 * HEAD_DIM)], (1, 1)
                ) + contract(
                    theirs[here, :], qkv[:, place_of(1 - scalars[0], 3 * HEAD_DIM)], (1, 1)
                )
                ffn_part = contract(pre_grad[here, :], up[...], (1, 1))
                for at, start, stop in strips(first, tile):
                    attn, ffn = attn_part[at : at + strip], ffn_part[at : at + strip]
                    mean, inverse = stats[start:stop, 0:1], stats[start:stop, 64:65]
                    held = piece[start:stop, place_of(side, tile)].astype(wide)
                    normed = (held - mean) * inverse
                    mixed = attn * attn_gain + ffn * ffn_gain
                    weighed = mixed * normed
                    parts = (attn * normed, attn, ffn * normed, ffn)
                    totals = [total + fold_rows(part) for total, part in zip(totals, parts)]
                    out[start:stop, half * tile : (half + 1) * tile] = mixed.astype(out.dtype)
                    across = jnp.where(
                        lane < 64,
                        jnp.sum(mixed[:, :128] + mixed[:, 128:], axis=1, keepdims=True),
                        jnp.sum(weighed[:, :128] + weighed[:, 128:], axis=1, keepdims=True),
                    )
                    if fresh and half == 0:
                        row_sums[start:stop, :] = across
                    else:
                        row_sums[start:stop, :] += across
            for place, total in enumerate(totals):
                sums[8 * place : 8 * place + 8, :] = total

    for joined in both:

        @pl.when(step == 0)
        def _():
            joined[:, place_of(scalars[0], 3 * HEAD_DIM)] = mine[...]
            joined[:, place_of(1 - scalars[0], 3 * HEAD_DIM)] = theirs[...]

    pl.when(step == 0)(partial(run, first_piece, first_out, True))
    pl.when(step == 1)(partial(run, second_piece, second_out, False))


def mix(scalars, mine, theirs, pre_grad, qkv, up, terms, stats, pieces, order, kinds, join=False):
    rows = pre_grad.shape[0]
    width = pieces[0].shape[1]
    depth = qkv[0].shape[1] + up[0].shape[1]

    def block(step, scalars):
        return scalars[2] ^ jnp.where(step == 0, order[0], order[1])

    weight = lambda x: pl.BlockSpec((tile, x.shape[1]), lambda step, scalars: (block(step, scalars), 0))
    term = lambda first: pl.BlockSpec((8, tile), lambda step, scalars: (0, first + block(step, scalars)))
    sums = pl.BlockSpec((32, tile), lambda step, scalars: (0, step))
    return call(
        mix_kernel,
        "mix",
        2,
        [fixed(mine.shape), fixed(mine.shape), fixed(pre_grad.shape)]
        + [weight(x) for x in (*qkv, *up)]
        + [term(0), term(4), fixed((rows, 128))]
        + [fixed((rows, width))] * 2,
        [kept((rows, width))] * 2
        + [sums, sums, kept((rows, 128))]
        + [kept((rows, 6 * HEAD_DIM))] * join,
        [shaped(rows, width, kind=kind) for kind in kinds]
        + [shaped(32, 2 * tile, kind=wide)] * 2
        + [shaped(rows, 128, kind=wide)]
        + [shaped(rows, 6 * HEAD_DIM)] * join,
        (scalars, mine, theirs, pre_grad, *qkv, *up, terms, terms, stats, pieces[order[0]], pieces[order[1]]),
        4 * rows * width * depth,
        2 * (4 * rows * width + 2 * depth * width + rows * depth),
    )


def attend_kernel(scalars, mine, theirs, info, packed, own_out, twin_out, log_total, natural, scale):
    rows = natural.shape[0]
    blocks = rows // tile
    own = place_of(scalars[0], rows // 2)
    twin = place_of(1 - scalars[0], rows // 2)
    for part in range(3):
        packed[part, own, :] = mine[part]
        packed[part, twin, :] = theirs[part]
    for block in range(blocks):
        span = (block + 1) * tile
        query = packed[0, block * tile : span, :]
        about = info[:, block * tile : span]
        scores = scores_of(packed[1, :span, :], query, about, scalars[1], block * tile, scale)
        top = jnp.max(scores, axis=0, keepdims=True)
        powers = jnp.exp(scores - top)
        total = jnp.sum(powers, axis=0, keepdims=True)
        probs = (powers * (1.0 / total)).astype(low)
        natural[block * tile : span, :] = contract(probs, packed[2, :span, :], (0, 0)).astype(low)
        log_total[0:1, block * tile : span] = top + jnp.log(total)
    own_out[...] = natural[own, :]
    twin_out[...] = natural[twin, :]


def attend(scalars, mine, theirs, info):
    held = mine.shape[1]
    rows = 2 * held
    pairs = rows * (rows + tile) // 2
    return call(
        partial(attend_kernel, scale=1.0 / math.sqrt(HEAD_DIM)),
        "attend",
        1,
        [fixed(mine.shape), fixed(mine.shape), fixed((8, rows))],
        [kept((3, rows, HEAD_DIM)), kept((held, HEAD_DIM)), kept((held, HEAD_DIM)), kept((8, rows))],
        [
            shaped(3, rows, HEAD_DIM),
            shaped(held, HEAD_DIM),
            shaped(held, HEAD_DIM),
            shaped(8, rows, kind=wide),
        ],
        (scalars, mine, theirs, info),
        pairs * HEAD_DIM * 4,
        rows * HEAD_DIM * 16,
        scratch=[pltpu.VMEM((rows, HEAD_DIM), low)],
        exps=pairs,
    )


def attend_back_kernel(
    scalars, packed, own_grads, twin_grads, log_total, cosine, sine, info, own_out, twin_out,
    bias_grad, grads, natural, key_grad, value_grad, scale
):
    rows = grads.shape[0]
    blocks = rows // tile
    shift = scalars[0] * (blocks // 2)
    own = place_of(scalars[0], rows // 2)
    twin = place_of(1 - scalars[0], rows // 2)
    grads[own, :] = own_grads[...]
    grads[twin, :] = twin_grads[...]
    bias_total = jnp.zeros((8, 3 * HEAD_DIM), wide)
    for block in reversed(range(blocks)):
        span = (block + 1) * tile
        before = block * tile
        query = packed[0, before:span, :]
        about = info[:, before:span]
        there = place_of(lax.rem(block + shift, blocks), tile)
        grad = grads[before:span, :]
        scores = scores_of(packed[1, :span, :], query, about, scalars[1], before, scale)
        probs = jnp.exp(scores - log_total[0:1, before:span])
        value_part = contract(probs.astype(low), grad, (1, 0))
        dots = contract(packed[2, :span, :], grad, (1, 1))
        delta = jnp.sum(probs * dots, axis=0, keepdims=True)
        score_grad = (probs * (dots - delta)).astype(low)
        query_grad = contract(score_grad, packed[1, :span, :], (0, 0)) * scale
        key_part = contract(score_grad, query, (1, 0)) * scale
        if block == blocks - 1:
            key_grad[...] = key_part
            value_grad[...] = value_part
        else:
            key_grad[:span, :] += key_part
            value_grad[:span, :] += value_part
        parts = (
            turn(query_grad, cosine[there, :], sine[there, :], -1.0),
            turn(key_grad[before:span, :], cosine[there, :], sine[there, :], -1.0),
            value_grad[before:span, :],
        )
        together = jnp.concatenate(parts, axis=1).astype(low)
        natural[before:span, :] = together
        bias_total += fold_rows(together.astype(wide))
    bias_grad[...] = bias_total
    own_out[...] = natural[own, :]
    twin_out[...] = natural[twin, :]


def attend_back(scalars, packed, own_grads, twin_grads, log_total, cosine, sine, info):
    held = own_grads.shape[0]
    rows = 2 * held
    pairs = rows * (rows + tile) // 2
    return call(
        partial(attend_back_kernel, scale=1.0 / math.sqrt(HEAD_DIM)),
        "attend_back",
        1,
        [
            fixed((3, rows, HEAD_DIM)),
            fixed((held, HEAD_DIM)),
            fixed((held, HEAD_DIM)),
            fixed((8, rows)),
            fixed((rows, 128)),
            fixed((rows, 128)),
            fixed((8, rows)),
        ],
        [kept((held, 3 * HEAD_DIM)), kept((held, 3 * HEAD_DIM)), kept((8, 3 * HEAD_DIM))],
        [
            shaped(held, 3 * HEAD_DIM),
            shaped(held, 3 * HEAD_DIM),
            shaped(8, 3 * HEAD_DIM, kind=wide),
        ],
        (scalars, packed, own_grads, twin_grads, log_total, cosine, sine, info),
        pairs * HEAD_DIM * 10,
        rows * HEAD_DIM * 16,
        scratch=[
            pltpu.VMEM((rows, HEAD_DIM), low),
            pltpu.VMEM((rows, 3 * HEAD_DIM), low),
            pltpu.VMEM((rows, HEAD_DIM), wide),
            pltpu.VMEM((rows, HEAD_DIM), wide),
        ],
        exps=pairs,
    )


def turn(rows, cosine, sine, sign):
    half_rot = ROTARY // 2
    lane = lax.broadcasted_iota(jnp.int32, cosine.shape, 1)
    front = rows[:, :128]
    ahead = pltpu.roll(front, 128 - half_rot, 1)
    behind = pltpu.roll(front, half_rot, 1)
    other = jnp.where(lane < half_rot, -ahead, behind)
    turned = front * cosine + other * (sine * sign)
    return jnp.concatenate([turned, rows[:, 128:]], axis=1)


def scores_of(keys, query, info, trunk_end, first_row, scale):
    scores = contract(keys, query, (1, 1)) * scale
    key_place = lax.broadcasted_iota(jnp.int32, scores.shape, 0)
    query_place = first_row + lax.broadcasted_iota(jnp.int32, scores.shape, 1)
    seen = (
        (key_place < trunk_end)
        | ((key_place >= info[0:1]) & (key_place < info[1:2]))
        | (key_place >= info[2:3])
    ) & (key_place <= query_place)
    return jnp.where(seen, scores, masked_score)


def tree_info(lengths, parent, rows):
    labels = jnp.arange(SEGS)
    ends = jnp.sum(jnp.where(labels[None, :] <= labels[:, None], lengths[None, :], 0), axis=1)
    starts = ends - lengths
    hot_parent = parent[:, None] == labels[None, :]
    parent_start = jnp.sum(jnp.where(hot_parent, starts[None, :], 0), axis=1)
    parent_end = jnp.sum(jnp.where(hot_parent, ends[None, :], 0), axis=1)
    places = jnp.arange(rows, dtype=jnp.int32)
    inside = (places[None, :] >= starts[:, None]) & (places[None, :] < ends[:, None])
    pick = lambda table: jnp.sum(jnp.where(inside, table[:, None], 0), axis=0)
    spans = [pick(parent_start), pick(parent_end), pick(starts)]
    return jnp.stack(spans + [places] * 5).astype(jnp.int32), ends[0]


def rotary_tables(depth):
    half_rot = ROTARY // 2
    lane = jnp.arange(128)
    frequency = jnp.power(10000.0, -2.0 * (lane % half_rot).astype(wide) / ROTARY)
    frequency = jnp.where(lane < ROTARY, frequency, 0.0)
    angles = depth.astype(wide)[:, None] * frequency[None, :]
    return jnp.cos(angles), jnp.sin(angles)


def on_device_split(
    residual,
    out_grad,
    path_depth,
    seg_lengths,
    parents,
    attn_norm_gain,
    attn_norm_bias,
    ffn_norm_gain,
    ffn_norm_bias,
    qkv_weight,
    qkv_bias,
    dense_weight,
    dense_bias,
    up_weight,
    up_bias,
    down_weight,
    down_bias,
):
    core = lax.axis_index("ctx")
    line = lax.axis_index("tp")
    plane = lax.axis_index("fsdp")
    rows, held_width = residual.shape
    width = 4 * held_width
    half = width // 2

    norm_rows = jnp.stack([attn_norm_gain, attn_norm_bias, ffn_norm_gain, ffn_norm_bias] * 4)
    held = jnp.concatenate([residual, norm_rows], axis=0)
    inward = jnp.concatenate([qkv_weight, up_weight], axis=1)
    split = qkv_weight.shape[1]
    other_depth = trade(path_depth, "ctx", 1)
    cosine, sine = rotary_tables(jnp.concatenate([path_depth, other_depth]))
    info, trunk_end = tree_info(seg_lengths[0], parents[0], 2 * rows)
    scalars = jnp.stack([core, trunk_end, line, plane]).astype(jnp.int32)
    qkv_shift = qkv_bias.astype(wide)[None, :]
    up_shift = up_bias.astype(wide)[None, :]
    near, far, cosine, sine, info = meet(
        trade(held, "tp", 1), trade(held, "tp", 2), cosine, sine, info
    )
    inward_near, inward_far, inward = meet(
        trade(inward, "fsdp", 1), trade(inward, "fsdp", 2), inward, near
    )[:3]
    middle = inward.shape[0] // 2
    upper_corner = trade(inward_far[:middle], "fsdp", 1)
    lower_corner = trade(inward_near[middle:], "fsdp", 2)
    corner = trade(far, "tp", 1)
    upper_corner, lower_corner, corner = meet(upper_corner, lower_corner, corner)
    qkv_own, up_own = assemble(
        scalars, (inward, inward_near, inward_far), (upper_corner, lower_corner), split
    )
    pieces = (held, near, far, corner)

    def both_cores(own, *gate):
        return own, trade(after(own, *gate), "ctx", 1)

    outward = jnp.concatenate([dense_weight, down_weight], axis=0)
    outward = lax.all_gather(after(outward, upper_corner), ("fsdp", "ctx"), axis=1, tiled=True)

    qkv = both_cores(qkv_own)
    up = both_cores(up_own)
    first_grad = after(out_grad, corner)
    grad_near = trade(first_grad, "tp", 1)
    grad_far = trade(first_grad, "tp", 2)

    attn_in, ffn_in, stats, terms = norm(scalars, pieces, rows)
    mine, theirs = heads(scalars, attn_in, qkv, qkv_shift, cosine, sine)
    theirs = trade(theirs, "ctx", 1)
    hidden, slope = expand(after(scalars, mine), ffn_in, up, up_shift)
    grad_corner = trade(after(grad_far, slope), "tp", 1)
    packed, attended, twin_attended, log_total = attend(
        after(scalars, slope, grad_near, grad_far), mine, theirs, info
    )
    other_attended = trade(twin_attended, "ctx", 1)
    chip_out = project(scalars, attended, other_attended, hidden, outward)
    shared_out = lax.psum_scatter(chip_out, "tp", scatter_dimension=1, tiled=True)

    grad_pieces = (out_grad, grad_near, grad_far, grad_corner)
    cotangent, pre_grad, head_grad, other_grad, up_bias_rows = hidden_back(
        after(scalars, chip_out), grad_pieces, slope, outward
    )
    other_grad = trade(other_grad, "ctx", 1)

    def outer(left, right):
        return contract(left, right, (0, 0))

    def add_low(own, arrived):
        return (own + arrived.astype(wide)).astype(low)

    def to_owner(total, dim):
        return lax.psum_scatter(total, "fsdp", scatter_dimension=dim, tiled=True)

    both_attended = join_cores(attended, other_attended, core, 1)
    down_other = outer(after(hidden, pre_grad), cotangent[:, half:]).astype(low)
    down_arrived = trade(down_other, "ctx", 1)
    up_other = outer(after(ffn_in, down_other)[:, half:], pre_grad).astype(low)
    up_arrived = trade(up_other, "ctx", 1)
    down_total = add_low(outer(after(hidden, up_other), cotangent[:, :half]), down_arrived)
    joined_grad, twin_grad, qkv_bias_rows = attend_back(
        after(scalars, down_total), packed, head_grad, other_grad, log_total, cosine, sine, info
    )
    other_joined = trade(twin_grad, "ctx", 1)
    down_parts, down_hop = scatter_plane(down_total, "fsdp", 1, joined_grad)
    dense_other = outer(after(both_attended, joined_grad, *down_hop), cotangent[:, half:]).astype(low)
    dense_arrived = trade(dense_other, "ctx", 1)
    up_total = add_low(outer(after(ffn_in, dense_other)[:, :half], pre_grad), up_arrived)
    up_grad = to_owner(up_total, 0)
    dense_total = add_low(
        outer(after(both_attended, up_total, other_joined), cotangent[:, :half]), dense_arrived
    )
    mix_in = (joined_grad, other_joined, pre_grad, qkv, up, terms, stats, pieces)
    *leave, sums_a, sums_b, row_a, both_joined = mix(
        after(scalars, dense_total), *mix_in, (3, 1), (low, low), True
    )
    mixed_side = trade(leave[0], "tp", 1)
    *stay_mixed, sums_c, sums_d, row_b = mix(
        after(scalars, leave[0], shared_out), *mix_in, (2, 0), (wide, wide)
    )
    passed = (stay_mixed[0] + mixed_side.astype(wide)).astype(low)
    row_sums = row_a + row_b
    row_total = jnp.stack([row_sums[:, 0], row_sums[:, 64]])
    fold = lambda x: jnp.sum(x.reshape(4, 8, 2, tile), axis=1)
    gather_sums = lambda own, other: jnp.stack([fold(own), fold(other)], axis=2).reshape(4, 2, 2 * tile)
    leaving, norm_sums = gather_sums(sums_a, sums_b), gather_sums(sums_c, sums_d)
    hop_side = trade(jnp.concatenate([leaving.reshape(-1), row_total.reshape(-1)]), "tp", 1)
    norm_sums = norm_sums + hop_side[: 8 * held_width].reshape(norm_sums.shape)
    row_total = row_total + hop_side[8 * held_width :].reshape(row_total.shape)
    hop_far = trade(jnp.concatenate([norm_sums[:, 0].reshape(-1), row_total.reshape(-1)]), "tp", 2)
    qkv_other = outer(
        after(attn_in, stay_mixed[0], passed, hop_side, down_parts)[:, half:], both_joined
    ).astype(low)
    qkv_arrived = trade(qkv_other, "ctx", 1)
    far_mixed = trade(after(passed, hop_far), "tp", 2)
    mixed_near = trade(after(leave[1], hop_far), "tp", 1)
    norm_total = norm_sums[:, 1] + hop_far[: 4 * held_width].reshape(4, held_width)
    row_total = row_total + hop_far[4 * held_width :].reshape(row_total.shape)
    row_means = row_total / width
    norm_total = join_cores(norm_total[:, :tile], norm_total[:, tile:], core, 1)
    down_grad = close_plane(down_parts, qkv_other)
    qkv_total = add_low(
        outer(after(attn_in, qkv_other, down_grad, hop_far)[:, :half], both_joined), qkv_arrived
    )
    shared_out = after(shared_out, qkv_total).astype(wide)
    shared_out = join_cores(shared_out[:, :tile], shared_out[:, tile:], core, 1)
    output = (
        residual.astype(wide) + shared_out + dense_bias.astype(wide) + down_bias.astype(wide)
    ).astype(low)

    held_grad_sum = jnp.sum(after(out_grad, qkv_total).astype(wide), axis=0)
    columns = jnp.concatenate(
        [
            norm_total.reshape(-1),
            held_grad_sum,
            jnp.sum(up_bias_rows, axis=0),
            jnp.sum(qkv_bias_rows, axis=0),
        ]
    )
    columns = after(columns, qkv_total)
    columns = columns + trade(columns, "fsdp", 1)
    columns = columns + trade(columns, "fsdp", 2)
    dense_grad = to_owner(after(dense_total, up_grad, qkv_total), 1)
    qkv_parts, qkv_hop = scatter_plane(qkv_total, "fsdp", 0)
    qkv_grad = close_plane(qkv_parts)
    dense_grad, up_grad = after(dense_grad, *qkv_hop), after(up_grad, *qkv_hop)
    other_columns = trade(columns, "ctx", 1)
    cut = columns.shape[0] - qkv_bias.shape[0] // 2
    qkv_bias_grad = join_cores(columns[cut:], other_columns[cut:], core, 0)
    together = columns[:cut] + other_columns[:cut]
    norm_grads = together[:width].reshape(4, held_width)
    out_bias_grad = together[width : width + held_width]
    up_bias_grad = together[width + held_width :]


    far_mixed = after(far_mixed, mixed_near, other_columns, *qkv_hop)
    shared_mixed = stay_mixed[1] + mixed_near.astype(wide) + far_mixed.astype(wide)
    shared_mixed = join_cores(shared_mixed[:, :tile], shared_mixed[:, tile:], core, 1)
    mean = stats[:, 0:1]
    inverse = stats[:, 64:65]
    own_normed = (residual.astype(wide) - mean) * inverse
    back = inverse * (shared_mixed - row_means[0][:, None] - own_normed * row_means[1][:, None])
    input_grad = (out_grad.astype(wide) + back).astype(low)
    return (
        output,
        input_grad,
        norm_grads[0],
        norm_grads[1],
        norm_grads[2],
        norm_grads[3],
        qkv_grad.astype(wide),
        qkv_bias_grad,
        dense_grad.astype(wide),
        out_bias_grad,
        up_grad.astype(wide),
        up_bias_grad,
        down_grad.astype(wide),
        out_bias_grad,
    )


def splits_heads(mesh):
    return mesh.shape["tp"] == 4 and mesh.shape["fsdp"] == 4 and mesh.shape["ctx"] == 2


def solution(mesh):
    placed = (
        P(("fsdp", "ctx"), "tp"),
        P(("fsdp", "ctx"), "tp"),
        P(("fsdp", "ctx")),
        P("fsdp", None),
        P("fsdp", None),
        P("tp"),
        P("tp"),
        P("tp"),
        P("tp"),
        P(("fsdp", "ctx"), "tp"),
        P("tp"),
        P("tp", ("fsdp", "ctx")),
        P("tp"),
        P(("fsdp", "ctx"), "tp"),
        P("tp"),
        P("tp", ("fsdp", "ctx")),
        P("tp"),
    )
    return jax.shard_map(
        on_device_split if splits_heads(mesh) else on_device,
        mesh=mesh,
        in_specs=placed,
        out_specs=(
            P(("fsdp", "ctx"), "tp"),
            P(("fsdp", "ctx"), "tp"),
            P("tp"),
            P("tp"),
            P("tp"),
            P("tp"),
            P(("fsdp", "ctx"), "tp"),
            P("tp"),
            P("tp", ("fsdp", "ctx")),
            P("tp"),
            P(("fsdp", "ctx"), "tp"),
            P("tp"),
            P("tp", ("fsdp", "ctx")),
            P("tp"),
        ),
        check_vma=False,
    )
```

```python
from functools import partial
import math

import jax
import jax.numpy as jnp
from jax import lax
from jax.experimental import pallas as pl
from jax.experimental.pallas import tpu as pltpu
from jax.sharding import PartitionSpec as P

HEAD_DIM = 256
ROTARY = 64
SEGS = 13


norm_epsilon = 1e-05
masked_score = -1e30
block_limit = 512


def from_behind(x, axis, by):
    peers = lax.axis_size(axis)
    pairs = [(i, i + by) for i in range(peers) if 0 <= i + by < peers]
    return lax.ppermute(x, axis, pairs)


def rotary(vectors, places):
    half_rot = ROTARY // 2
    frequency = jnp.power(10000.0, -2.0 * jnp.arange(half_rot).astype(jnp.float32) / ROTARY)
    angles = places.astype(jnp.float32)[:, None] * frequency[None, :]
    cosine = jnp.cos(angles)[:, None, :]
    sine_part = jnp.sin(angles)[:, None, :]
    first_half = vectors[..., :half_rot]
    second_half = vectors[..., half_rot:ROTARY]
    return jnp.concatenate(
        [
            first_half * cosine - second_half * sine_part,
            second_half * cosine + first_half * sine_part,
            vectors[..., ROTARY:],
        ],
        axis=-1,
    )


def tree_tables(lengths, parent):
    starts = jnp.cumsum(lengths) - lengths
    labels = jnp.arange(SEGS)
    grand_parent = jnp.sum(
        jnp.where(parent[:, None] == labels[None, :], parent[None, :], 0), axis=1
    )
    ancestor = (
        (labels[None, :] == labels[:, None])
        | (labels[None, :] == parent[:, None])
        | (labels[None, :] == grand_parent[:, None])
    )
    return (starts, ancestor.astype(jnp.float32))


def segment_onehot(places, starts):
    membership = jnp.sum((places[:, None] >= starts[None, :]).astype(jnp.int32), axis=1) - 1
    return (membership[:, None] == jnp.arange(SEGS)[None, :]).astype(jnp.float32)


def visible(hot_query, place_query, hot_key, place_key, ancestor):
    reachable = jnp.dot(jnp.dot(hot_query, ancestor), hot_key.T)
    return (reachable > 0.5) & (place_key[None, :] <= place_query[:, None])


def on_device(
    residual,
    out_grad,
    path_depth,
    seg_lengths,
    parents,
    attn_norm_gain,
    attn_norm_bias,
    ffn_norm_gain,
    ffn_norm_bias,
    qkv_weight,
    qkv_bias,
    dense_weight,
    dense_bias,
    up_weight,
    up_bias,
    down_weight,
    down_bias,
):
    row_count = residual.shape[0]
    local_width = residual.shape[1]
    head_count = qkv_weight.shape[1] // (3 * HEAD_DIM)
    score_scale = 1.0 / math.sqrt(HEAD_DIM)
    ctx_index = lax.axis_index("ctx")
    tp_index = lax.axis_index("tp")
    norm_stack = jnp.stack([attn_norm_gain, attn_norm_bias, ffn_norm_gain, ffn_norm_bias])
    full_rows, norm_terms = (
        lax.all_gather(residual, "tp", axis=1, tiled=True),
        lax.all_gather(norm_stack, "tp", axis=1, tiled=True),
    )
    norm_terms = norm_terms.astype(jnp.float32)
    qkv_full, up_full = (
        lax.all_gather(qkv_weight, ("fsdp", "ctx"), axis=0, tiled=True),
        lax.all_gather(up_weight, ("fsdp", "ctx"), axis=0, tiled=True),
    )
    dense_full, down_full = (
        lax.all_gather(dense_weight, ("fsdp", "ctx"), axis=1, tiled=True),
        lax.all_gather(down_weight, ("fsdp", "ctx"), axis=1, tiled=True),
    )
    rows_wide = full_rows.astype(jnp.float32)
    centred = rows_wide - jnp.mean(rows_wide, axis=1, keepdims=True)
    inverse_scale = lax.rsqrt(jnp.mean(centred * centred, axis=1, keepdims=True) + norm_epsilon)
    normed = centred * inverse_scale
    attn_in = (normed * norm_terms[0] + norm_terms[1]).astype(jnp.bfloat16)
    ffn_in = (normed * norm_terms[2] + norm_terms[3]).astype(jnp.bfloat16)
    joined = (
        jnp.dot(attn_in, qkv_full, preferred_element_type=jnp.float32)
        + qkv_bias.astype(jnp.float32)
    ).reshape(row_count, head_count, 3, HEAD_DIM)
    queries_pre = joined[:, :, 0]
    query_rows = rotary(queries_pre, path_depth).astype(jnp.bfloat16)
    key_rows = rotary(joined[:, :, 1], path_depth).astype(jnp.bfloat16)
    value_rows = joined[:, :, 2].astype(jnp.bfloat16)
    far_keys, far_values = from_behind((key_rows, value_rows), "ctx", 1)
    starts, ancestor = tree_tables(seg_lengths[0], parents[0])
    places = ctx_index * row_count + jnp.arange(row_count, dtype=jnp.int32)
    key_places = jnp.concatenate([places - row_count, places])
    hot_query = segment_onehot(places, starts)
    hot_key = segment_onehot(key_places, starts)
    all_keys = jnp.concatenate([far_keys, key_rows], axis=0)
    all_values = jnp.concatenate([far_values, value_rows], axis=0)
    block_starts = list(range(0, row_count, block_limit))

    def block_scores(block_start, block_size, key_set):
        key_span = row_count + block_start + block_size
        query_block = query_rows[block_start : block_start + block_size]
        scores = (
            jnp.einsum(
                "nhe,lhe->hnl", query_block, key_set[:key_span], preferred_element_type=jnp.float32
            )
            * score_scale
        )
        reachable = visible(
            hot_query[block_start : block_start + block_size],
            places[block_start : block_start + block_size],
            hot_key[:key_span],
            key_places[:key_span],
            ancestor,
        )
        return jnp.where(reachable[None], scores, masked_score)

    out_blocks = []
    log_totals = []
    for block_start in block_starts:
        block_size = min(block_limit, row_count - block_start)
        key_span = row_count + block_start + block_size
        scores = block_scores(block_start, block_size, all_keys)
        row_top = jnp.max(scores, axis=-1, keepdims=True)
        exp_scores = jnp.exp(scores - row_top)
        exp_total = jnp.sum(exp_scores, axis=-1, keepdims=True)
        attn_probs = exp_scores / exp_total
        out_blocks.append(
            jnp.einsum(
                "hnl,lhe->nhe",
                attn_probs.astype(jnp.bfloat16),
                all_values[:key_span],
                preferred_element_type=jnp.float32,
            )
        )
        log_totals.append(row_top + jnp.log(exp_total))
    attended = (
        jnp.concatenate(out_blocks, axis=0)
        .reshape(row_count, head_count * HEAD_DIM)
        .astype(jnp.bfloat16)
    )
    hidden_pre = jnp.dot(ffn_in, up_full, preferred_element_type=jnp.float32) + up_bias.astype(
        jnp.float32
    )
    hidden_wide, gelu_back = jax.vjp(partial(jax.nn.gelu, approximate=False), hidden_pre)
    hidden = hidden_wide.astype(jnp.bfloat16)
    partial_out = jnp.dot(attended, dense_full, preferred_element_type=jnp.float32) + jnp.dot(
        hidden, down_full, preferred_element_type=jnp.float32
    )
    shared_out = lax.psum_scatter(partial_out, "tp", scatter_dimension=1, tiled=True)
    output = (
        residual.astype(jnp.float32)
        + shared_out
        + dense_bias.astype(jnp.float32)
        + down_bias.astype(jnp.float32)
    ).astype(jnp.bfloat16)
    cotangent = lax.all_gather(out_grad, "tp", axis=1, tiled=True)
    grad_out_bias = jnp.sum(out_grad.astype(jnp.float32), axis=0)
    grad_dense_w = jnp.einsum("rf,rd->fd", attended, cotangent, preferred_element_type=jnp.float32)
    grad_down_w = jnp.einsum("rf,rd->fd", hidden, cotangent, preferred_element_type=jnp.float32)
    grad_attended = jnp.einsum(
        "rd,fd->rf", cotangent, dense_full, preferred_element_type=jnp.float32
    ).astype(jnp.bfloat16)
    grad_hidden = jnp.einsum("rd,fd->rf", cotangent, down_full, preferred_element_type=jnp.float32)
    grad_pre = gelu_back(grad_hidden)[0].astype(jnp.bfloat16)
    grad_up_w = jnp.einsum("rd,rf->df", ffn_in, grad_pre, preferred_element_type=jnp.float32)
    grad_up_b = jnp.sum(grad_pre.astype(jnp.float32), axis=0)
    grad_ffn_in = jnp.einsum("rf,df->rd", grad_pre, up_full, preferred_element_type=jnp.float32)
    key_set = all_keys
    grad_att_heads = grad_attended.reshape(row_count, head_count, HEAD_DIM)
    grad_query_parts = []
    grad_key_all = jnp.zeros((2 * row_count, head_count, HEAD_DIM), jnp.float32)
    grad_value_all = jnp.zeros((2 * row_count, head_count, HEAD_DIM), jnp.float32)
    for block_number, block_start in enumerate(block_starts):
        block_size = min(block_limit, row_count - block_start)
        key_span = row_count + block_start + block_size
        scores = block_scores(block_start, block_size, key_set)
        attn_probs = jnp.exp(scores - log_totals[block_number])
        grad_block = grad_att_heads[block_start : block_start + block_size]
        grad_value_all = grad_value_all.at[:key_span].add(
            jnp.einsum(
                "hnl,nhe->lhe",
                attn_probs.astype(jnp.bfloat16),
                grad_block,
                preferred_element_type=jnp.float32,
            )
        )
        grad_dots = jnp.einsum(
            "nhe,lhe->hnl", grad_block, all_values[:key_span], preferred_element_type=jnp.float32
        )
        row_delta = jnp.sum(attn_probs * grad_dots, axis=-1, keepdims=True)
        grad_scores = (attn_probs * (grad_dots - row_delta)).astype(jnp.bfloat16)
        grad_query_parts.append(
            jnp.einsum(
                "hnl,lhe->nhe", grad_scores, key_set[:key_span], preferred_element_type=jnp.float32
            )
            * score_scale
        )
        grad_key_all = grad_key_all.at[:key_span].add(
            jnp.einsum(
                "hnl,nhe->lhe",
                grad_scores,
                query_rows[block_start : block_start + block_size],
                preferred_element_type=jnp.float32,
            )
            * score_scale
        )
    arriving_keys, arriving_values = from_behind(
        (grad_key_all[:row_count], grad_value_all[:row_count]), "ctx", -1
    )
    grad_keys = grad_key_all[row_count:] + arriving_keys
    grad_values = grad_value_all[row_count:] + arriving_values
    grad_queries = jnp.concatenate(grad_query_parts, axis=0)
    rotated_unused, rotary_back = jax.vjp(lambda vectors: rotary(vectors, path_depth), queries_pre)
    grad_joined = (
        jnp.stack([rotary_back(grad_queries)[0], rotary_back(grad_keys)[0], grad_values], axis=2)
        .astype(jnp.bfloat16)
        .reshape(row_count, head_count * 3 * HEAD_DIM)
    )
    grad_qkv_w = jnp.einsum("rd,rf->df", attn_in, grad_joined, preferred_element_type=jnp.float32)
    grad_qkv_b = jnp.sum(grad_joined.astype(jnp.float32), axis=0)
    grad_attn_in = jnp.einsum(
        "rf,df->rd", grad_joined, qkv_full, preferred_element_type=jnp.float32
    )
    total_attn, total_ffn = lax.psum((grad_attn_in, grad_ffn_in), "tp")

    def norm_back(total_grad, gain_row):
        scaled = total_grad * gain_row
        mean_plain = jnp.mean(scaled, axis=1, keepdims=True)
        mean_normed = jnp.mean(scaled * normed, axis=1, keepdims=True)
        back_rows = inverse_scale * (scaled - mean_plain - normed * mean_normed)
        gain_grad = jnp.sum(total_grad * normed, axis=0)
        shift_grad = jnp.sum(total_grad, axis=0)
        return (
            lax.dynamic_slice_in_dim(back_rows, tp_index * local_width, local_width, 1),
            lax.dynamic_slice_in_dim(gain_grad, tp_index * local_width, local_width, 0),
            lax.dynamic_slice_in_dim(shift_grad, tp_index * local_width, local_width, 0),
        )

    back_attn, attn_gain_grad, attn_shift_grad = norm_back(total_attn, norm_terms[0])
    back_ffn, ffn_gain_grad, ffn_shift_grad = norm_back(total_ffn, norm_terms[2])
    norm_grads = jnp.stack([attn_gain_grad, attn_shift_grad, ffn_gain_grad, ffn_shift_grad])
    back_total = back_attn + back_ffn
    input_grad = (out_grad.astype(jnp.float32) + back_total).astype(jnp.bfloat16)
    qkv_bias_grad, up_bias_grad, out_bias_grad, norm_totals = lax.psum(
        (grad_qkv_b, grad_up_b, grad_out_bias, norm_grads), ("fsdp", "ctx")
    )
    qkv_weight_grad, up_weight_grad = (
        lax.psum_scatter(
            grad_qkv_w.astype(jnp.bfloat16), ("fsdp", "ctx"), scatter_dimension=0, tiled=True
        ).astype(jnp.float32),
        lax.psum_scatter(
            grad_up_w.astype(jnp.bfloat16), ("fsdp", "ctx"), scatter_dimension=0, tiled=True
        ).astype(jnp.float32),
    )
    dense_weight_grad, down_weight_grad = (
        lax.psum_scatter(
            grad_dense_w.astype(jnp.bfloat16), ("fsdp", "ctx"), scatter_dimension=1, tiled=True
        ).astype(jnp.float32),
        lax.psum_scatter(
            grad_down_w.astype(jnp.bfloat16), ("fsdp", "ctx"), scatter_dimension=1, tiled=True
        ).astype(jnp.float32),
    )
    return (
        output,
        input_grad,
        norm_totals[0],
        norm_totals[1],
        norm_totals[2],
        norm_totals[3],
        qkv_weight_grad,
        qkv_bias_grad,
        dense_weight_grad,
        out_bias_grad,
        up_weight_grad,
        up_bias_grad,
        down_weight_grad,
        out_bias_grad,
    )


low = jnp.bfloat16
wide = jnp.float32
tile = 256
megabyte = 1024 * 1024
pace = {"assemble": 4000, "attend_back": 1, "mix": 1}
room = {"project": 56, "mix": 56}


def trade(x, axis, bit):
    peers = lax.axis_size(axis)
    return lax.ppermute(x, axis, [(i, i ^ bit) for i in range(peers)])


def after(x, *earlier):
    return lax.optimization_barrier((x, *earlier))[0]


def meet(*values):
    return lax.optimization_barrier(values)


def block_of(x, index, dim, blocks):
    width = x.shape[dim] // blocks
    return lax.dynamic_slice_in_dim(x, index * width, width, dim)


def lay_out(pieces, place, dim):
    width = pieces[0].shape[dim]
    shape = list(pieces[0].shape)
    shape[dim] = width * 4
    whole = jnp.zeros(shape, pieces[0].dtype)
    for step, piece in enumerate(pieces):
        whole = lax.dynamic_update_slice_in_dim(whole, piece, (place ^ step) * width, dim)
    return whole


def plane_corner(near, far, axis):
    half = near.shape[0] // 2
    corner = [trade(far[:half], axis, 1), trade(near[half:], axis, 2)]
    return jnp.concatenate(corner, axis=0)


def scatter_plane(total, axis, dim, *gate):
    place = lax.axis_index(axis)
    own, near, far, corner = (block_of(total, place ^ k, dim, 4) for k in range(4))
    half = own.shape[0] // 2
    upper = trade(corner[:half].astype(low), axis, 1)
    lower = trade(corner[half:].astype(low), axis, 2)
    upper, lower = after(upper, *gate), after(lower, *gate)
    add = lambda a, b: (a.astype(wide) + b.astype(wide)).astype(low)
    far = jnp.concatenate([add(far[:half], upper), far[half:].astype(low)], axis=0)
    near = jnp.concatenate([near[:half].astype(low), add(near[half:], lower)], axis=0)
    return (own, trade(near, axis, 1), trade(far, axis, 2)), (far, near)


def close_plane(parts, *gate):
    own, near, far = (part.astype(wide) for part in after(parts, *gate))
    return (own + near + far).astype(low)


def half_of(x, index, dim):
    return block_of(x, index, dim, 2)


def join_cores(mine, theirs, core, dim):
    first = jnp.where(core == 0, mine, theirs)
    second = jnp.where(core == 0, theirs, mine)
    return jnp.concatenate([first, second], axis=dim)


def contract(a, b, dims):
    return lax.dot_general(a, b, ((dims[:1], dims[1:]), ((), ())), preferred_element_type=wide)


def place_of(index, size):
    return pl.ds(pl.multiple_of(index * size, size), size)


def fold_rows(x):
    return jnp.sum(x.reshape(x.shape[0] // 8, 8, x.shape[1]), axis=0)


def fixed(shape):
    return pl.BlockSpec(
        shape, lambda step, scalars: (0,) * len(shape), pipeline_mode=pl.Buffered(1)
    )


def kept(shape):
    return pl.BlockSpec(shape, lambda step, scalars: (0,) * len(shape))


def by_row(width):
    return pl.BlockSpec((tile, width), lambda step, scalars: (step, 0))


def by_column(rows, width, first=0):
    return pl.BlockSpec((rows, width), lambda step, scalars: (0, jnp.maximum(step - first, 0)))


def call(
    kernel, name, steps, in_specs, out_specs, out_shape, operands, flops, moved, scratch=(), exps=0
):
    return pl.pallas_call(
        kernel,
        grid_spec=pltpu.PrefetchScalarGridSpec(
            num_scalar_prefetch=1,
            grid=(steps,),
            in_specs=in_specs,
            out_specs=out_specs,
            scratch_shapes=list(scratch),
        ),
        out_shape=out_shape,
        compiler_params=pltpu.CompilerParams(vmem_limit_bytes=room.get(name, 28) * megabyte),
        cost_estimate=pl.CostEstimate(
            flops=int(flops * pace.get(name, 16)),
            bytes_accessed=int(moved * pace.get(name, 16)),
            transcendentals=int(exps * pace.get(name, 16)),
        ),
        name=name,
    )(*operands)


def shaped(*shape, kind=low):
    return jax.ShapeDtypeStruct(shape, kind)


def own_first(piece, core):
    return piece[:, place_of(core, tile)], piece[:, place_of(1 - core, tile)]


def norm_kernel(scalars, *refs):
    pieces, terms = refs[:4], refs[4:8]
    attn_out, ffn_out, stats_out, terms_out = refs[8:]
    width = 8 * tile
    lane = lax.broadcasted_iota(jnp.int32, (strip, 128), 1)
    for start in range(0, stats_out.shape[0], strip):
        here = slice(start, start + strip)
        parts = [piece[here, :].astype(wide) for piece in pieces]
        total = sum(jnp.sum(part, axis=1, keepdims=True) for part in parts)
        mean = total * (1.0 / width)
        spread = sum(
            jnp.sum((part - mean) * (part - mean), axis=1, keepdims=True) for part in parts
        )
        inverse = lax.rsqrt(spread * (1.0 / width) + norm_epsilon)
        for k in range(4):
            block = scalars[2] ^ k
            for half in range(2):
                side = scalars[0] if half == 0 else 1 - scalars[0]
                source = place_of(side, tile)
                columns = place_of(4 * half + block, tile)
                normed = (pieces[k][here, source].astype(wide) - mean) * inverse
                term = terms[k][:, source].astype(wide)
                attn_out[here, columns] = (normed * term[0:1] + term[1:2]).astype(low)
                ffn_out[here, columns] = (normed * term[2:3] + term[3:4]).astype(low)
        stats_out[here, :] = jnp.where(lane < 64, mean, inverse)

    @pl.when(pl.program_id(0) == 0)
    def _():
        for k in range(4):
            for half in range(2):
                side = scalars[0] if half == 0 else 1 - scalars[0]
                columns = place_of(4 * half + (scalars[2] ^ k), tile)
                terms_out[:, columns] = terms[k][0:8, place_of(side, tile)].astype(wide)


def norm(scalars, pieces, rows):
    width = pieces[0].shape[1]
    term = pl.BlockSpec((16, width), lambda step, scalars: (rows // 16, 0))
    return call(
        norm_kernel,
        "norm",
        rows // tile,
        [by_row(width)] * 4 + [term] * 4,
        [by_row(4 * width), by_row(4 * width), by_row(128), kept((8, 4 * width))],
        [
            shaped(rows, 4 * width),
            shaped(rows, 4 * width),
            shaped(rows, 128, kind=wide),
            shaped(8, 4 * width, kind=wide),
        ],
        (scalars, *pieces, *pieces),
        rows * width * 40,
        rows * width * 24,
    )


def assemble_kernel(scalars, own, near, far, upper, lower, first_out, second_out):
    step = pl.program_id(0)
    split = first_out.shape[1]
    middle = upper.shape[0]

    def write(piece, rows):
        first_out[rows, :] = piece[:, :split]
        second_out[rows, :] = piece[:, split:]

    for k, piece in enumerate((own, near, far)):
        pl.when(step == k)(partial(write, piece, slice(None)))

    @pl.when(step == 3)
    def _():
        write(upper, slice(0, middle))
        write(lower, slice(middle, 2 * middle))


def assemble(scalars, pieces, halves, split):
    rows, columns = pieces[0].shape
    place = lambda step, scalars: (scalars[3] ^ step, 0)
    return call(
        assemble_kernel,
        "assemble",
        4,
        [fixed((rows, columns))] * 3 + [fixed((rows // 2, columns))] * 2,
        [pl.BlockSpec((rows, split), place), pl.BlockSpec((rows, columns - split), place)],
        [shaped(4 * rows, split), shaped(4 * rows, columns - split)],
        (scalars, *pieces, *halves),
        rows * columns,
        rows * columns * 16,
    )


strip = 32


def strips(first, rows):
    return [(at, first + at, first + at + strip) for at in range(0, rows, strip)]


def double(rows_in, own, other):
    half = rows_in.shape[1] // 2
    return contract(rows_in[:, :half], own, (1, 0)) + contract(rows_in[:, half:], other, (1, 0))


def heads_kernel(scalars, rows_in, own, other, shift_row, cosine, sine, mine, theirs):
    def run(out):
        for first in range(0, rows_in.shape[0], tile):
            product = double(rows_in.at[first : first + tile, :], own[...], other[...])
            for at, start, stop in strips(first, tile):
                joined = product[at : at + strip] + shift_row[0:1, :]
                for part in range(3):
                    vectors = joined[:, part * HEAD_DIM : (part + 1) * HEAD_DIM]
                    if part < 2:
                        vectors = turn(vectors, cosine[start:stop, :], sine[start:stop, :], 1.0)
                    out[part, start:stop, :] = vectors.astype(low)

    pl.when(pl.program_id(0) == 0)(partial(run, theirs))
    pl.when(pl.program_id(0) == 1)(partial(run, mine))


def heads(scalars, attn_in, weights, shift_row, cosine, sine):
    rows, width = attn_in.shape
    columns = 3 * HEAD_DIM

    def column(step, scalars):
        return 0, jnp.where(step == 0, 1 - scalars[0], scalars[0])

    weight = pl.BlockSpec((width // 2, columns), column)
    return call(
        heads_kernel,
        "heads",
        2,
        [fixed(attn_in.shape), weight, weight, pl.BlockSpec((1, columns), column)]
        + [fixed((rows, 128))] * 2,
        [kept((3, rows, HEAD_DIM))] * 2,
        [shaped(3, rows, HEAD_DIM)] * 2,
        (scalars, attn_in, *weights, shift_row, cosine, sine),
        4 * rows * width * columns,
        2 * (rows * width + 2 * width * columns + 2 * rows * columns),
    )


def expand_kernel(scalars, rows_in, own, other, shift_row, hidden, slope):
    for first in range(0, rows_in.shape[0], tile):
        product = double(rows_in.at[first : first + tile, :], own[...], other[...])
        for at, start, stop in strips(first, tile):
            pre = product[at : at + strip] + shift_row[0:1, :]
            phi = 0.5 + 0.5 * lax.erf(pre * math.sqrt(0.5))
            density = jnp.exp(pre * pre * -0.5) * (1.0 / math.sqrt(2.0 * math.pi))
            hidden[start:stop, :] = (pre * phi).astype(low)
            slope[start:stop, :] = (phi + pre * density).astype(low)


def expand(scalars, ffn_in, weights, shift_row):
    rows, width = ffn_in.shape
    columns = weights[0].shape[1]
    return call(
        expand_kernel,
        "expand",
        columns // tile,
        [fixed(ffn_in.shape)] + [by_column(width // 2, tile)] * 2 + [by_column(1, tile)],
        [by_column(rows, tile)] * 2,
        [shaped(rows, columns), shaped(rows, columns)],
        (scalars, ffn_in, *weights, shift_row),
        2 * rows * width * columns,
        2 * (rows * width + width * columns + 2 * rows * columns),
        exps=2 * rows * columns,
    )


def project_kernel(scalars, mine, theirs, hidden, own, other, out):
    heads_rows = 2 * HEAD_DIM
    for half, weight in enumerate((own, other)):
        total = contract(hidden[...], weight[heads_rows:, :], (1, 0))
        total += contract(mine[...], weight[place_of(scalars[0], HEAD_DIM), :], (1, 0))
        total += contract(theirs[...], weight[place_of(1 - scalars[0], HEAD_DIM), :], (1, 0))
        out[:, half * tile : (half + 1) * tile] = total.astype(out.dtype)


def project(scalars, mine, theirs, hidden, outward):
    rows = hidden.shape[0]
    depth = outward.shape[0]
    return call(
        project_kernel,
        "project",
        4,
        [fixed(mine.shape), fixed(mine.shape), fixed(hidden.shape)]
        + [
            pl.BlockSpec((depth, tile), lambda step, scalars: (0, 2 * step + scalars[0])),
            pl.BlockSpec((depth, tile), lambda step, scalars: (0, 2 * step + 1 - scalars[0])),
        ],
        [by_column(rows, 2 * tile)],
        [shaped(rows, 8 * tile)],
        (scalars, mine, theirs, hidden, outward, outward),
        16 * rows * tile * depth,
        2 * (rows * 8 * tile + depth * 8 * tile + rows * depth),
    )[0]


def hidden_back_kernel(scalars, *refs):
    pieces, (slope, weight) = refs[:4], refs[4:6]
    cotangent, pre_grad, mine, theirs, bias_grad, natural, both = refs[6:]
    step = pl.program_id(0)
    width = pieces[0].shape[1]

    @pl.when(step == 0)
    def _():
        for k in range(4):
            block = scalars[2] ^ k
            natural[:, place_of(block, width)] = pieces[k][...]
            own, other = own_first(pieces[k], scalars[0])
            cotangent[:, place_of(block, tile)] = own
            cotangent[:, place_of(4 + block, tile)] = other

    rows = natural.shape[0]

    @pl.when(step == 0)
    def _():
        both[...] = contract(natural[...], weight[...], (1, 1)).astype(low)
        theirs[...] = both[:, place_of(1 - scalars[0], HEAD_DIM)]
        mine[...] = both[:, place_of(scalars[0], HEAD_DIM)]

    @pl.when(step >= 1)
    def _():
        total = jnp.zeros((8, weight.shape[0]), wide)
        for first in range(0, rows, tile):
            grad = contract(natural[first : first + tile, :], weight[...], (1, 1))
            for at, start, stop in strips(first, tile):
                scaled = grad[at : at + strip] * slope[start:stop, :].astype(wide)
                scaled = scaled.astype(low)
                pre_grad[start:stop, :] = scaled
                total += fold_rows(scaled.astype(wide))
        bias_grad[...] = total


def hidden_back(scalars, pieces, slope, outward):
    rows, width = pieces[0].shape
    depth = outward.shape[0]
    hidden = depth - 2 * HEAD_DIM

    weight = pl.BlockSpec((2 * tile, 4 * width), lambda step, scalars: (step, 0))
    return call(
        hidden_back_kernel,
        "hidden_back",
        depth // (2 * tile),
        [fixed((rows, width))] * 4 + [by_column(rows, 2 * tile, 1), weight],
        [
            kept((rows, 4 * width)),
            by_column(rows, 2 * tile, 1),
            kept((rows, HEAD_DIM)),
            kept((rows, HEAD_DIM)),
            by_column(8, 2 * tile, 1),
        ],
        [
            shaped(rows, 4 * width),
            shaped(rows, hidden),
            shaped(rows, HEAD_DIM),
            shaped(rows, HEAD_DIM),
            shaped(8, hidden, kind=wide),
        ],
        (scalars, *pieces, slope, outward),
        8 * rows * width * depth,
        rows * width * 16 + 8 * width * depth + rows * hidden * 4,
        scratch=[pltpu.VMEM((rows, 4 * width), low), pltpu.VMEM((rows, 2 * HEAD_DIM), low)],
    )


def mix_kernel(
    scalars, mine, theirs, pre_grad, qkv_own, qkv_other, up_own, up_other, terms_own, terms_other,
    stats, first_piece, second_piece, first_out, second_out, sums_own, sums_other, row_sums,
    *both
):
    step = pl.program_id(0)
    rows = pre_grad.shape[0]
    lane = lax.broadcasted_iota(jnp.int32, (strip, 128), 1)

    def run(piece, out, fresh):
        for half, qkv, up, terms, sums in (
            (0, qkv_own, up_own, terms_own, sums_own),
            (1, qkv_other, up_other, terms_other, sums_other),
        ):
            side = scalars[0] if half == 0 else 1 - scalars[0]
            totals = [jnp.zeros((8, tile), wide)] * 4
            attn_gain, ffn_gain = terms[0:1, :], terms[2:3, :]
            for first in range(0, rows, tile):
                here = slice(first, first + tile)
                attn_part = contract(
                    mine[here, :], qkv[:, place_of(scalars[0], 3 * HEAD_DIM)], (1, 1)
                ) + contract(
                    theirs[here, :], qkv[:, place_of(1 - scalars[0], 3 * HEAD_DIM)], (1, 1)
                )
                ffn_part = contract(pre_grad[here, :], up[...], (1, 1))
                for at, start, stop in strips(first, tile):
                    attn, ffn = attn_part[at : at + strip], ffn_part[at : at + strip]
                    mean, inverse = stats[start:stop, 0:1], stats[start:stop, 64:65]
                    held = piece[start:stop, place_of(side, tile)].astype(wide)
                    normed = (held - mean) * inverse
                    mixed = attn * attn_gain + ffn * ffn_gain
                    weighed = mixed * normed
                    parts = (attn * normed, attn, ffn * normed, ffn)
                    totals = [total + fold_rows(part) for total, part in zip(totals, parts)]
                    out[start:stop, half * tile : (half + 1) * tile] = mixed.astype(out.dtype)
                    across = jnp.where(
                        lane < 64,
                        jnp.sum(mixed[:, :128] + mixed[:, 128:], axis=1, keepdims=True),
                        jnp.sum(weighed[:, :128] + weighed[:, 128:], axis=1, keepdims=True),
                    )
                    if fresh and half == 0:
                        row_sums[start:stop, :] = across
                    else:
                        row_sums[start:stop, :] += across
            for place, total in enumerate(totals):
                sums[8 * place : 8 * place + 8, :] = total

    for joined in both:

        @pl.when(step == 0)
        def _():
            joined[:, place_of(scalars[0], 3 * HEAD_DIM)] = mine[...]
            joined[:, place_of(1 - scalars[0], 3 * HEAD_DIM)] = theirs[...]

    pl.when(step == 0)(partial(run, first_piece, first_out, True))
    pl.when(step == 1)(partial(run, second_piece, second_out, False))


def mix(scalars, mine, theirs, pre_grad, qkv, up, terms, stats, pieces, order, kinds, join=False):
    rows = pre_grad.shape[0]
    width = pieces[0].shape[1]
    depth = qkv[0].shape[1] + up[0].shape[1]

    def block(step, scalars):
        return scalars[2] ^ jnp.where(step == 0, order[0], order[1])

    weight = lambda x: pl.BlockSpec((tile, x.shape[1]), lambda step, scalars: (block(step, scalars), 0))
    term = lambda first: pl.BlockSpec((8, tile), lambda step, scalars: (0, first + block(step, scalars)))
    sums = pl.BlockSpec((32, tile), lambda step, scalars: (0, step))
    return call(
        mix_kernel,
        "mix",
        2,
        [fixed(mine.shape), fixed(mine.shape), fixed(pre_grad.shape)]
        + [weight(x) for x in (*qkv, *up)]
        + [term(0), term(4), fixed((rows, 128))]
        + [fixed((rows, width))] * 2,
        [kept((rows, width))] * 2
        + [sums, sums, kept((rows, 128))]
        + [kept((rows, 6 * HEAD_DIM))] * join,
        [shaped(rows, width, kind=kind) for kind in kinds]
        + [shaped(32, 2 * tile, kind=wide)] * 2
        + [shaped(rows, 128, kind=wide)]
        + [shaped(rows, 6 * HEAD_DIM)] * join,
        (scalars, mine, theirs, pre_grad, *qkv, *up, terms, terms, stats, pieces[order[0]], pieces[order[1]]),
        4 * rows * width * depth,
        2 * (4 * rows * width + 2 * depth * width + rows * depth),
    )


def attend_kernel(scalars, mine, theirs, info, packed, own_out, twin_out, log_total, natural, scale):
    rows = natural.shape[0]
    blocks = rows // tile
    own = place_of(scalars[0], rows // 2)
    twin = place_of(1 - scalars[0], rows // 2)
    for part in range(3):
        packed[part, own, :] = mine[part]
        packed[part, twin, :] = theirs[part]
    for block in range(blocks):
        span = (block + 1) * tile
        query = packed[0, block * tile : span, :]
        about = info[:, block * tile : span]
        scores = scores_of(packed[1, :span, :], query, about, scalars[1], block * tile, scale)
        top = jnp.max(scores, axis=0, keepdims=True)
        powers = jnp.exp(scores - top)
        total = jnp.sum(powers, axis=0, keepdims=True)
        probs = (powers * (1.0 / total)).astype(low)
        natural[block * tile : span, :] = contract(probs, packed[2, :span, :], (0, 0)).astype(low)
        log_total[0:1, block * tile : span] = top + jnp.log(total)
    own_out[...] = natural[own, :]
    twin_out[...] = natural[twin, :]


def attend(scalars, mine, theirs, info):
    held = mine.shape[1]
    rows = 2 * held
    pairs = rows * (rows + tile) // 2
    return call(
        partial(attend_kernel, scale=1.0 / math.sqrt(HEAD_DIM)),
        "attend",
        1,
        [fixed(mine.shape), fixed(mine.shape), fixed((8, rows))],
        [kept((3, rows, HEAD_DIM)), kept((held, HEAD_DIM)), kept((held, HEAD_DIM)), kept((8, rows))],
        [
            shaped(3, rows, HEAD_DIM),
            shaped(held, HEAD_DIM),
            shaped(held, HEAD_DIM),
            shaped(8, rows, kind=wide),
        ],
        (scalars, mine, theirs, info),
        pairs * HEAD_DIM * 4,
        rows * HEAD_DIM * 16,
        scratch=[pltpu.VMEM((rows, HEAD_DIM), low)],
        exps=pairs,
    )


def attend_back_kernel(
    scalars, packed, own_grads, twin_grads, log_total, cosine, sine, info, own_out, twin_out,
    bias_grad, grads, natural, key_grad, value_grad, scale
):
    rows = grads.shape[0]
    blocks = rows // tile
    shift = scalars[0] * (blocks // 2)
    own = place_of(scalars[0], rows // 2)
    twin = place_of(1 - scalars[0], rows // 2)
    grads[own, :] = own_grads[...]
    grads[twin, :] = twin_grads[...]
    bias_total = jnp.zeros((8, 3 * HEAD_DIM), wide)
    for block in reversed(range(blocks)):
        span = (block + 1) * tile
        before = block * tile
        query = packed[0, before:span, :]
        about = info[:, before:span]
        there = place_of(lax.rem(block + shift, blocks), tile)
        grad = grads[before:span, :]
        scores = scores_of(packed[1, :span, :], query, about, scalars[1], before, scale)
        probs = jnp.exp(scores - log_total[0:1, before:span])
        value_part = contract(probs.astype(low), grad, (1, 0))
        dots = contract(packed[2, :span, :], grad, (1, 1))
        delta = jnp.sum(probs * dots, axis=0, keepdims=True)
        score_grad = (probs * (dots - delta)).astype(low)
        query_grad = contract(score_grad, packed[1, :span, :], (0, 0)) * scale
        key_part = contract(score_grad, query, (1, 0)) * scale
        if block == blocks - 1:
            key_grad[...] = key_part
            value_grad[...] = value_part
        else:
            key_grad[:span, :] += key_part
            value_grad[:span, :] += value_part
        parts = (
            turn(query_grad, cosine[there, :], sine[there, :], -1.0),
            turn(key_grad[before:span, :], cosine[there, :], sine[there, :], -1.0),
            value_grad[before:span, :],
        )
        together = jnp.concatenate(parts, axis=1).astype(low)
        natural[before:span, :] = together
        bias_total += fold_rows(together.astype(wide))
    bias_grad[...] = bias_total
    own_out[...] = natural[own, :]
    twin_out[...] = natural[twin, :]


def attend_back(scalars, packed, own_grads, twin_grads, log_total, cosine, sine, info):
    held = own_grads.shape[0]
    rows = 2 * held
    pairs = rows * (rows + tile) // 2
    return call(
        partial(attend_back_kernel, scale=1.0 / math.sqrt(HEAD_DIM)),
        "attend_back",
        1,
        [
            fixed((3, rows, HEAD_DIM)),
            fixed((held, HEAD_DIM)),
            fixed((held, HEAD_DIM)),
            fixed((8, rows)),
            fixed((rows, 128)),
            fixed((rows, 128)),
            fixed((8, rows)),
        ],
        [kept((held, 3 * HEAD_DIM)), kept((held, 3 * HEAD_DIM)), kept((8, 3 * HEAD_DIM))],
        [
            shaped(held, 3 * HEAD_DIM),
            shaped(held, 3 * HEAD_DIM),
            shaped(8, 3 * HEAD_DIM, kind=wide),
        ],
        (scalars, packed, own_grads, twin_grads, log_total, cosine, sine, info),
        pairs * HEAD_DIM * 10,
        rows * HEAD_DIM * 16,
        scratch=[
            pltpu.VMEM((rows, HEAD_DIM), low),
            pltpu.VMEM((rows, 3 * HEAD_DIM), low),
            pltpu.VMEM((rows, HEAD_DIM), wide),
            pltpu.VMEM((rows, HEAD_DIM), wide),
        ],
        exps=pairs,
    )


def turn(rows, cosine, sine, sign):
    half_rot = ROTARY // 2
    lane = lax.broadcasted_iota(jnp.int32, cosine.shape, 1)
    front = rows[:, :128]
    ahead = pltpu.roll(front, 128 - half_rot, 1)
    behind = pltpu.roll(front, half_rot, 1)
    other = jnp.where(lane < half_rot, -ahead, behind)
    turned = front * cosine + other * (sine * sign)
    return jnp.concatenate([turned, rows[:, 128:]], axis=1)


def scores_of(keys, query, info, trunk_end, first_row, scale):
    scores = contract(keys, query, (1, 1)) * scale
    key_place = lax.broadcasted_iota(jnp.int32, scores.shape, 0)
    query_place = first_row + lax.broadcasted_iota(jnp.int32, scores.shape, 1)
    seen = (
        (key_place < trunk_end)
        | ((key_place >= info[0:1]) & (key_place < info[1:2]))
        | (key_place >= info[2:3])
    ) & (key_place <= query_place)
    return jnp.where(seen, scores, masked_score)


def tree_info(lengths, parent, rows):
    labels = jnp.arange(SEGS)
    ends = jnp.sum(jnp.where(labels[None, :] <= labels[:, None], lengths[None, :], 0), axis=1)
    starts = ends - lengths
    hot_parent = parent[:, None] == labels[None, :]
    parent_start = jnp.sum(jnp.where(hot_parent, starts[None, :], 0), axis=1)
    parent_end = jnp.sum(jnp.where(hot_parent, ends[None, :], 0), axis=1)
    places = jnp.arange(rows, dtype=jnp.int32)
    inside = (places[None, :] >= starts[:, None]) & (places[None, :] < ends[:, None])
    pick = lambda table: jnp.sum(jnp.where(inside, table[:, None], 0), axis=0)
    spans = [pick(parent_start), pick(parent_end), pick(starts)]
    return jnp.stack(spans + [places] * 5).astype(jnp.int32), ends[0]


def rotary_tables(depth):
    half_rot = ROTARY // 2
    lane = jnp.arange(128)
    frequency = jnp.power(10000.0, -2.0 * (lane % half_rot).astype(wide) / ROTARY)
    frequency = jnp.where(lane < ROTARY, frequency, 0.0)
    angles = depth.astype(wide)[:, None] * frequency[None, :]
    return jnp.cos(angles), jnp.sin(angles)


def on_device_split(
    residual,
    out_grad,
    path_depth,
    seg_lengths,
    parents,
    attn_norm_gain,
    attn_norm_bias,
    ffn_norm_gain,
    ffn_norm_bias,
    qkv_weight,
    qkv_bias,
    dense_weight,
    dense_bias,
    up_weight,
    up_bias,
    down_weight,
    down_bias,
):
    core = lax.axis_index("ctx")
    line = lax.axis_index("tp")
    plane = lax.axis_index("fsdp")
    rows, held_width = residual.shape
    width = 4 * held_width
    half = width // 2

    norm_rows = jnp.stack([attn_norm_gain, attn_norm_bias, ffn_norm_gain, ffn_norm_bias] * 4)
    held = jnp.concatenate([residual, norm_rows], axis=0)
    inward = jnp.concatenate([qkv_weight, up_weight], axis=1)
    split = qkv_weight.shape[1]
    other_depth = trade(path_depth, "ctx", 1)
    cosine, sine = rotary_tables(jnp.concatenate([path_depth, other_depth]))
    info, trunk_end = tree_info(seg_lengths[0], parents[0], 2 * rows)
    scalars = jnp.stack([core, trunk_end, line, plane]).astype(jnp.int32)
    qkv_shift = qkv_bias.astype(wide)[None, :]
    up_shift = up_bias.astype(wide)[None, :]
    near, far, cosine, sine, info = meet(
        trade(held, "tp", 1), trade(held, "tp", 2), cosine, sine, info
    )
    inward_near, inward_far, inward = meet(
        trade(inward, "fsdp", 1), trade(inward, "fsdp", 2), inward, near
    )[:3]
    middle = inward.shape[0] // 2
    upper_corner = trade(inward_far[:middle], "fsdp", 1)
    lower_corner = trade(inward_near[middle:], "fsdp", 2)
    corner = trade(far, "tp", 1)
    upper_corner, lower_corner, corner = meet(upper_corner, lower_corner, corner)
    qkv_own, up_own = assemble(
        scalars, (inward, inward_near, inward_far), (upper_corner, lower_corner), split
    )
    pieces = (held, near, far, corner)

    def both_cores(own, *gate):
        return own, trade(after(own, *gate), "ctx", 1)

    outward = jnp.concatenate([dense_weight, down_weight], axis=0)
    outward = lax.all_gather(after(outward, upper_corner), ("fsdp", "ctx"), axis=1, tiled=True)

    qkv = both_cores(qkv_own)
    up = both_cores(up_own)
    first_grad = after(out_grad, corner)
    grad_near = trade(first_grad, "tp", 1)
    grad_far = trade(first_grad, "tp", 2)

    attn_in, ffn_in, stats, terms = norm(scalars, pieces, rows)
    mine, theirs = heads(scalars, attn_in, qkv, qkv_shift, cosine, sine)
    theirs = trade(theirs, "ctx", 1)
    hidden, slope = expand(after(scalars, mine), ffn_in, up, up_shift)
    grad_corner = trade(after(grad_far, slope), "tp", 1)
    packed, attended, twin_attended, log_total = attend(
        after(scalars, slope, grad_near, grad_far), mine, theirs, info
    )
    other_attended = trade(twin_attended, "ctx", 1)
    chip_out = project(scalars, attended, other_attended, hidden, outward)
    shared_out = lax.psum_scatter(chip_out, "tp", scatter_dimension=1, tiled=True)

    grad_pieces = (out_grad, grad_near, grad_far, grad_corner)
    cotangent, pre_grad, head_grad, other_grad, up_bias_rows = hidden_back(
        after(scalars, chip_out), grad_pieces, slope, outward
    )
    other_grad = trade(other_grad, "ctx", 1)

    def outer(left, right):
        return contract(left, right, (0, 0))

    def add_low(own, arrived):
        return (own + arrived.astype(wide)).astype(low)

    def to_owner(total, dim):
        return lax.psum_scatter(total, "fsdp", scatter_dimension=dim, tiled=True)

    both_attended = join_cores(attended, other_attended, core, 1)
    down_other = outer(after(hidden, pre_grad), cotangent[:, half:]).astype(low)
    down_arrived = trade(down_other, "ctx", 1)
    up_other = outer(after(ffn_in, down_other)[:, half:], pre_grad).astype(low)
    up_arrived = trade(up_other, "ctx", 1)
    down_total = add_low(outer(after(hidden, up_other), cotangent[:, :half]), down_arrived)
    joined_grad, twin_grad, qkv_bias_rows = attend_back(
        after(scalars, down_total), packed, head_grad, other_grad, log_total, cosine, sine, info
    )
    other_joined = trade(twin_grad, "ctx", 1)
    down_parts, down_hop = scatter_plane(down_total, "fsdp", 1, joined_grad)
    dense_other = outer(after(both_attended, joined_grad, *down_hop), cotangent[:, half:]).astype(low)
    dense_arrived = trade(dense_other, "ctx", 1)
    up_total = add_low(outer(after(ffn_in, dense_other)[:, :half], pre_grad), up_arrived)
    up_grad = to_owner(up_total, 0)
    dense_total = add_low(
        outer(after(both_attended, up_total, other_joined), cotangent[:, :half]), dense_arrived
    )
    mix_in = (joined_grad, other_joined, pre_grad, qkv, up, terms, stats, pieces)
    *leave, sums_a, sums_b, row_a, both_joined = mix(
        after(scalars, dense_total), *mix_in, (3, 1), (low, low), True
    )
    mixed_side = trade(leave[0], "tp", 1)
    *stay_mixed, sums_c, sums_d, row_b = mix(
        after(scalars, leave[0], shared_out), *mix_in, (2, 0), (wide, wide)
    )
    passed = (stay_mixed[0] + mixed_side.astype(wide)).astype(low)
    row_sums = row_a + row_b
    row_total = jnp.stack([row_sums[:, 0], row_sums[:, 64]])
    fold = lambda x: jnp.sum(x.reshape(4, 8, 2, tile), axis=1)
    gather_sums = lambda own, other: jnp.stack([fold(own), fold(other)], axis=2).reshape(4, 2, 2 * tile)
    leaving, norm_sums = gather_sums(sums_a, sums_b), gather_sums(sums_c, sums_d)
    hop_side = trade(jnp.concatenate([leaving.reshape(-1), row_total.reshape(-1)]), "tp", 1)
    norm_sums = norm_sums + hop_side[: 8 * held_width].reshape(norm_sums.shape)
    row_total = row_total + hop_side[8 * held_width :].reshape(row_total.shape)
    hop_far = trade(jnp.concatenate([norm_sums[:, 0].reshape(-1), row_total.reshape(-1)]), "tp", 2)
    qkv_other = outer(
        after(attn_in, stay_mixed[0], passed, hop_side, down_parts)[:, half:], both_joined
    ).astype(low)
    qkv_arrived = trade(qkv_other, "ctx", 1)
    far_mixed = trade(after(passed, hop_far), "tp", 2)
    mixed_near = trade(after(leave[1], hop_far), "tp", 1)
    norm_total = norm_sums[:, 1] + hop_far[: 4 * held_width].reshape(4, held_width)
    row_total = row_total + hop_far[4 * held_width :].reshape(row_total.shape)
    row_means = row_total / width
    norm_total = join_cores(norm_total[:, :tile], norm_total[:, tile:], core, 1)
    down_grad = close_plane(down_parts, qkv_other)
    qkv_total = add_low(
        outer(after(attn_in, qkv_other, down_grad, hop_far)[:, :half], both_joined), qkv_arrived
    )
    shared_out = after(shared_out, qkv_total).astype(wide)
    shared_out = join_cores(shared_out[:, :tile], shared_out[:, tile:], core, 1)
    output = (
        residual.astype(wide) + shared_out + dense_bias.astype(wide) + down_bias.astype(wide)
    ).astype(low)

    held_grad_sum = jnp.sum(after(out_grad, qkv_total).astype(wide), axis=0)
    columns = jnp.concatenate(
        [
            norm_total.reshape(-1),
            held_grad_sum,
            jnp.sum(up_bias_rows, axis=0),
            jnp.sum(qkv_bias_rows, axis=0),
        ]
    )
    columns = after(columns, qkv_total)
    columns = columns + trade(columns, "fsdp", 1)
    columns = columns + trade(columns, "fsdp", 2)
    dense_grad = to_owner(after(dense_total, up_grad, qkv_total), 1)
    qkv_parts, qkv_hop = scatter_plane(qkv_total, "fsdp", 0)
    qkv_grad = close_plane(qkv_parts)
    dense_grad, up_grad = after(dense_grad, *qkv_hop), after(up_grad, *qkv_hop)
    other_columns = trade(columns, "ctx", 1)
    cut = columns.shape[0] - qkv_bias.shape[0] // 2
    qkv_bias_grad = join_cores(columns[cut:], other_columns[cut:], core, 0)
    together = columns[:cut] + other_columns[:cut]
    norm_grads = together[:width].reshape(4, held_width)
    out_bias_grad = together[width : width + held_width]
    up_bias_grad = together[width + held_width :]


    up_grad = up_grad.astype(wide)
    far_mixed = after(far_mixed, mixed_near, other_columns, output, up_grad, *qkv_hop)
    shared_mixed = stay_mixed[1] + mixed_near.astype(wide) + far_mixed.astype(wide)
    shared_mixed = join_cores(shared_mixed[:, :tile], shared_mixed[:, tile:], core, 1)
    mean = stats[:, 0:1]
    inverse = stats[:, 64:65]
    own_normed = (residual.astype(wide) - mean) * inverse
    back = inverse * (shared_mixed - row_means[0][:, None] - own_normed * row_means[1][:, None])
    input_grad = (out_grad.astype(wide) + back).astype(low)
    return (
        output,
        input_grad,
        norm_grads[0],
        norm_grads[1],
        norm_grads[2],
        norm_grads[3],
        qkv_grad.astype(wide),
        qkv_bias_grad,
        dense_grad.astype(wide),
        out_bias_grad,
        up_grad,
        up_bias_grad,
        down_grad.astype(wide),
        out_bias_grad,
    )


def splits_heads(mesh):
    return mesh.shape["tp"] == 4 and mesh.shape["fsdp"] == 4 and mesh.shape["ctx"] == 2


def solution(mesh):
    placed = (
        P(("fsdp", "ctx"), "tp"),
        P(("fsdp", "ctx"), "tp"),
        P(("fsdp", "ctx")),
        P("fsdp", None),
        P("fsdp", None),
        P("tp"),
        P("tp"),
        P("tp"),
        P("tp"),
        P(("fsdp", "ctx"), "tp"),
        P("tp"),
        P("tp", ("fsdp", "ctx")),
        P("tp"),
        P(("fsdp", "ctx"), "tp"),
        P("tp"),
        P("tp", ("fsdp", "ctx")),
        P("tp"),
    )
    return jax.shard_map(
        on_device_split if splits_heads(mesh) else on_device,
        mesh=mesh,
        in_specs=placed,
        out_specs=(
            P(("fsdp", "ctx"), "tp"),
            P(("fsdp", "ctx"), "tp"),
            P("tp"),
            P("tp"),
            P("tp"),
            P("tp"),
            P(("fsdp", "ctx"), "tp"),
            P("tp"),
            P("tp", ("fsdp", "ctx")),
            P("tp"),
            P(("fsdp", "ctx"), "tp"),
            P("tp"),
            P("tp", ("fsdp", "ctx")),
            P("tp"),
        ),
        check_vma=False,
    )
```
